32 devices in a mesh: dom: 8 (over z, y), rep: 4 (over x, core).
Axes of the slice: x: 2, y: 2, z: 4, core: 2. Of those that a mesh axis runs over, the one named last changes fastest.
Arguments:
- features: bfloat16 [16384, 768], P(('dom', 'rep')), may hold values from -13 to 13
- sketch_matrix: bfloat16 [768, 256], replicated, may hold values from -0.21875 to 0.21875
- tiles: bfloat16 [8, 20, 256, 256], P('dom'), may hold values from 0 to 2, as said below
- tile_dst: int32 [8, 20], P('dom'), may hold values from -1 to 7, as said below
- tile_src: int32 [8, 20], P('dom'), may hold values from 0 to 11, as said below
- halo_index: int32 [8, 1024], P('dom'), may hold values from 0 to 2047
- send_order: int32 [8, 2048], P('dom'), may hold values from 0 to 2047, each once within a row
- arrival_place: int32 [8, 2048], P('dom'), may hold values from 0 to 2047, each once within a row
Outputs:
- signals: bfloat16 [3, 256, 16384], P(None, 'rep', 'dom')
The draws below stay inside these ranges and needn't reach their ends.
Inputs may be any that keep to these rules, and one draw needn't show every extreme that they name: `tiles`: entries are zero or positive; in slot t < 8 of every partition the tile's diagonal is positive. `tile_dst`: in every partition slot t < 8 holds t, the live slots come first and the others hold -1; some partition uses every slot and some only the first 12. `tile_src`: slot t < 12 holds t in every partition; empty slots hold 0. `halo_index`: A row may be listed for several peers and more than once. `send_order`: each row is a permutation. `arrival_place`: each row is a permutation.
All inputs are finite; a program needn't handle non-finite values.
Results may differ from the reference program's by a relative error of at most 0.0034.
Values may be sent and summed in bfloat16 or wider, within the bound.
No kernel may reach another device: no remote copies, remote signals or barrier semaphores. Data moves between devices by JAX's collectives and lax.ppermute only.
A program may use at most 64 MiB of HBM per device.

```python
import jax
import jax.numpy as jnp
from jax import lax

IN_WIDTH = 768
SKETCH = 256
TILE_SIDE = 256
ROWS_DEV = 2048
TILES_DEV = 20
HALO_ROWS = 1024
HALO_SLOT = 128
LAYOUT_SLOT = 256
NODE_COUNT = 16384
N_DOM = 8


def tile_lists(key):
    block_count = ROWS_DEV // TILE_SIDE
    halo_blocks = HALO_ROWS // TILE_SIDE
    spare = TILES_DEV - block_count - halo_blocks
    base = jax.random.fold_in(key, 7)
    first_key, second_key, third_key, fourth_key = jax.random.split(base, 4)
    spread = jax.random.randint(first_key, (N_DOM,), 0, spare + 1)
    extra = spread * spread // spare
    full_part = jax.random.randint(second_key, (), 0, N_DOM)
    owners = jnp.arange(N_DOM, dtype=jnp.int32)
    extra = jnp.where(owners == full_part, spare, extra)
    extra = jnp.where(owners == (full_part + 1) % N_DOM, 0, extra)
    slot = jnp.arange(TILES_DEV, dtype=jnp.int32)[None, :]
    random_dst = jax.random.randint(third_key, (N_DOM, TILES_DEV), 0, block_count)
    random_src = jax.random.randint(fourth_key, (N_DOM, TILES_DEV), 0, block_count + halo_blocks)
    targets = jnp.where(slot < block_count, slot, random_dst)
    sources = jnp.where(slot < block_count + halo_blocks, slot, random_src)
    live = slot < block_count + halo_blocks + extra[:, None]
    targets = jnp.where(live, targets, -1)
    sources = jnp.where(live, sources, 0)
    return (targets.astype(jnp.int32), sources.astype(jnp.int32))


def draw_tile_dst(key, part):
    return tile_lists(key)[0]


def draw_tile_src(key, part):
    return tile_lists(key)[1]


def draw_features(key, part):
    noise_key, level_key, factor_key, vector_key = jax.random.split(jax.random.fold_in(key, 23), 4)
    shape = (NODE_COUNT, IN_WIDTH)
    noise = jnp.clip(jax.random.normal(noise_key, shape, jnp.float32), -4.0, 4.0)
    levels = jnp.exp(jax.random.uniform(level_key, (N_DOM, 1), jnp.float32, jnp.log(0.3), jnp.log(3.0)))
    factors = jnp.exp(jax.random.uniform(factor_key, (N_DOM, ROWS_DEV), jnp.float32, jnp.log(0.7), 0.0))
    direction = jnp.clip(jax.random.normal(vector_key, (1, IN_WIDTH), jnp.float32), -3.0, 3.0)
    common = (levels * factors).reshape(NODE_COUNT, 1) * direction
    return (noise + common).astype(jnp.bfloat16)


def draw_tiles(key, part):
    block_count = ROWS_DEV // TILE_SIDE
    first_key, second_key, third_key = jax.random.split(jax.random.fold_in(key, 11), 3)
    shape = (N_DOM, TILES_DEV, TILE_SIDE, TILE_SIDE)
    present = (jax.random.randint(first_key, shape, 0, 32) == 0).astype(jnp.float32)
    values = jnp.exp(jax.random.uniform(second_key, shape, jnp.float32, jnp.log(0.001), 0.0))
    selfw = jnp.exp(jax.random.uniform(third_key, (N_DOM, TILES_DEV, 1, TILE_SIDE), jnp.float32, jnp.log(0.1), 0.0))
    diagonal_slot = (jnp.arange(TILES_DEV) < block_count).astype(jnp.float32)[None, :, None, None]
    identity = jnp.eye(TILE_SIDE, dtype=jnp.float32)[None, None, :, :]
    result = present * values + identity * selfw * diagonal_slot
    return result.astype(jnp.bfloat16)


def set_ends(array, stream_key, smallest, largest):
    longest = array.shape.index(max(array.shape))
    spots = []
    for shift in (0, 1):
        where = [jax.random.randint(jax.random.fold_in(stream_key, axis), (), 0, length) for axis, length in enumerate(array.shape)]
        where[longest] = (where[longest] + shift) % array.shape[longest]
        spots.append(tuple(where))
    return array.at[spots[0]].set(smallest).at[spots[1]].set(largest)


def scatter_about(stream_key, shape, width, reach, kind=jnp.bfloat16):
    return jnp.clip(width * jax.random.normal(stream_key, shape, jnp.float32), -reach, reach).astype(kind)


def setup_inputs(seed: int = 0) -> dict:
    keys = jax.random.split(jax.random.key(seed), 9)
    return {
        "features": draw_features(jax.random.fold_in(keys[8], 71), 0),
        "sketch_matrix": scatter_about(keys[1], (IN_WIDTH, SKETCH), IN_WIDTH ** -0.5, 0.21875),
        "tiles": draw_tiles(jax.random.fold_in(keys[8], 71), 0),
        "tile_dst": draw_tile_dst(jax.random.fold_in(keys[8], 71), 0),
        "tile_src": draw_tile_src(jax.random.fold_in(keys[8], 71), 0),
        "halo_index": set_ends(jax.random.randint(keys[5], (N_DOM, HALO_ROWS), 0, ROWS_DEV), jax.random.fold_in(keys[5], 1), 0, ROWS_DEV - 1).astype(jnp.int32),
        "send_order": jax.vmap(lambda own: jax.random.permutation(own, ROWS_DEV))(jax.random.split(keys[6], N_DOM)).reshape((N_DOM, ROWS_DEV)).astype(jnp.int32),
        "arrival_place": jax.vmap(lambda own: jax.random.permutation(own, ROWS_DEV))(jax.random.split(keys[7], N_DOM)).reshape((N_DOM, ROWS_DEV)).astype(jnp.int32),
    }


def propagate(layer, tiles, tile_dst, tile_src, halo_cols, partitions):
    block_count = ROWS_DEV // TILE_SIDE

    def one_part(inputs):
        tile_set, targets, sources, halo_row, index = inputs
        local = lax.dynamic_slice_in_dim(layer, index * ROWS_DEV, ROWS_DEV, 1)
        columns = jnp.concatenate([local, jnp.take(layer, halo_row, axis=1)], 1)
        blocks = columns.reshape(SKETCH, -1, TILE_SIDE)[:, sources, :]
        products = jnp.einsum("ctj,tij->cti", blocks.astype(jnp.float32), tile_set.astype(jnp.float32),
                              precision=lax.Precision.HIGHEST)
        onehot = (targets[:, None] == jnp.arange(block_count, dtype=jnp.int32)[None, :]).astype(jnp.float32)
        summed = jnp.einsum("cti,tb->cbi", products, onehot, precision=lax.Precision.HIGHEST).reshape(SKETCH, ROWS_DEV)
        row_sums = jnp.sum(tile_set, axis=2, dtype=jnp.float32)
        degree = jnp.einsum("ti,tb->bi", row_sums, onehot, precision=lax.Precision.HIGHEST).reshape(ROWS_DEV)
        return (summed / degree[None, :]).astype(jnp.bfloat16)

    result = lax.map(one_part, (tiles, tile_dst, tile_src, halo_cols, partitions))
    return result.transpose(1, 0, 2).reshape(SKETCH, NODE_COUNT)


def reference(features, sketch_matrix, tiles, tile_dst, tile_src, halo_index, send_order, arrival_place):
    hop0 = jnp.dot(features, sketch_matrix, preferred_element_type=jnp.float32).astype(jnp.bfloat16).T
    partitions = jnp.arange(N_DOM, dtype=jnp.int32)
    halo_cols = halo_index.reshape(N_DOM, N_DOM, HALO_SLOT).transpose(1, 0, 2)
    halo_cols = (halo_cols + (partitions * ROWS_DEV)[None, :, None]).reshape(N_DOM, HALO_ROWS).astype(jnp.int32)
    hop1 = propagate(hop0, tiles, tile_dst, tile_src, halo_cols, partitions)
    hop2 = propagate(hop1, tiles, tile_dst, tile_src, halo_cols, partitions)
    source_node = send_order.reshape(N_DOM, N_DOM, LAYOUT_SLOT).transpose(1, 0, 2)
    source_node = (source_node + (partitions * ROWS_DEV)[None, :, None]).reshape(NODE_COUNT).astype(jnp.int32)
    target_node = (arrival_place + (partitions * ROWS_DEV)[:, None]).reshape(NODE_COUNT).astype(jnp.int32)
    stacked = jnp.stack([hop0, hop1, hop2])
    signals = jnp.zeros_like(stacked).at[:, :, target_node].set(stacked[:, :, source_node])
    return signals
```

```python
import functools

import jax
import jax.numpy as jnp
from jax import lax
from jax.experimental import pallas as pl
from jax.experimental.pallas import tpu as pltpu
from jax.sharding import PartitionSpec as P

BF16 = jnp.bfloat16
F32 = jnp.float32
EXTRA = 16
VMEM_LIMIT = 40 * 1024 * 1024


def params():
    return pltpu.CompilerParams(vmem_limit_bytes=VMEM_LIMIT)


def cost(flops, size):
    return pl.CostEstimate(flops=flops, bytes_accessed=size, transcendentals=0)


def whole(count):
    return [pl.BlockSpec(memory_space=pltpu.VMEM)] * count


def table_kernel(index_ref, table_ref):
    rows, columns = table_ref.shape
    step = 256
    index = index_ref[...]

    def body(chunk, carry):
        base = chunk * step
        row = lax.broadcasted_iota(jnp.int32, (step, columns), 0) + base
        table_ref[pl.ds(pl.multiple_of(base, step), step), :] = jnp.where(
            row == index, 1.0, 0.0
        ).astype(BF16)
        return carry

    lax.fori_loop(0, rows // step, body, 0)


def make_table(index, rows):
    columns = index.shape[1]
    return pl.pallas_call(
        table_kernel,
        out_shape=jax.ShapeDtypeStruct((rows, columns), BF16),
        in_specs=whole(1),
        out_specs=pl.BlockSpec(memory_space=pltpu.VMEM),
        compiler_params=params(),
        cost_estimate=cost(4 * rows * columns, 2 * rows * columns),
        name="table",
    )(index)


def store_slots(send_ref, picked):
    if len(send_ref.shape) == 2:
        send_ref[...] = picked
    else:
        slot = send_ref.shape[2]
        for peer in range(send_ref.shape[0]):
            send_ref[peer] = picked[:, peer * slot : (peer + 1) * slot]


def pick_kernel(arrived_ref, table_ref, hop_ref, send_ref):
    parts, _, width = arrived_ref.shape
    for part in range(parts):
        hop_ref[:, part * width : (part + 1) * width] = arrived_ref[part]
    picked = jnp.dot(hop_ref[...], table_ref[...], preferred_element_type=F32)
    store_slots(send_ref, picked.astype(BF16))


def send_shape(channels, peers, slot):
    if slot % 128:
        return jax.ShapeDtypeStruct((channels, peers * slot), BF16)
    return jax.ShapeDtypeStruct((peers, channels, slot), BF16)


def chunk_major(send, peers):
    if send.ndim == 3:
        return send
    channels = send.shape[0]
    return send.reshape(channels, peers, -1).transpose(1, 0, 2)


def exchange(send, peers):
    return lax.all_to_all(chunk_major(send, peers), "dom", 0, 0, tiled=True)


def wide(arrived):
    if arrived.shape[2] % 128 == 0:
        return arrived
    return arrived.transpose(1, 0, 2).reshape(arrived.shape[1], -1)


def load_wide(ref):
    if len(ref.shape) == 2:
        return ref[...]
    return jnp.concatenate([ref[peer] for peer in range(ref.shape[0])], axis=1)


def local_kernel(hop_ref, tiles_ref, total_ref):
    channels, nodes = hop_ref.shape
    side = tiles_ref.shape[1]
    ones = jnp.ones((EXTRA, side), BF16)
    for block in range(nodes // side):
        columns = jnp.concatenate([hop_ref[:, block * side : (block + 1) * side], ones], 0)
        total_ref[block] = lax.dot_general(
            columns, tiles_ref[block], (((1,), (1,)), ((), ())), preferred_element_type=F32
        )


def local_part(hop, tiles):
    channels, nodes = hop.shape
    side = tiles.shape[1]
    blocks = nodes // side
    return pl.pallas_call(
        local_kernel,
        out_shape=jax.ShapeDtypeStruct((blocks, channels + EXTRA, side), F32),
        in_specs=[
            pl.BlockSpec((channels, nodes), lambda i: (0, 0)),
            pl.BlockSpec((blocks, side, side), lambda i: (0, 0, 0)),
        ],
        out_specs=pl.BlockSpec((blocks, channels + EXTRA, side), lambda i: (0, 0, 0)),
        grid=(1,),
        compiler_params=params(),
        cost_estimate=cost(2 * nodes * side * channels, 2 * nodes * side),
        name="local_part",
    )(hop, tiles)


def combine_body(
    dst_ref, src_ref, hop_ref, total_ref, arrived_ref, tiles_ref, columns, sums, result_ref
):
    channels, nodes = hop_ref.shape
    slots, side, _ = tiles_ref.shape
    blocks = nodes // side
    arrived = load_wide(arrived_ref)
    fixed = blocks + arrived.shape[1] // side
    columns[:, channels:, :] = jnp.ones((fixed, EXTRA, side), BF16)
    for block in range(blocks):
        columns[block, :channels, :] = hop_ref[:, block * side : (block + 1) * side]
        sums[block] = total_ref[block]
    for block in range(blocks, fixed):
        start = (block - blocks) * side
        columns[block, :channels, :] = arrived[:, start : start + side]
    for slot in range(blocks, slots):
        target = dst_ref[0, slot]
        target = jnp.where(target < 0, blocks, target)
        source = slot if slot < fixed else src_ref[0, slot]
        product = lax.dot_general(
            columns[source], tiles_ref[slot], (((1,), (1,)), ((), ())), preferred_element_type=F32
        )
        sums[target] = sums[target] + product
    for block in range(blocks):
        block_sums = sums[block]
        result_ref[:, block * side : (block + 1) * side] = (
            block_sums[:channels] / block_sums[channels : channels + 1]
        ).astype(BF16)


def combine_pick_kernel(
    dst_ref, src_ref, hop_ref, total_ref, arrived_ref, tiles_ref, table_ref,
    result_ref, send_ref, columns, sums,
):
    combine_body(
        dst_ref, src_ref, hop_ref, total_ref, arrived_ref, tiles_ref, columns, sums, result_ref
    )
    picked = jnp.dot(result_ref[...], table_ref[...], preferred_element_type=F32)
    store_slots(send_ref, picked.astype(BF16))


def combine_last_kernel(
    dst_ref, src_ref, hop0_ref, hop_ref, total_ref, arrived_ref, tiles_ref, table_ref,
    send_ref, result_ref, columns, sums,
):
    combine_body(
        dst_ref, src_ref, hop_ref, total_ref, arrived_ref, tiles_ref, columns, sums, result_ref
    )
    stacked = jnp.concatenate([hop0_ref[...], hop_ref[...], result_ref[...]], 0)
    picked = jnp.dot(stacked, table_ref[...], preferred_element_type=F32)
    store_slots(send_ref, picked.astype(BF16))


def combine_scratch(channels, nodes, halo, side):
    return [
        pltpu.VMEM(((nodes + halo) // side, channels + EXTRA, side), BF16),
        pltpu.VMEM((nodes // side + 1, channels + EXTRA, side), F32),
    ]


def smem(count):
    return [pl.BlockSpec(memory_space=pltpu.SMEM)] * count


def place_kernel(arrived_ref, table_ref, out_ref):
    hops, channels, nodes = out_ref.shape
    stacked = load_wide(arrived_ref)
    side = 256
    for start in range(0, nodes, side):
        placed = lax.dot_general(
            stacked, table_ref[start : start + side, :], (((1,), (1,)), ((), ())),
            preferred_element_type=F32,
        ).astype(BF16)
        for hop in range(hops):
            out_ref[hop, :, start : start + side] = placed[hop * channels : (hop + 1) * channels]


def on_device(
    features, sketch_matrix, tiles, tile_dst, tile_src, halo_index, send_order, arrival_place
):
    sketched = lax.dot_general(
        sketch_matrix, features, (((0,), (1,)), ((), ())), preferred_element_type=F32
    ).astype(BF16)
    reps = lax.axis_size("rep")
    peers = lax.axis_size("dom")
    channels = sketched.shape[0] // reps
    arrived = lax.all_to_all(
        sketched.reshape(reps, channels, -1), "rep", 0, 0, tiled=True
    )
    nodes = arrived.shape[2] * reps
    halo = halo_index.shape[1]
    tiles = tiles[0]
    side = tiles.shape[-1]
    halo_table = make_table(halo_index, nodes)
    send_table = make_table(send_order, nodes)
    place_table = make_table(arrival_place, nodes)
    hop_shape = jax.ShapeDtypeStruct((channels, nodes), BF16)
    halo_shape = send_shape(channels, peers, halo // peers)
    hop0, send = pl.pallas_call(
        pick_kernel,
        out_shape=(hop_shape, halo_shape),
        in_specs=whole(2),
        out_specs=tuple(whole(2)),
        compiler_params=params(),
        name="pick",
    )(arrived, halo_table)
    halo0 = wide(exchange(send, peers))
    total0 = local_part(hop0, tiles)
    hop1, send = pl.pallas_call(
        combine_pick_kernel,
        out_shape=(hop_shape, halo_shape),
        in_specs=smem(2) + whole(5),
        out_specs=tuple(whole(2)),
        scratch_shapes=combine_scratch(channels, nodes, halo, side),
        compiler_params=params(),
        name="combine_pick",
    )(tile_dst, tile_src, hop0, total0, halo0, tiles, halo_table)
    halo1 = wide(exchange(send, peers))
    total1 = local_part(hop1, tiles)
    send = pl.pallas_call(
        combine_last_kernel,
        out_shape=send_shape(3 * channels, peers, nodes // peers),
        in_specs=smem(2) + whole(6),
        out_specs=whole(1)[0],
        scratch_shapes=[pltpu.VMEM((channels, nodes), BF16)]
        + combine_scratch(channels, nodes, halo, side),
        compiler_params=params(),
        name="combine_last",
    )(tile_dst, tile_src, hop0, hop1, total1, halo1, tiles, send_table)
    last = wide(exchange(send, peers))
    return pl.pallas_call(
        place_kernel,
        out_shape=jax.ShapeDtypeStruct((3, channels, nodes), BF16),
        in_specs=whole(2),
        out_specs=whole(1)[0],
        compiler_params=params(),
        name="place",
    )(last, place_table)


def solution(mesh):
    in_specs = (
        P(("dom", "rep"), None),
        P(),
        P("dom", None, None, None),
        P("dom", None),
        P("dom", None),
        P("dom", None),
        P("dom", None),
        P("dom", None),
    )
    out_specs = P(None, "rep", "dom")
    return jax.shard_map(
        on_device, mesh=mesh, in_specs=in_specs, out_specs=out_specs, check_vma=False
    )
```

```python
import jax
import jax.numpy as jnp
from jax import lax
from jax.experimental import pallas as pl
from jax.experimental.pallas import tpu as pltpu
from jax.sharding import PartitionSpec as P

BF16 = jnp.bfloat16
F32 = jnp.float32
EXTRA = 16
NN = (((1,), (0,)), ((), ()))
NT = (((1,), (1,)), ((), ()))
VMEM = pl.BlockSpec(memory_space=pltpu.VMEM)
SMEM = pl.BlockSpec(memory_space=pltpu.SMEM)
HBM = pl.BlockSpec(memory_space=pltpu.HBM)


def params():
    return pltpu.CompilerParams(vmem_limit_bytes=40 * 1024 * 1024)


def cost(flops, size):
    return pl.CostEstimate(flops=flops, bytes_accessed=size, transcendentals=0)


def dot(left, right, dims=NN):
    return lax.dot_general(left, right, dims, preferred_element_type=F32)


def one_hot(index, base, rows):
    row = lax.broadcasted_iota(jnp.int32, (rows, index.shape[1]), 0) + base
    return jnp.where(row == index, 1.0, 0.0).astype(BF16)


def pick(blocks, index, side, group):
    parts = []
    for start in range(0, index.shape[1], group):
        some = index[:, start : start + group]
        total = None
        for block, columns in enumerate(blocks):
            term = dot(columns, one_hot(some, block * side, side))
            total = term if total is None else total + term
        parts.append(total.astype(BF16))
    return parts


def store_slots(buffer, parts, group):
    if len(buffer.shape) == 2:
        for place, part in enumerate(parts):
            buffer[:, place * group : (place + 1) * group] = part
        return
    slot = buffer.shape[2]
    for place, part in enumerate(parts):
        for start in range(0, group, slot):
            buffer[(place * group + start) // slot] = part[:, start : start + slot]


def send_shape(channels, peers, slot):
    if slot % 128:
        return (channels, peers * slot)
    return (peers, channels, slot)


def exchange(send, peers):
    if send.ndim == 2:
        send = send.reshape(send.shape[0], peers, -1).transpose(1, 0, 2)
    arrived = lax.all_to_all(send, "dom", 0, 0, tiled=True)
    if arrived.shape[2] % 128 == 0:
        return arrived
    return arrived.transpose(1, 0, 2).reshape(arrived.shape[1], -1)


def load_wide(ref):
    if len(ref.shape) == 2:
        return ref[...]
    return jnp.concatenate([ref[peer] for peer in range(ref.shape[0])], axis=1)


def sketch_kernel(count, me_ref, features_ref, sketch_ref, *rest):
    outs, full = rest[:count], rest[count]
    channels = outs[0].shape[0]
    product = dot(features_ref[...], sketch_ref[...])
    product = product.T.astype(BF16)
    for part in range(count):
        full[part] = product[part * channels : (part + 1) * channels]
    me = me_ref[0, 0]
    for step in range(count):
        outs[step][...] = full[partner(me, step, count)]


def partner(me, step, count):
    if count & (count - 1) == 0:
        return me ^ step
    return lax.rem(me + step, count)


def source(me, step, count):
    if count & (count - 1) == 0:
        return me ^ step
    return lax.rem(me + count - step, count)


def pick_kernel(count, group, me_ref, index_ref, *rest):
    arrived, (hop_out, send_out, hop, send, sems) = rest[:count], rest[count:]
    blocks, _, side = hop.shape
    per = blocks // count
    me = me_ref[0, 0]
    for step in range(count):
        first = source(me, step, count) * per
        for part in range(per):
            hop[first + part] = arrived[step][:, part * side : (part + 1) * side]
    hop_copy = pltpu.make_async_copy(hop, hop_out, sems.at[0])
    hop_copy.start()
    parts = pick([hop[block] for block in range(blocks)], index_ref[...], side, group)
    store_slots(send, parts, group)
    send_copy = pltpu.make_async_copy(send, send_out, sems.at[1])
    send_copy.start()
    hop_copy.wait()
    send_copy.wait()


def combine(dst_ref, src_ref, hop_in, arrived_ref, tiles_ref, columns, sums, result, sem):
    blocks, channels, side = result.shape
    slots = tiles_ref.shape[0]
    fixed = columns.shape[0]
    fetch = pltpu.make_async_copy(
        hop_in, columns.at[pl.ds(0, blocks), pl.ds(0, channels), :], sem
    )
    fetch.start()
    columns[:, channels:, :] = jnp.ones((fixed, EXTRA, side), BF16)
    arrived = load_wide(arrived_ref)
    for block in range(blocks, fixed):
        start = (block - blocks) * side
        columns[block, :channels, :] = arrived[:, start : start + side]
    fetch.wait()
    for block in range(blocks):
        sums[block] = dot(columns[block], tiles_ref[block], NT)
    for slot in range(blocks, slots):
        target = dst_ref[0, slot]
        target = jnp.where(target < 0, blocks, target)
        start = slot if slot < fixed else src_ref[0, slot]
        sums[target] = sums[target] + dot(columns[start], tiles_ref[slot], NT)
    for block in range(blocks):
        block_sums = sums[block]
        result[block] = (block_sums[:channels] / block_sums[channels : channels + 1]).astype(BF16)


def combine_pick_kernel(
    group, dst_ref, src_ref, index_ref, hop_in, arrived_ref, tiles_ref, hop_out, send_out,
    columns, sums, result, send, sems,
):
    blocks, _, side = result.shape
    combine(
        dst_ref, src_ref, hop_in, arrived_ref, tiles_ref, columns, sums, result, sems.at[2]
    )
    hop_copy = pltpu.make_async_copy(result, hop_out, sems.at[0])
    hop_copy.start()
    parts = pick([result[block] for block in range(blocks)], index_ref[...], side, group)
    store_slots(send, parts, group)
    send_copy = pltpu.make_async_copy(send, send_out, sems.at[1])
    send_copy.start()
    hop_copy.wait()
    send_copy.wait()


def combine_last_kernel(
    group, dst_ref, src_ref, index_ref, hop0_in, hop_in, arrived_ref, tiles_ref, send_out,
    columns, sums, result, hop0, send, sems,
):
    blocks, channels, side = result.shape
    first = pltpu.make_async_copy(hop0_in, hop0, sems.at[1])
    first.start()
    combine(
        dst_ref, src_ref, hop_in, arrived_ref, tiles_ref, columns, sums, result, sems.at[2]
    )
    first.wait()
    stacks = [
        jnp.concatenate([hop0[block], columns[block, :channels, :], result[block]], 0)
        for block in range(blocks)
    ]
    parts = pick(stacks, index_ref[...], side, group)
    store_slots(send, parts, group)
    send_copy = pltpu.make_async_copy(send, send_out, sems.at[0])
    send_copy.start()
    send_copy.wait()


def place_kernel(index_ref, arrived_ref, out_ref):
    hops, channels, width = out_ref.shape
    stacked = load_wide(arrived_ref)
    table = one_hot(index_ref[...], pl.program_id(0) * width, width)
    placed = dot(stacked, table, NT).astype(BF16)
    for hop in range(hops):
        out_ref[hop] = placed[hop * channels : (hop + 1) * channels]


def on_device(
    features, sketch_matrix, tiles, tile_dst, tile_src, halo_index, send_order, arrival_place
):
    reps = lax.axis_size("rep")
    peers = lax.axis_size("dom")
    width = features.shape[0]
    nodes = width * reps
    channels = sketch_matrix.shape[1] // reps
    halo = halo_index.shape[1]
    tiles = tiles[0]
    slots, side, _ = tiles.shape
    blocks = nodes // side
    fixed = (nodes + halo) // side
    me = lax.axis_index("rep").astype(jnp.int32).reshape(1, 1)
    vmem, dma = pltpu.VMEM, pltpu.SemaphoreType.DMA
    hop_shape = (blocks, channels, side)
    halo_shape = send_shape(channels, peers, halo // peers)
    last_shape = send_shape(3 * channels, peers, nodes // peers)
    group = 256

    def out(shape):
        return jax.ShapeDtypeStruct(shape, BF16)

    own = pl.pallas_call(
        lambda *refs: sketch_kernel(reps, *refs),
        out_shape=(out((channels, width)),) * reps,
        in_specs=[SMEM, VMEM, VMEM],
        out_specs=(VMEM,) * reps,
        scratch_shapes=[vmem((reps, channels, width), BF16)],
        compiler_params=params(),
        name="sketch",
    )(me, features, sketch_matrix)
    arrived = [own[0]]
    for step in range(1, reps):
        pairs = [(rank, int(partner_static(rank, step, reps))) for rank in range(reps)]
        arrived.append(lax.ppermute(own[step], "rep", pairs))
    hop0, send = pl.pallas_call(
        lambda *refs: pick_kernel(reps, group, *refs),
        out_shape=(out(hop_shape), out(halo_shape)),
        in_specs=[SMEM, VMEM] + [VMEM] * reps,
        out_specs=(HBM, HBM),
        scratch_shapes=[vmem(hop_shape, BF16), vmem(halo_shape, BF16), dma((2,))],
        compiler_params=params(),
        name="pick",
    )(me, halo_index, *arrived)
    halo0 = exchange(send, peers)
    work = [
        vmem((fixed, channels + EXTRA, side), BF16),
        vmem((blocks + 1, channels + EXTRA, side), F32),
        vmem(hop_shape, BF16),
    ]
    hop1, send = pl.pallas_call(
        lambda *refs: combine_pick_kernel(group, *refs),
        out_shape=(out(hop_shape), out(halo_shape)),
        in_specs=[SMEM, SMEM, VMEM, HBM, VMEM, VMEM],
        out_specs=(HBM, HBM),
        scratch_shapes=work + [vmem(halo_shape, BF16), dma((3,))],
        compiler_params=params(),
        name="combine_pick",
    )(tile_dst, tile_src, halo_index, hop0, halo0, tiles)
    halo1 = exchange(send, peers)
    send = pl.pallas_call(
        lambda *refs: combine_last_kernel(group, *refs),
        out_shape=out(last_shape),
        in_specs=[SMEM, SMEM, VMEM, HBM, HBM, VMEM, VMEM],
        out_specs=HBM,
        scratch_shapes=work + [vmem(hop_shape, BF16), vmem(last_shape, BF16), dma((3,))],
        compiler_params=params(),
        name="combine_last",
    )(tile_dst, tile_src, send_order, hop0, hop1, halo1, tiles)
    last = exchange(send, peers)
    return pl.pallas_call(
        place_kernel,
        out_shape=out((3, channels, nodes)),
        in_specs=[
            pl.BlockSpec((1, nodes), lambda i: (0, 0)),
            pl.BlockSpec(last.shape, lambda i: (0,) * last.ndim),
        ],
        out_specs=pl.BlockSpec((3, channels, side), lambda i: (0, 0, i)),
        grid=(blocks,),
        compiler_params=params(),
        name="place",
    )(arrival_place, last)


def partner_static(rank, step, count):
    if count & (count - 1) == 0:
        return rank ^ step
    return (rank + step) % count


def solution(mesh):
    in_specs = (
        P(("dom", "rep"), None),
        P(),
        P("dom", None, None, None),
        P("dom", None),
        P("dom", None),
        P("dom", None),
        P("dom", None),
        P("dom", None),
    )
    out_specs = P(None, "rep", "dom")
    return jax.shard_map(
        on_device, mesh=mesh, in_specs=in_specs, out_specs=out_specs, check_vma=False
    )
```

```python
import jax
import jax.numpy as jnp
from jax import lax
from jax.experimental import pallas as pl
from jax.experimental.pallas import tpu as pltpu
from jax.sharding import PartitionSpec as P

BF16 = jnp.bfloat16
F32 = jnp.float32
EXTRA = 16
NN = (((1,), (0,)), ((), ()))
NT = (((1,), (1,)), ((), ()))
VMEM = pl.BlockSpec(memory_space=pltpu.VMEM)
SMEM = pl.BlockSpec(memory_space=pltpu.SMEM)
HBM = pl.BlockSpec(memory_space=pltpu.HBM)


def params():
    return pltpu.CompilerParams(vmem_limit_bytes=40 * 1024 * 1024)


def in_hbm(array):
    return pltpu.with_memory_space_constraint(array, pltpu.HBM)


def dot(left, right, dims=NN):
    return lax.dot_general(left, right, dims, preferred_element_type=F32)


def split(index, side, blocks):
    block = jnp.zeros_like(index)
    for edge in range(1, blocks):
        block += (index >= edge * side).astype(jnp.int32)
    return block, index - block * side


def one_hot(index, rows):
    row = lax.broadcasted_iota(jnp.int32, (rows, index.shape[1]), 0)
    return jnp.where(row == index, 1.0, 0.0).astype(BF16)


def pick(stack, blocks, index, side, group):
    rows = stack.shape[0] // blocks
    parts = []
    for start in range(0, index.shape[1], group):
        block, inner = split(index[:, start : start + group], side, blocks)
        every = dot(stack, one_hot(inner, side))
        chosen = every[:rows]
        for other in range(1, blocks):
            chosen = jnp.where(block == other, every[other * rows : (other + 1) * rows], chosen)
        parts.append(chosen.astype(BF16))
    return parts


def store_slots(buffer, parts, group):
    if len(buffer.shape) == 2:
        for place, part in enumerate(parts):
            buffer[:, place * group : (place + 1) * group] = part
        return
    slot = buffer.shape[2]
    for place, part in enumerate(parts):
        for start in range(0, group, slot):
            buffer[(place * group + start) // slot] = part[:, start : start + slot]


def send_shape(channels, peers, slot):
    if slot % 128:
        return (channels, peers * slot)
    return (peers, channels, slot)


def exchange(send, peers):
    if send.ndim == 2:
        send = send.reshape(send.shape[0], peers, -1).transpose(1, 0, 2)
    arrived = lax.all_to_all(send, "dom", 0, 0, tiled=True)
    if arrived.shape[2] % 128 == 0:
        return arrived
    return arrived.transpose(1, 0, 2).reshape(arrived.shape[1], -1)


def load_wide(ref):
    if len(ref.shape) == 2:
        return ref[...]
    return jnp.concatenate([ref[peer] for peer in range(ref.shape[0])], axis=1)


def partner(me, step, count):
    if count & (count - 1) == 0:
        return me ^ step
    return lax.rem(me + step, count)


def source(me, step, count):
    if count & (count - 1) == 0:
        return me ^ step
    return lax.rem(me + count - step, count)


def pairs(step, count):
    if count & (count - 1) == 0:
        return [(rank, rank ^ step) for rank in range(count)]
    return [(rank, (rank + step) % count) for rank in range(count)]


def sketch_kernel(count, chunks, me_ref, features_in, sketch_in, *rest):
    outs, (full, features, sketch, sems) = rest[:count], rest[count:]
    channels, width = outs[0].shape
    step = width // chunks
    copies = [pltpu.make_async_copy(sketch_in, sketch, sems.at[chunks])]
    for chunk in range(chunks):
        rows = pl.ds(chunk * step, step)
        copies.append(
            pltpu.make_async_copy(features_in.at[rows, :], features.at[rows, :], sems.at[chunk])
        )
    for copy in copies:
        copy.start()
    copies[0].wait()
    for chunk in range(chunks):
        copies[chunk + 1].wait()
        rows = slice(chunk * step, (chunk + 1) * step)
        product = dot(features[rows, :], sketch[...]).T.astype(BF16)
        for part in range(count):
            full[part, :, rows] = product[part * channels : (part + 1) * channels]
    me = me_ref[0, 0]
    for part in range(count):
        outs[part][...] = full[partner(me, part, count)]


def pick_kernel(count, group, me_ref, index_in, *rest):
    arrived, (hop, send, index, sem) = rest[:count], rest[count:]
    fetch = pltpu.make_async_copy(index_in, index, sem)
    fetch.start()
    blocks, _, side = hop.shape
    per = blocks // count
    me = me_ref[0, 0]
    for step in range(count):
        first = source(me, step, count) * per
        for part in range(per):
            hop[first + part] = arrived[step][:, part * side : (part + 1) * side]
    stack = jnp.concatenate([hop[block] for block in range(blocks)], 0)
    fetch.wait()
    store_slots(send, pick(stack, blocks, index[...], side, group), group)


def combine(dst_in, src_in, index_in, tiles_in, hop, arrived_ref, scratch, store):
    dst, src, index, tiles, columns, sums, sems = scratch
    blocks, channels, side = hop.shape
    slots = tiles.shape[0]
    fixed = columns.shape[0]
    small = [
        pltpu.make_async_copy(dst_in, dst, sems.at[0]),
        pltpu.make_async_copy(src_in, src, sems.at[1]),
        pltpu.make_async_copy(index_in, index, sems.at[2]),
    ]
    chunk = 4
    large = []
    for start in range(0, slots, chunk):
        rows = pl.ds(start, chunk)
        large.append(
            pltpu.make_async_copy(tiles_in.at[rows], tiles.at[rows], sems.at[3 + start // chunk])
        )
    for copy in large + small:
        copy.start()
    columns[:, channels:, :] = jnp.ones((fixed, EXTRA, side), BF16)
    for block in range(blocks):
        columns[block, :channels, :] = hop[block]
    arrived = load_wide(arrived_ref)
    for block in range(blocks, fixed):
        start = (block - blocks) * side
        columns[block, :channels, :] = arrived[:, start : start + side]
    for slot in range(slots):
        if slot % chunk == 0:
            large[slot // chunk].wait()
        if slot < blocks:
            sums[slot] = dot(columns[slot], tiles[slot], NT)
            continue
        if slot == blocks:
            for copy in small:
                copy.wait()
        target = dst[0, slot]
        target = jnp.where(target < 0, blocks, target)
        start = slot if slot < fixed else src[0, slot]
        sums[target] = sums[target] + dot(columns[start], tiles[slot], NT)
    results = []
    for block in range(blocks):
        total = sums[block]
        result = (total[:channels] / total[channels : channels + 1]).astype(BF16)
        store(block, result)
        results.append(result)
    return results


def combine_pick_kernel(
    group, dst_in, src_in, index_in, tiles_in, hop, arrived_ref, result, send, *scratch
):
    def store(block, value):
        result[block] = value

    results = combine(dst_in, src_in, index_in, tiles_in, hop, arrived_ref, scratch, store)
    blocks, _, side = hop.shape
    index = scratch[2]
    stack = jnp.concatenate(results, 0)
    store_slots(send, pick(stack, blocks, index[...], side, group), group)


def combine_last_kernel(
    group, dst_in, src_in, index_in, tiles_in, hop, arrived_ref, hop0, send, *scratch
):
    results = combine(
        dst_in, src_in, index_in, tiles_in, hop, arrived_ref, scratch, lambda *_: None
    )
    blocks, _, side = hop.shape
    index = scratch[2]
    stack = []
    for block in range(blocks):
        stack += [hop0[block], hop[block], results[block]]
    stack = jnp.concatenate(stack, 0)
    store_slots(send, pick(stack, blocks, index[...], side, group), group)


def place_kernel(side, index_ref, arrived_ref, out_ref):
    hops, channels, nodes = out_ref.shape
    blocks = nodes // side
    stacked = load_wide(arrived_ref)
    rows = hops * channels
    block, inner = split(index_ref[...], side, blocks)
    table = one_hot(inner, side)
    for other in range(blocks):
        mask = jnp.where(block == other, 1.0, 0.0).astype(BF16)
        placed = dot(stacked * mask, table, NT).astype(BF16)
        for hop in range(hops):
            out_ref[hop, :, other * side : (other + 1) * side] = placed[
                hop * channels : (hop + 1) * channels
            ]


def on_device(
    features, sketch_matrix, tiles, tile_dst, tile_src, halo_index, send_order, arrival_place
):
    reps = lax.axis_size("rep")
    peers = lax.axis_size("dom")
    width = features.shape[0]
    nodes = width * reps
    channels = sketch_matrix.shape[1] // reps
    halo = halo_index.shape[1]
    tiles = tiles[0]
    slots, side, _ = tiles.shape
    blocks = nodes // side
    fixed = (nodes + halo) // side
    me = lax.axis_index("rep").astype(jnp.int32).reshape(1, 1)
    vmem, smem, dma = pltpu.VMEM, pltpu.SMEM, pltpu.SemaphoreType.DMA
    hop_shape = (blocks, channels, side)
    halo_shape = send_shape(channels, peers, halo // peers)
    last_shape = send_shape(3 * channels, peers, nodes // peers)
    group = 256
    chunks = 4

    def out(shape):
        return jax.ShapeDtypeStruct(shape, BF16)

    own = pl.pallas_call(
        lambda *refs: sketch_kernel(reps, chunks, *refs),
        out_shape=(out((channels, width)),) * reps,
        in_specs=[SMEM, HBM, HBM],
        out_specs=(VMEM,) * reps,
        scratch_shapes=[
            vmem((reps, channels, width), BF16),
            vmem(features.shape, BF16),
            vmem(sketch_matrix.shape, BF16),
            dma((chunks + 1,)),
        ],
        compiler_params=params(),
        name="sketch",
    )(me, in_hbm(features), in_hbm(sketch_matrix))
    arrived = [own[0]]
    for step in range(1, reps):
        arrived.append(lax.ppermute(own[step], "rep", pairs(step, reps)))
    hop0, send = pl.pallas_call(
        lambda *refs: pick_kernel(reps, group, *refs),
        out_shape=(out(hop_shape), out(halo_shape)),
        in_specs=[SMEM, HBM] + [VMEM] * reps,
        out_specs=(VMEM, VMEM),
        scratch_shapes=[vmem(halo_index.shape, jnp.int32), dma],
        compiler_params=params(),
        name="pick",
    )(me, in_hbm(halo_index), *arrived)
    halo0 = exchange(send, peers)

    def work(index):
        return [
            smem(tile_dst.shape, jnp.int32),
            smem(tile_src.shape, jnp.int32),
            vmem(index.shape, jnp.int32),
            vmem(tiles.shape, BF16),
            vmem((fixed, channels + EXTRA, side), BF16),
            vmem((blocks + 1, channels + EXTRA, side), F32),
            dma((3 + slots // 4,)),
        ]

    hop1, send = pl.pallas_call(
        lambda *refs: combine_pick_kernel(group, *refs),
        out_shape=(out(hop_shape), out(halo_shape)),
        in_specs=[HBM] * 4 + [VMEM] * 2,
        out_specs=(VMEM, VMEM),
        scratch_shapes=work(halo_index),
        compiler_params=params(),
        name="combine_pick",
    )(in_hbm(tile_dst), in_hbm(tile_src), in_hbm(halo_index), in_hbm(tiles), hop0, halo0)
    halo1 = exchange(send, peers)
    send = pl.pallas_call(
        lambda *refs: combine_last_kernel(group, *refs),
        out_shape=out(last_shape),
        in_specs=[HBM] * 4 + [VMEM] * 3,
        out_specs=VMEM,
        scratch_shapes=work(send_order),
        compiler_params=params(),
        name="combine_last",
    )(in_hbm(tile_dst), in_hbm(tile_src), in_hbm(send_order), in_hbm(tiles), hop1, halo1, hop0)
    last = exchange(send, peers)
    return pl.pallas_call(
        lambda *refs: place_kernel(side, *refs),
        out_shape=out((3, channels, nodes)),
        in_specs=[VMEM, VMEM],
        out_specs=VMEM,
        compiler_params=params(),
        name="place",
    )(arrival_place, last)


def solution(mesh):
    in_specs = (
        P(("dom", "rep"), None),
        P(),
        P("dom", None, None, None),
        P("dom", None),
        P("dom", None),
        P("dom", None),
        P("dom", None),
        P("dom", None),
    )
    out_specs = P(None, "rep", "dom")
    return jax.shard_map(
        on_device, mesh=mesh, in_specs=in_specs, out_specs=out_specs, check_vma=False
    )
```

```python
import jax
import jax.numpy as jnp
from jax import lax
from jax.experimental import pallas as pl
from jax.experimental.pallas import tpu as pltpu
from jax.sharding import PartitionSpec as P

BF16 = jnp.bfloat16
F32 = jnp.float32
EXTRA = 16
NN = (((1,), (0,)), ((), ()))
NT = (((1,), (1,)), ((), ()))
VMEM = pl.BlockSpec(memory_space=pltpu.VMEM)
SMEM = pl.BlockSpec(memory_space=pltpu.SMEM)
HBM = pl.BlockSpec(memory_space=pltpu.HBM)


def params():
    return pltpu.CompilerParams(vmem_limit_bytes=40 * 1024 * 1024)


def cost(flops, size):
    return pl.CostEstimate(flops=flops, bytes_accessed=size, transcendentals=0)


def in_hbm(array):
    return pltpu.with_memory_space_constraint(array, pltpu.HBM)


def dot(left, right, dims=NN):
    return lax.dot_general(left, right, dims, preferred_element_type=F32)


def split(index, side, blocks):
    block = jnp.zeros_like(index)
    for edge in range(1, blocks):
        block += (index >= edge * side).astype(jnp.int32)
    return block, index - block * side


def one_hot(index, rows):
    row = lax.broadcasted_iota(jnp.int32, (rows, index.shape[1]), 0)
    return jnp.where(row == index, 1.0, 0.0).astype(BF16)


def pick(stack, blocks, index, side, group):
    rows = stack.shape[0] // blocks
    parts = []
    for start in range(0, index.shape[1], group):
        block, inner = split(index[:, start : start + group], side, blocks)
        every = dot(stack, one_hot(inner, side))
        chosen = every[:rows]
        for other in range(1, blocks):
            chosen = jnp.where(block == other, every[other * rows : (other + 1) * rows], chosen)
        parts.append(chosen.astype(BF16))
    return parts


def store_slots(buffer, parts, group):
    if len(buffer.shape) == 2:
        for place, part in enumerate(parts):
            buffer[:, place * group : (place + 1) * group] = part
        return
    slot = buffer.shape[2]
    for place, part in enumerate(parts):
        for start in range(0, group, slot):
            buffer[(place * group + start) // slot] = part[:, start : start + slot]


def send_shape(channels, peers, slot):
    if slot % 128:
        return (channels, peers * slot)
    return (peers, channels, slot)


def exchange(send, peers):
    if send.ndim == 2:
        send = send.reshape(send.shape[0], peers, -1).transpose(1, 0, 2)
    arrived = lax.all_to_all(send, "dom", 0, 0, tiled=True)
    if arrived.shape[2] % 128 == 0:
        return arrived
    return arrived.transpose(1, 0, 2).reshape(arrived.shape[1], -1)


def load_wide(ref):
    if len(ref.shape) == 2:
        return ref[...]
    return jnp.concatenate([ref[peer] for peer in range(ref.shape[0])], axis=1)


def partner(me, step, count):
    if count & (count - 1) == 0:
        return me ^ step
    return lax.rem(me + step, count)


def source(me, step, count):
    if count & (count - 1) == 0:
        return me ^ step
    return lax.rem(me + count - step, count)


def pairs(step, count):
    if count & (count - 1) == 0:
        return [(rank, rank ^ step) for rank in range(count)]
    return [(rank, (rank + step) % count) for rank in range(count)]


def sketch_kernel(count, chunks, me_ref, features_in, sketch_in, *rest):
    outs, (full, features, sketch, sems) = rest[:count], rest[count:]
    channels, width = outs[0].shape
    step = width // chunks
    copies = [pltpu.make_async_copy(sketch_in, sketch, sems.at[chunks])]
    for chunk in range(chunks):
        rows = pl.ds(chunk * step, step)
        copies.append(
            pltpu.make_async_copy(features_in.at[rows, :], features.at[rows, :], sems.at[chunk])
        )
    for copy in copies:
        copy.start()
    copies[0].wait()
    for chunk in range(chunks):
        copies[chunk + 1].wait()
        rows = slice(chunk * step, (chunk + 1) * step)
        product = dot(features[rows, :], sketch[...]).T.astype(BF16)
        for part in range(count):
            full[part, :, rows] = product[part * channels : (part + 1) * channels]
    me = me_ref[0, 0]
    for part in range(count):
        outs[part][...] = full[partner(me, part, count)]


def pick_kernel(count, group, me_ref, index_in, *rest):
    arrived, (hop, send, index, sem) = rest[:count], rest[count:]
    fetch = pltpu.make_async_copy(index_in, index, sem)
    fetch.start()
    blocks, _, side = hop.shape
    per = blocks // count
    me = me_ref[0, 0]
    for step in range(count):
        first = source(me, step, count) * per
        for part in range(per):
            hop[first + part] = arrived[step][:, part * side : (part + 1) * side]
    stack = jnp.concatenate([hop[block] for block in range(blocks)], 0)
    fetch.wait()
    store_slots(send, pick(stack, blocks, index[...], side, group), group)


def combine(dst_in, src_in, index_in, tiles_in, hop, arrived_ref, scratch, store):
    dst, src, index, tiles, columns, sums, sems = scratch
    blocks, channels, side = hop.shape
    slots = tiles.shape[0]
    fixed = columns.shape[0]
    small = [
        pltpu.make_async_copy(dst_in, dst, sems.at[0]),
        pltpu.make_async_copy(src_in, src, sems.at[1]),
        pltpu.make_async_copy(index_in, index, sems.at[2]),
    ]
    chunk = 4
    large = []
    for start in range(0, slots, chunk):
        rows = pl.ds(start, chunk)
        large.append(
            pltpu.make_async_copy(tiles_in.at[rows], tiles.at[rows], sems.at[3 + start // chunk])
        )
    for copy in large + small:
        copy.start()
    columns[:, channels:, :] = jnp.ones((fixed, EXTRA, side), BF16)
    for block in range(blocks):
        columns[block, :channels, :] = hop[block]
    arrived = load_wide(arrived_ref)
    for block in range(blocks, fixed):
        start = (block - blocks) * side
        columns[block, :channels, :] = arrived[:, start : start + side]
    for slot in range(slots):
        if slot % chunk == 0:
            large[slot // chunk].wait()
        if slot < blocks:
            sums[slot] = dot(columns[slot], tiles[slot], NT)
            continue
        if slot == blocks:
            for copy in small:
                copy.wait()
        target = dst[0, slot]
        target = jnp.where(target < 0, blocks, target)
        start = slot if slot < fixed else src[0, slot]
        sums[target] = sums[target] + dot(columns[start], tiles[slot], NT)
    results = []
    for block in range(blocks):
        total = sums[block]
        result = (total[:channels] / total[channels : channels + 1]).astype(BF16)
        store(block, result)
        results.append(result)
    return results


def combine_pick_kernel(
    group, dst_in, src_in, index_in, tiles_in, hop, arrived_ref, result, send, *scratch
):
    def store(block, value):
        result[block] = value

    results = combine(dst_in, src_in, index_in, tiles_in, hop, arrived_ref, scratch, store)
    blocks, _, side = hop.shape
    index = scratch[2]
    stack = jnp.concatenate(results, 0)
    store_slots(send, pick(stack, blocks, index[...], side, group), group)


def early_kernel(me_ref, index_in, hop0, hop1, *rest):
    peers = len(rest) - 3
    outs, (full, index, sem) = rest[:peers], rest[peers:]
    fetch = pltpu.make_async_copy(index_in, index, sem)
    fetch.start()
    blocks, _, side = hop0.shape
    stack = []
    for block in range(blocks):
        stack += [hop0[block], hop1[block]]
    stack = jnp.concatenate(stack, 0)
    fetch.wait()
    slot = full.shape[2]
    for peer, part in enumerate(pick(stack, blocks, index[...], side, slot)):
        full[peer] = part
    me = me_ref[0, 0]
    for step in range(peers):
        outs[step][...] = full[partner(me, step, peers)]


def late_kernel(
    peers, near, me_ref, dst_in, src_in, index_in, tiles_in, hop, arrived_ref, *rest
):
    early, outs, full = rest[:near], rest[near : near + peers], rest[near + peers]
    scratch = rest[near + peers + 1 :]
    results = combine(
        dst_in, src_in, index_in, tiles_in, hop, arrived_ref, scratch, lambda *_: None
    )
    blocks, channels, side = hop.shape
    index = scratch[2]
    stack = jnp.concatenate(results, 0)
    for peer, part in enumerate(pick(stack, blocks, index[...], side, full.shape[2])):
        full[peer] = part
    me = me_ref[0, 0]
    for step in range(near):
        rows = early[step].shape[0]
        outs[step][:rows] = early[step][...]
        outs[step][rows:] = full[partner(me, step, peers)]
    for step in range(near, peers):
        outs[step][...] = full[partner(me, step, peers)]


def combine_last_kernel(
    group, dst_in, src_in, index_in, tiles_in, hop, arrived_ref, hop0, send, *scratch
):
    results = combine(
        dst_in, src_in, index_in, tiles_in, hop, arrived_ref, scratch, lambda *_: None
    )
    blocks, _, side = hop.shape
    index = scratch[2]
    stack = []
    for block in range(blocks):
        stack += [hop0[block], hop[block], results[block]]
    stack = jnp.concatenate(stack, 0)
    store_slots(send, pick(stack, blocks, index[...], side, group), group)


def place_steps_kernel(peers, near, side, me_ref, index_ref, *rest):
    whole, early, late = rest[:near], rest[near:peers], rest[peers : 2 * peers - near]
    out_ref, out, sems = rest[2 * peers - near :]
    hops, channels, nodes = out.shape
    blocks = nodes // side
    slot = nodes // peers
    me = me_ref[0, 0]
    parts, indexes = [], []
    for step in range(peers):
        start = pl.multiple_of(source(me, step, peers) * slot, slot)
        indexes.append(index_ref[:, pl.ds(start, slot)])
        if step < near:
            parts.append(whole[step][...])
        else:
            parts.append(
                jnp.concatenate([early[step - near][...], late[step - near][...]], 0)
            )
    block, inner = split(jnp.concatenate(indexes, 1), side, blocks)
    table = one_hot(inner, side)
    stacked = jnp.concatenate(parts, 1)
    copies = []
    for other in range(blocks):
        mask = jnp.where(block == other, 1.0, 0.0).astype(BF16)
        placed = dot(stacked * mask, table, NT).astype(BF16)
        columns = slice(other * side, (other + 1) * side)
        for hop in range(hops):
            out[hop, :, columns] = placed[hop * channels : (hop + 1) * channels]
        columns = pl.ds(other * side, side)
        copies.append(
            pltpu.make_async_copy(
                out.at[:, :, columns], out_ref.at[:, :, columns], sems.at[other]
            )
        )
        copies[-1].start()
    for copy in copies:
        copy.wait()


def place_kernel(side, index_ref, arrived_ref, out_ref):
    hops, channels, nodes = out_ref.shape
    blocks = nodes // side
    stacked = load_wide(arrived_ref)
    rows = hops * channels
    block, inner = split(index_ref[...], side, blocks)
    table = one_hot(inner, side)
    for other in range(blocks):
        mask = jnp.where(block == other, 1.0, 0.0).astype(BF16)
        placed = dot(stacked * mask, table, NT).astype(BF16)
        for hop in range(hops):
            out_ref[hop, :, other * side : (other + 1) * side] = placed[
                hop * channels : (hop + 1) * channels
            ]


def on_device(
    features, sketch_matrix, tiles, tile_dst, tile_src, halo_index, send_order, arrival_place
):
    reps = lax.axis_size("rep")
    peers = lax.axis_size("dom")
    width = features.shape[0]
    nodes = width * reps
    channels = sketch_matrix.shape[1] // reps
    halo = halo_index.shape[1]
    tiles = tiles[0]
    slots, side, _ = tiles.shape
    blocks = nodes // side
    fixed = (nodes + halo) // side
    me = lax.axis_index("rep").astype(jnp.int32).reshape(1, 1)
    vmem, smem, dma = pltpu.VMEM, pltpu.SMEM, pltpu.SemaphoreType.DMA
    hop_shape = (blocks, channels, side)
    halo_shape = send_shape(channels, peers, halo // peers)
    last_shape = send_shape(3 * channels, peers, nodes // peers)
    group = 256
    chunks = 4

    def out(shape):
        return jax.ShapeDtypeStruct(shape, BF16)

    own = pl.pallas_call(
        lambda *refs: sketch_kernel(reps, chunks, *refs),
        out_shape=(out((channels, width)),) * reps,
        in_specs=[SMEM, HBM, HBM],
        out_specs=(VMEM,) * reps,
        scratch_shapes=[
            vmem((reps, channels, width), BF16),
            vmem(features.shape, BF16),
            vmem(sketch_matrix.shape, BF16),
            dma((chunks + 1,)),
        ],
        compiler_params=params(),
        name="sketch",
    )(me, in_hbm(features), in_hbm(sketch_matrix))
    arrived = [own[0]]
    for step in range(1, reps):
        arrived.append(lax.ppermute(own[step], "rep", pairs(step, reps)))
    hop0, send = pl.pallas_call(
        lambda *refs: pick_kernel(reps, group, *refs),
        out_shape=(out(hop_shape), out(halo_shape)),
        in_specs=[SMEM, HBM] + [VMEM] * reps,
        out_specs=(VMEM, VMEM),
        scratch_shapes=[vmem(halo_index.shape, jnp.int32), dma],
        compiler_params=params(),
        name="pick",
    )(me, in_hbm(halo_index), *arrived)
    halo0 = exchange(send, peers)

    def work(index):
        return [
            smem(tile_dst.shape, jnp.int32),
            smem(tile_src.shape, jnp.int32),
            vmem(index.shape, jnp.int32),
            vmem(tiles.shape, BF16),
            vmem((fixed, channels + EXTRA, side), BF16),
            vmem((blocks + 1, channels + EXTRA, side), F32),
            dma((3 + slots // 4,)),
        ]

    hop1, send = pl.pallas_call(
        lambda *refs: combine_pick_kernel(group, *refs),
        out_shape=(out(hop_shape), out(halo_shape)),
        in_specs=[HBM] * 4 + [VMEM] * 2,
        out_specs=(VMEM, VMEM),
        scratch_shapes=work(halo_index),
        compiler_params=params(),
        name="combine_pick",
    )(in_hbm(tile_dst), in_hbm(tile_src), in_hbm(halo_index), in_hbm(tiles), hop0, halo0)
    halo1 = exchange(send, peers)
    slot = nodes // peers
    if slot % 128 == 0 and peers & (peers - 1) == 0:
        near = max(peers // 2, 1)
        rank = lax.axis_index("dom").astype(jnp.int32).reshape(1, 1)
        two, one = out((2 * channels, slot)), out((channels, slot))
        early = pl.pallas_call(
            early_kernel,
            out_shape=(two,) * peers,
            in_specs=[SMEM, HBM, VMEM, VMEM],
            out_specs=(VMEM,) * peers,
            scratch_shapes=[
                vmem((peers, 2 * channels, slot), BF16),
                vmem(send_order.shape, jnp.int32),
                dma,
            ],
            compiler_params=params(),
            cost_estimate=cost(4 * channels * nodes * nodes, 8 * channels * nodes),
            name="early",
        )(rank, in_hbm(send_order), hop0, hop1)
        sent = [
            lax.ppermute(early[step], "dom", pairs(step, peers)) for step in range(near, peers)
        ]
        late = pl.pallas_call(
            lambda *refs: late_kernel(peers, near, *refs),
            out_shape=(out((3 * channels, slot)),) * near + (one,) * (peers - near),
            in_specs=[SMEM] + [HBM] * 4 + [VMEM] * (2 + near),
            out_specs=(VMEM,) * peers,
            scratch_shapes=[vmem((peers, channels, slot), BF16)] + work(send_order),
            compiler_params=params(),
            name="late",
        )(
            rank, in_hbm(tile_dst), in_hbm(tile_src), in_hbm(send_order), in_hbm(tiles),
            hop1, halo1, *early[:near],
        )
        order = list(range(near, peers)) + list(range(1, near))
        moved = {0: late[0]}
        for step in order:
            moved[step] = lax.ppermute(late[step], "dom", pairs(step, peers))
        return pl.pallas_call(
            lambda *refs: place_steps_kernel(peers, near, side, *refs),
            out_shape=out((3, channels, nodes)),
            in_specs=[SMEM, VMEM] + [VMEM] * (2 * peers - near),
            out_specs=HBM,
            scratch_shapes=[vmem((3, channels, nodes), BF16), dma((blocks,))],
            compiler_params=params(),
            name="place",
        )(
            rank, arrival_place, *[moved[step] for step in range(near)], *sent,
            *[moved[step] for step in range(near, peers)],
        )
    send = pl.pallas_call(
        lambda *refs: combine_last_kernel(group, *refs),
        out_shape=out(last_shape),
        in_specs=[HBM] * 4 + [VMEM] * 3,
        out_specs=VMEM,
        scratch_shapes=work(send_order),
        compiler_params=params(),
        name="combine_last",
    )(in_hbm(tile_dst), in_hbm(tile_src), in_hbm(send_order), in_hbm(tiles), hop1, halo1, hop0)
    last = exchange(send, peers)
    return pl.pallas_call(
        lambda *refs: place_kernel(side, *refs),
        out_shape=out((3, channels, nodes)),
        in_specs=[VMEM, VMEM],
        out_specs=VMEM,
        compiler_params=params(),
        name="place",
    )(arrival_place, last)


def solution(mesh):
    in_specs = (
        P(("dom", "rep"), None),
        P(),
        P("dom", None, None, None),
        P("dom", None),
        P("dom", None),
        P("dom", None),
        P("dom", None),
        P("dom", None),
    )
    out_specs = P(None, "rep", "dom")
    return jax.shard_map(
        on_device, mesh=mesh, in_specs=in_specs, out_specs=out_specs, check_vma=False
    )
```

```python
import jax
import jax.numpy as jnp
from jax import lax
from jax.experimental import pallas as pl
from jax.experimental.pallas import tpu as pltpu
from jax.sharding import PartitionSpec as P


BF16 = jnp.bfloat16
F32 = jnp.float32
EXTRA = 16
NN = (((1,), (0,)), ((), ()))
NT = (((1,), (1,)), ((), ()))
VMEM = pl.BlockSpec(memory_space=pltpu.VMEM)
SMEM = pl.BlockSpec(memory_space=pltpu.SMEM)
HBM = pl.BlockSpec(memory_space=pltpu.HBM)


def params():
    return pltpu.CompilerParams(vmem_limit_bytes=40 * 1024 * 1024)


def cost(flops, size):
    return pl.CostEstimate(flops=flops, bytes_accessed=size, transcendentals=0)


def in_hbm(array):
    return pltpu.with_memory_space_constraint(array, pltpu.HBM)


def dot(left, right, dims=NN):
    return lax.dot_general(left, right, dims, preferred_element_type=F32)


def split(index, side, blocks):
    block = jnp.zeros_like(index)
    for edge in range(1, blocks):
        block += (index >= edge * side).astype(jnp.int32)
    return block, index - block * side


def one_hot(index, rows):
    row = lax.broadcasted_iota(jnp.int32, (rows, index.shape[1]), 0)
    return jnp.where(row == index, 1.0, 0.0).astype(BF16)


def pick(stack, blocks, index, side, group):
    rows = stack.shape[0] // blocks
    parts = []
    for start in range(0, index.shape[1], group):
        block, inner = split(index[:, start : start + group], side, blocks)
        every = dot(stack, one_hot(inner, side))
        chosen = every[:rows]
        for other in range(1, blocks):
            chosen = jnp.where(block == other, every[other * rows : (other + 1) * rows], chosen)
        parts.append(chosen.astype(BF16))
    return parts


def store_slots(buffer, parts, group):
    if len(buffer.shape) == 2:
        for place, part in enumerate(parts):
            buffer[:, place * group : (place + 1) * group] = part
        return
    slot = buffer.shape[2]
    for place, part in enumerate(parts):
        for start in range(0, group, slot):
            buffer[(place * group + start) // slot] = part[:, start : start + slot]


def send_shape(channels, peers, slot):
    if slot % 128:
        return (channels, peers * slot)
    return (peers, channels, slot)


def exchange(send, peers):
    if send.ndim == 2:
        send = send.reshape(send.shape[0], peers, -1).transpose(1, 0, 2)
    arrived = lax.all_to_all(send, "dom", 0, 0, tiled=True)
    if arrived.shape[2] % 128 == 0:
        return arrived
    return arrived.transpose(1, 0, 2).reshape(arrived.shape[1], -1)


def load_wide(ref):
    if len(ref.shape) == 2:
        return ref[...]
    return jnp.concatenate([ref[peer] for peer in range(ref.shape[0])], axis=1)


def partner(me, step, count):
    if count & (count - 1) == 0:
        return me ^ step
    return lax.rem(me + step, count)


def source(me, step, count):
    if count & (count - 1) == 0:
        return me ^ step
    return lax.rem(me + count - step, count)


def pairs(step, count):
    if count & (count - 1) == 0:
        return [(rank, rank ^ step) for rank in range(count)]
    return [(rank, (rank + step) % count) for rank in range(count)]


def sketch_kernel(count, chunks, me_ref, features_in, sketch_in, *rest):
    outs, (full, features, sketch, sems) = rest[:count], rest[count:]
    channels, width = outs[0].shape
    step = width // chunks
    copies = [pltpu.make_async_copy(sketch_in, sketch, sems.at[chunks])]
    for chunk in range(chunks):
        rows = pl.ds(chunk * step, step)
        copies.append(
            pltpu.make_async_copy(features_in.at[rows, :], features.at[rows, :], sems.at[chunk])
        )
    for copy in copies:
        copy.start()
    copies[0].wait()
    for chunk in range(chunks):
        copies[chunk + 1].wait()
        rows = slice(chunk * step, (chunk + 1) * step)
        product = dot(features[rows, :], sketch[...]).T.astype(BF16)
        for part in range(count):
            full[part, :, rows] = product[part * channels : (part + 1) * channels]
    me = me_ref[0, 0]
    for part in range(count):
        outs[part][...] = full[partner(me, part, count)]


def pick_kernel(count, group, me_ref, index_in, *rest):
    arrived, (hop, send, index, sem) = rest[:count], rest[count:]
    fetch = pltpu.make_async_copy(index_in, index, sem)
    fetch.start()
    blocks, _, side = hop.shape
    per = blocks // count
    me = me_ref[0, 0]
    for step in range(count):
        first = source(me, step, count) * per
        for part in range(per):
            hop[first + part] = arrived[step][:, part * side : (part + 1) * side]
    stack = jnp.concatenate([hop[block] for block in range(blocks)], 0)
    fetch.wait()
    store_slots(send, pick(stack, blocks, index[...], side, group), group)


def combine(dst_in, src_in, index_in, tiles_in, hop, arrived_ref, scratch, store):
    dst, src, index, tiles, columns, sums, sems = scratch
    blocks, channels, side = hop.shape
    slots = tiles.shape[0]
    fixed = columns.shape[0]
    small = [
        pltpu.make_async_copy(dst_in, dst, sems.at[0]),
        pltpu.make_async_copy(src_in, src, sems.at[1]),
        pltpu.make_async_copy(index_in, index, sems.at[2]),
    ]
    chunk = 4
    large = []
    for start in range(0, slots, chunk):
        rows = pl.ds(start, chunk)
        large.append(
            pltpu.make_async_copy(tiles_in.at[rows], tiles.at[rows], sems.at[3 + start // chunk])
        )
    for copy in large + small:
        copy.start()
    columns[:, channels:, :] = jnp.ones((fixed, EXTRA, side), BF16)
    for block in range(blocks):
        columns[block, :channels, :] = hop[block]
    arrived = load_wide(arrived_ref)
    for block in range(blocks, fixed):
        start = (block - blocks) * side
        columns[block, :channels, :] = arrived[:, start : start + side]
    for slot in range(slots):
        if slot % chunk == 0:
            large[slot // chunk].wait()
        if slot < blocks:
            sums[slot] = dot(columns[slot], tiles[slot], NT)
            continue
        if slot == blocks:
            for copy in small:
                copy.wait()
        target = dst[0, slot]
        target = jnp.where(target < 0, blocks, target)
        start = slot if slot < fixed else src[0, slot]
        sums[target] = sums[target] + dot(columns[start], tiles[slot], NT)
    results = []
    for block in range(blocks):
        total = sums[block]
        result = (total[:channels] / total[channels : channels + 1]).astype(BF16)
        store(block, result)
        results.append(result)
    return results


def combine_pick_kernel(
    group, dst_in, src_in, index_in, tiles_in, hop, arrived_ref, result, send, *scratch
):
    def store(block, value):
        result[block] = value

    results = combine(dst_in, src_in, index_in, tiles_in, hop, arrived_ref, scratch, store)
    blocks, _, side = hop.shape
    index = scratch[2]
    stack = jnp.concatenate(results, 0)
    store_slots(send, pick(stack, blocks, index[...], side, group), group)


def early_kernel(me_ref, index_in, hop, near, far, full, index, sem):
    fetch = pltpu.make_async_copy(index_in, index, sem)
    fetch.start()
    blocks, _, side = hop.shape
    peers, _, slot = full.shape
    stack = jnp.concatenate([hop[block] for block in range(blocks)], 0)
    fetch.wait()
    for peer, part in enumerate(pick(stack, blocks, index[...], side, slot)):
        full[peer] = part
    me = me_ref[0, 0]
    half = peers // 2
    for step in range(half):
        near[step] = full[me ^ step]
        far[step] = full[me ^ half ^ step]


def relay_kernel(*refs):
    half = refs[0].shape[0]
    ins, outs = refs[: len(refs) - half], refs[len(refs) - half :]
    channels = ins[0].shape[1]
    for step in range(half):
        for place, blocks in enumerate(ins):
            outs[step][place * channels : (place + 1) * channels] = blocks[step]


def combine_alone_kernel(
    group, dst_in, src_in, index_in, tiles_in, hop, arrived_ref, send, *scratch
):
    results = combine(
        dst_in, src_in, index_in, tiles_in, hop, arrived_ref, scratch, lambda *_: None
    )
    blocks, _, side = hop.shape
    stack = jnp.concatenate(results, 0)
    store_slots(send, pick(stack, blocks, scratch[2][...], side, group), group)


def combine_last_kernel(
    group, dst_in, src_in, index_in, tiles_in, hop, arrived_ref, hop0, send, *scratch
):
    results = combine(
        dst_in, src_in, index_in, tiles_in, hop, arrived_ref, scratch, lambda *_: None
    )
    blocks, _, side = hop.shape
    index = scratch[2]
    stack = []
    for block in range(blocks):
        stack += [hop0[block], hop[block], results[block]]
    stack = jnp.concatenate(stack, 0)
    store_slots(send, pick(stack, blocks, index[...], side, group), group)


def place_steps_kernel(peers, side, me_ref, index_ref, *rest):
    half = peers // 2
    moved, last, (out_ref, out, sems) = rest[:half], rest[half], rest[half + 1 :]
    hops, channels, nodes = out.shape
    blocks = nodes // side
    slot = nodes // peers
    me = me_ref[0, 0]
    parts, indexes = [], []
    for step in range(peers):
        origin = me ^ step
        start = pl.multiple_of(origin * slot, slot)
        indexes.append(index_ref[:, pl.ds(start, slot)])
        first = (step // half) * channels
        from_step = moved[step % half]
        parts.append(
            jnp.concatenate(
                [
                    from_step[first + 2 * channels * hop : first + (2 * hop + 1) * channels]
                    for hop in range(hops - 1)
                ]
                + [last[origin]],
                0,
            )
        )
    block, inner = split(jnp.concatenate(indexes, 1), side, blocks)
    table = one_hot(inner, side)
    stacked = jnp.concatenate(parts, 1)
    copies = []
    for other in range(blocks):
        mask = jnp.where(block == other, 1.0, 0.0).astype(BF16)
        placed = dot(stacked * mask, table, NT).astype(BF16)
        columns = slice(other * side, (other + 1) * side)
        for hop in range(hops):
            out[hop, :, columns] = placed[hop * channels : (hop + 1) * channels]
        columns = pl.ds(other * side, side)
        copies.append(
            pltpu.make_async_copy(
                out.at[:, :, columns], out_ref.at[:, :, columns], sems.at[other]
            )
        )
        copies[-1].start()
    for copy in copies:
        copy.wait()


def place_kernel(side, index_ref, arrived_ref, out_ref):
    hops, channels, nodes = out_ref.shape
    blocks = nodes // side
    stacked = load_wide(arrived_ref)
    block, inner = split(index_ref[...], side, blocks)
    table = one_hot(inner, side)
    for other in range(blocks):
        mask = jnp.where(block == other, 1.0, 0.0).astype(BF16)
        placed = dot(stacked * mask, table, NT).astype(BF16)
        for hop in range(hops):
            out_ref[hop, :, other * side : (other + 1) * side] = placed[
                hop * channels : (hop + 1) * channels
            ]


def on_device(
    features, sketch_matrix, tiles, tile_dst, tile_src, halo_index, send_order, arrival_place
):
    reps = lax.axis_size("rep")
    peers = lax.axis_size("dom")
    width = features.shape[0]
    nodes = width * reps
    channels = sketch_matrix.shape[1] // reps
    halo = halo_index.shape[1]
    tiles = tiles[0]
    slots, side, _ = tiles.shape
    blocks = nodes // side
    fixed = (nodes + halo) // side
    me = lax.axis_index("rep").astype(jnp.int32).reshape(1, 1)
    vmem, smem, dma = pltpu.VMEM, pltpu.SMEM, pltpu.SemaphoreType.DMA
    hop_shape = (blocks, channels, side)
    halo_shape = send_shape(channels, peers, halo // peers)
    last_shape = send_shape(3 * channels, peers, nodes // peers)
    group = 256
    chunks = 4

    def out(shape):
        return jax.ShapeDtypeStruct(shape, BF16)

    def early(hop):
        shape = (peers // 2, channels, slot)
        near, far = early_call(hop, shape)
        return near, lax.ppermute(far, "dom", pairs(peers // 2, peers))

    def early_call(hop, shape):
        return pl.pallas_call(
            early_kernel,
            out_shape=(out(shape), out(shape)),
            in_specs=[SMEM, HBM, VMEM],
            out_specs=(VMEM, VMEM),
            scratch_shapes=[
                vmem((peers, channels, slot), BF16),
                vmem(send_order.shape, jnp.int32),
                dma,
            ],
            compiler_params=params(),
            cost_estimate=cost(2 * channels * nodes * nodes, 8 * channels * nodes),
            name="early",
        )(rank, in_hbm(send_order), hop)

    own = pl.pallas_call(
        lambda *refs: sketch_kernel(reps, chunks, *refs),
        out_shape=(out((channels, width)),) * reps,
        in_specs=[SMEM, HBM, HBM],
        out_specs=(VMEM,) * reps,
        scratch_shapes=[
            vmem((reps, channels, width), BF16),
            vmem(features.shape, BF16),
            vmem(sketch_matrix.shape, BF16),
            dma((chunks + 1,)),
        ],
        compiler_params=params(),
        name="sketch",
    )(me, in_hbm(features), in_hbm(sketch_matrix))
    arrived = [own[0]]
    for step in range(1, reps):
        arrived.append(lax.ppermute(own[step], "rep", pairs(step, reps)))
    hop0, send = pl.pallas_call(
        lambda *refs: pick_kernel(reps, group, *refs),
        out_shape=(out(hop_shape), out(halo_shape)),
        in_specs=[SMEM, HBM] + [VMEM] * reps,
        out_specs=(VMEM, VMEM),
        scratch_shapes=[vmem(halo_index.shape, jnp.int32), dma],
        compiler_params=params(),
        name="pick",
    )(me, in_hbm(halo_index), *arrived)
    slot = nodes // peers
    stepped = slot % 128 == 0 and peers > 1 and peers & (peers - 1) == 0
    if stepped:
        rank = lax.axis_index("dom").astype(jnp.int32).reshape(1, 1)
        early0 = early(hop0)
    halo0 = exchange(send, peers)

    def work(index):
        return [
            smem(tile_dst.shape, jnp.int32),
            smem(tile_src.shape, jnp.int32),
            vmem(index.shape, jnp.int32),
            vmem(tiles.shape, BF16),
            vmem((fixed, channels + EXTRA, side), BF16),
            vmem((blocks + 1, channels + EXTRA, side), F32),
            dma((3 + slots // 4,)),
        ]

    hop1, send = pl.pallas_call(
        lambda *refs: combine_pick_kernel(group, *refs),
        out_shape=(out(hop_shape), out(halo_shape)),
        in_specs=[HBM] * 4 + [VMEM] * 2,
        out_specs=(VMEM, VMEM),
        scratch_shapes=work(halo_index),
        compiler_params=params(),
        name="combine_pick",
    )(in_hbm(tile_dst), in_hbm(tile_src), in_hbm(halo_index), in_hbm(tiles), hop0, halo0)
    halo1 = exchange(send, peers)
    if stepped:
        half = peers // 2
        moved = pl.pallas_call(
            relay_kernel,
            out_shape=(out((4 * channels, slot)),) * half,
            in_specs=[VMEM] * 4,
            out_specs=(VMEM,) * half,
            compiler_params=params(),
            cost_estimate=cost(0, 16 * channels * nodes),
            name="relay",
        )(*early0, *early(hop1))
        moved = [moved[0]] + [
            lax.ppermute(moved[step], "dom", pairs(step, peers)) for step in range(1, half)
        ]
        send = pl.pallas_call(
            lambda *refs: combine_alone_kernel(group, *refs),
            out_shape=out((peers, channels, slot)),
            in_specs=[HBM] * 4 + [VMEM] * 2,
            out_specs=VMEM,
            scratch_shapes=work(send_order),
            compiler_params=params(),
            name="combine_last",
        )(in_hbm(tile_dst), in_hbm(tile_src), in_hbm(send_order), in_hbm(tiles), hop1, halo1)
        last = exchange(send, peers)
        return pl.pallas_call(
            lambda *refs: place_steps_kernel(peers, side, *refs),
            out_shape=out((3, channels, nodes)),
            in_specs=[SMEM, VMEM] + [VMEM] * (half + 1),
            out_specs=HBM,
            scratch_shapes=[vmem((3, channels, nodes), BF16), dma((blocks,))],
            compiler_params=params(),
            name="place",
        )(rank, arrival_place, *moved, last)
    send = pl.pallas_call(
        lambda *refs: combine_last_kernel(group, *refs),
        out_shape=out(last_shape),
        in_specs=[HBM] * 4 + [VMEM] * 3,
        out_specs=VMEM,
        scratch_shapes=work(send_order),
        compiler_params=params(),
        name="combine_last",
    )(in_hbm(tile_dst), in_hbm(tile_src), in_hbm(send_order), in_hbm(tiles), hop1, halo1, hop0)
    last = exchange(send, peers)
    return pl.pallas_call(
        lambda *refs: place_kernel(side, *refs),
        out_shape=out((3, channels, nodes)),
        in_specs=[VMEM, VMEM],
        out_specs=VMEM,
        compiler_params=params(),
        name="place",
    )(arrival_place, last)


def solution(mesh):
    in_specs = (
        P(("dom", "rep"), None),
        P(),
        P("dom", None, None, None),
        P("dom", None),
        P("dom", None),
        P("dom", None),
        P("dom", None),
        P("dom", None),
    )
    out_specs = P(None, "rep", "dom")

    return jax.shard_map(
        on_device, mesh=mesh, in_specs=in_specs, out_specs=out_specs, check_vma=False
    )
```

```python
import jax
import jax.numpy as jnp
from jax import lax
from jax.experimental import pallas as pl
from jax.experimental.pallas import tpu as pltpu
from jax.sharding import PartitionSpec as P


BF16 = jnp.bfloat16
F32 = jnp.float32
EXTRA = 16
NN = (((1,), (0,)), ((), ()))
NT = (((1,), (1,)), ((), ()))
VMEM = pl.BlockSpec(memory_space=pltpu.VMEM)
SMEM = pl.BlockSpec(memory_space=pltpu.SMEM)
HBM = pl.BlockSpec(memory_space=pltpu.HBM)


def params():
    return pltpu.CompilerParams(vmem_limit_bytes=40 * 1024 * 1024)


def cost(flops, size):
    return pl.CostEstimate(flops=flops, bytes_accessed=size, transcendentals=0)


def in_hbm(array):
    return pltpu.with_memory_space_constraint(array, pltpu.HBM)


def dot(left, right, dims=NN):
    return lax.dot_general(left, right, dims, preferred_element_type=F32)


def split(index, side, blocks):
    block = jnp.zeros_like(index)
    for edge in range(1, blocks):
        block += (index >= edge * side).astype(jnp.int32)
    return block, index - block * side


def one_hot(index, rows):
    row = lax.broadcasted_iota(jnp.int32, (rows, index.shape[1]), 0)
    return jnp.where(row == index, 1.0, 0.0).astype(BF16)


def pick(stack, blocks, index, side, group):
    rows = stack.shape[0] // blocks
    parts = []
    for start in range(0, index.shape[1], group):
        block, inner = split(index[:, start : start + group], side, blocks)
        every = dot(stack, one_hot(inner, side))
        chosen = every[:rows]
        for other in range(1, blocks):
            chosen = jnp.where(block == other, every[other * rows : (other + 1) * rows], chosen)
        parts.append(chosen.astype(BF16))
    return parts


def store_slots(buffer, parts, group):
    if len(buffer.shape) == 2:
        for place, part in enumerate(parts):
            buffer[:, place * group : (place + 1) * group] = part
        return
    slot = buffer.shape[2]
    for place, part in enumerate(parts):
        for start in range(0, group, slot):
            buffer[(place * group + start) // slot] = part[:, start : start + slot]


def send_shape(channels, peers, slot):
    if slot % 128:
        return (channels, peers * slot)
    return (peers, channels, slot)


def exchange(send, peers):
    if send.ndim == 2:
        send = send.reshape(send.shape[0], peers, -1).transpose(1, 0, 2)
    arrived = lax.all_to_all(send, "dom", 0, 0, tiled=True)
    if arrived.shape[2] % 128 == 0:
        return arrived
    return arrived.transpose(1, 0, 2).reshape(arrived.shape[1], -1)


def load_wide(ref):
    if len(ref.shape) == 2:
        return ref[...]
    return jnp.concatenate([ref[peer] for peer in range(ref.shape[0])], axis=1)


def partner(me, step, count):
    if count & (count - 1) == 0:
        return me ^ step
    return lax.rem(me + step, count)


def source(me, step, count):
    if count & (count - 1) == 0:
        return me ^ step
    return lax.rem(me + count - step, count)


def pairs(step, count):
    if count & (count - 1) == 0:
        return [(rank, rank ^ step) for rank in range(count)]
    return [(rank, (rank + step) % count) for rank in range(count)]


def sketch_kernel(count, chunks, me_ref, features_in, sketch_in, *rest):
    outs, (full, features, sketch, sems) = rest[:count], rest[count:]
    channels, width = outs[0].shape
    step = width // chunks
    copies = [pltpu.make_async_copy(sketch_in, sketch, sems.at[chunks])]
    for chunk in range(chunks):
        rows = pl.ds(chunk * step, step)
        copies.append(
            pltpu.make_async_copy(features_in.at[rows, :], features.at[rows, :], sems.at[chunk])
        )
    for copy in copies:
        copy.start()
    copies[0].wait()
    for chunk in range(chunks):
        copies[chunk + 1].wait()
        rows = slice(chunk * step, (chunk + 1) * step)
        product = dot(features[rows, :], sketch[...]).T.astype(BF16)
        for part in range(count):
            full[part, :, rows] = product[part * channels : (part + 1) * channels]
    me = me_ref[0, 0]
    for part in range(count):
        outs[part][...] = full[partner(me, part, count)]


def pick_kernel(count, group, me_ref, index_in, *rest):
    arrived, (hop, send, index, sem) = rest[:count], rest[count:]
    fetch = pltpu.make_async_copy(index_in, index, sem)
    fetch.start()
    blocks, _, side = hop.shape
    per = blocks // count
    me = me_ref[0, 0]
    for step in range(count):
        first = source(me, step, count) * per
        for part in range(per):
            hop[first + part] = arrived[step][:, part * side : (part + 1) * side]
    stack = jnp.concatenate([hop[block] for block in range(blocks)], 0)
    fetch.wait()
    store_slots(send, pick(stack, blocks, index[...], side, group), group)


def combine(dst_in, src_in, index_in, tiles_in, hop, arrived_ref, scratch, store):
    dst, src, index, tiles, columns, sums, sems = scratch
    blocks, channels, side = hop.shape
    slots = tiles.shape[0]
    fixed = columns.shape[0]
    small = [
        pltpu.make_async_copy(dst_in, dst, sems.at[0]),
        pltpu.make_async_copy(src_in, src, sems.at[1]),
        pltpu.make_async_copy(index_in, index, sems.at[2]),
    ]
    chunk = 4
    large = []
    for start in range(0, slots, chunk):
        rows = pl.ds(start, chunk)
        large.append(
            pltpu.make_async_copy(tiles_in.at[rows], tiles.at[rows], sems.at[3 + start // chunk])
        )
    for copy in large + small:
        copy.start()
    columns[:, channels:, :] = jnp.ones((fixed, EXTRA, side), BF16)
    for block in range(blocks):
        columns[block, :channels, :] = hop[block]
    arrived = load_wide(arrived_ref)
    for block in range(blocks, fixed):
        start = (block - blocks) * side
        columns[block, :channels, :] = arrived[:, start : start + side]
    for slot in range(slots):
        if slot % chunk == 0:
            large[slot // chunk].wait()
        if slot < blocks:
            sums[slot] = dot(columns[slot], tiles[slot], NT)
            continue
        if slot == blocks:
            for copy in small:
                copy.wait()
        target = dst[0, slot]
        target = jnp.where(target < 0, blocks, target)
        start = slot if slot < fixed else src[0, slot]
        sums[target] = sums[target] + dot(columns[start], tiles[slot], NT)
    results = []
    for block in range(blocks):
        total = sums[block]
        result = (total[:channels] / total[channels : channels + 1]).astype(BF16)
        store(block, result)
        results.append(result)
    return results


def combine_pick_kernel(
    group, dst_in, src_in, index_in, tiles_in, hop, arrived_ref, result, send, *scratch
):
    def store(block, value):
        result[block] = value

    results = combine(dst_in, src_in, index_in, tiles_in, hop, arrived_ref, scratch, store)
    blocks, _, side = hop.shape
    index = scratch[2]
    stack = jnp.concatenate(results, 0)
    store_slots(send, pick(stack, blocks, index[...], side, group), group)


def early_kernel(staged, me_ref, index_in, tiles_in, hop, near, far, total, *rest):
    full, index, tiles, sems = rest[-4:]
    blocks, _, side = hop.shape
    copies = [
        pltpu.make_async_copy(index_in, index, sems.at[0]),
        pltpu.make_async_copy(tiles_in.at[pl.ds(0, blocks)], tiles, sems.at[1]),
    ]
    if staged:
        others = tiles_in.shape[0] - blocks
        copies.append(
            pltpu.make_async_copy(tiles_in.at[pl.ds(blocks, others)], rest[0], sems.at[2])
        )
    for copy in copies:
        copy.start()
    peers, _, slot = full.shape
    stack = jnp.concatenate([hop[block] for block in range(blocks)], 0)
    copies[0].wait()
    for peer, part in enumerate(pick(stack, blocks, index[...], side, slot)):
        full[peer] = part
    me = me_ref[0, 0]
    half = peers // 2
    for step in range(half):
        near[step] = full[me ^ step]
        far[step] = full[me ^ half ^ step]
    ones = jnp.ones((EXTRA, side), BF16)
    copies[1].wait()
    for block in range(blocks):
        columns = jnp.concatenate([hop[block], ones], 0)
        total[block] = dot(columns, tiles[block], NT)
    if staged:
        copies[2].wait()


def finish(dst, src, tiles, total, hop, arrived, columns, sums):
    blocks, channels, side = hop.shape
    fixed = columns.shape[0]
    columns[:, channels:, :] = jnp.ones((fixed, EXTRA, side), BF16)
    for block in range(blocks):
        columns[block, :channels, :] = hop[block]
        sums[block] = total[block]
    wide = load_wide(arrived)
    for block in range(blocks, fixed):
        start = (block - blocks) * side
        columns[block, :channels, :] = wide[:, start : start + side]
    for other in range(tiles.shape[0]):
        slot = blocks + other
        target = dst[0, slot]
        target = jnp.where(target < 0, blocks, target)
        start = slot if slot < fixed else src[0, slot]
        sums[target] = sums[target] + dot(columns[start], tiles[other], NT)
    results = []
    for block in range(blocks):
        whole = sums[block]
        results.append((whole[:channels] / whole[channels : channels + 1]).astype(BF16))
    return results


def finish_kernel(
    group, keep, dst, src, index, tiles, total, hop, arrived, *rest
):
    columns, sums = rest[-2:]
    send = rest[-3]
    results = finish(dst, src, tiles, total, hop, arrived, columns, sums)
    blocks, _, side = hop.shape
    if keep:
        for block, result in enumerate(results):
            rest[0][block] = result
    stack = jnp.concatenate(results, 0)
    store_slots(send, pick(stack, blocks, index[...], side, group), group)


def relay_kernel(*refs):
    half = refs[0].shape[0]
    ins, outs = refs[: len(refs) - half], refs[len(refs) - half :]
    channels = ins[0].shape[1]
    for step in range(half):
        for place, blocks in enumerate(ins):
            outs[step][place * channels : (place + 1) * channels] = blocks[step]


def combine_last_kernel(
    group, dst_in, src_in, index_in, tiles_in, hop, arrived_ref, hop0, send, *scratch
):
    results = combine(
        dst_in, src_in, index_in, tiles_in, hop, arrived_ref, scratch, lambda *_: None
    )
    blocks, _, side = hop.shape
    index = scratch[2]
    stack = []
    for block in range(blocks):
        stack += [hop0[block], hop[block], results[block]]
    stack = jnp.concatenate(stack, 0)
    store_slots(send, pick(stack, blocks, index[...], side, group), group)


def place_steps_kernel(peers, side, me_ref, index_ref, *rest):
    half = peers // 2
    moved, last, (out_ref, out, sems) = rest[:half], rest[half], rest[half + 1 :]
    hops, channels, nodes = out.shape
    blocks = nodes // side
    slot = nodes // peers
    me = me_ref[0, 0]
    parts, indexes = [], []
    for step in range(peers):
        origin = me ^ step
        start = pl.multiple_of(origin * slot, slot)
        indexes.append(index_ref[:, pl.ds(start, slot)])
        first = (step // half) * channels
        from_step = moved[step % half]
        parts.append(
            jnp.concatenate(
                [
                    from_step[first + 2 * channels * hop : first + (2 * hop + 1) * channels]
                    for hop in range(hops - 1)
                ]
                + [last[origin]],
                0,
            )
        )
    block, inner = split(jnp.concatenate(indexes, 1), side, blocks)
    table = one_hot(inner, side)
    stacked = jnp.concatenate(parts, 1)
    copies = []
    for other in range(blocks):
        mask = jnp.where(block == other, 1.0, 0.0).astype(BF16)
        placed = dot(stacked * mask, table, NT).astype(BF16)
        columns = slice(other * side, (other + 1) * side)
        for hop in range(hops):
            out[hop, :, columns] = placed[hop * channels : (hop + 1) * channels]
        columns = pl.ds(other * side, side)
        copies.append(
            pltpu.make_async_copy(
                out.at[:, :, columns], out_ref.at[:, :, columns], sems.at[other]
            )
        )
        copies[-1].start()
    for copy in copies:
        copy.wait()


def place_kernel(side, index_ref, arrived_ref, out_ref):
    hops, channels, nodes = out_ref.shape
    blocks = nodes // side
    stacked = load_wide(arrived_ref)
    block, inner = split(index_ref[...], side, blocks)
    table = one_hot(inner, side)
    for other in range(blocks):
        mask = jnp.where(block == other, 1.0, 0.0).astype(BF16)
        placed = dot(stacked * mask, table, NT).astype(BF16)
        for hop in range(hops):
            out_ref[hop, :, other * side : (other + 1) * side] = placed[
                hop * channels : (hop + 1) * channels
            ]


def on_device(
    features, sketch_matrix, tiles, tile_dst, tile_src, halo_index, send_order, arrival_place
):
    reps = lax.axis_size("rep")
    peers = lax.axis_size("dom")
    width = features.shape[0]
    nodes = width * reps
    channels = sketch_matrix.shape[1] // reps
    halo = halo_index.shape[1]
    tiles = tiles[0]
    slots, side, _ = tiles.shape
    blocks = nodes // side
    fixed = (nodes + halo) // side
    me = lax.axis_index("rep").astype(jnp.int32).reshape(1, 1)
    vmem, smem, dma = pltpu.VMEM, pltpu.SMEM, pltpu.SemaphoreType.DMA
    hop_shape = (blocks, channels, side)
    halo_shape = send_shape(channels, peers, halo // peers)
    last_shape = send_shape(3 * channels, peers, nodes // peers)
    group = 256
    chunks = 4

    def out(shape):
        return jax.ShapeDtypeStruct(shape, BF16)

    def early(hop, staged):
        shape = (peers // 2, channels, slot)
        others = (slots - blocks, side, side)
        near, far, total, *rest = pl.pallas_call(
            lambda *refs: early_kernel(staged, *refs),
            out_shape=(
                out(shape),
                out(shape),
                jax.ShapeDtypeStruct((blocks, channels + EXTRA, side), F32),
            )
            + (out(others),) * staged,
            in_specs=[SMEM, HBM, HBM, VMEM],
            out_specs=(VMEM,) * (3 + staged),
            scratch_shapes=[
                vmem((peers, channels, slot), BF16),
                vmem(send_order.shape, jnp.int32),
                vmem((blocks, side, side), BF16),
                dma((3,)),
            ],
            compiler_params=params(),
            cost_estimate=cost(2 * channels * nodes * nodes, 8 * channels * nodes),
            name="early",
        )(rank, in_hbm(send_order), in_hbm(tiles), hop)
        sent = lax.ppermute(far, "dom", pairs(peers // 2, peers))
        return (near, sent), total, rest

    def late(keep, index, others, total, hop, arrived):
        shape = (peers, channels, index.shape[1] // peers)
        return pl.pallas_call(
            lambda *refs: finish_kernel(group, keep, *refs),
            out_shape=(out(hop_shape),) * keep + (out(shape),),
            in_specs=[SMEM, SMEM] + [VMEM] * 5,
            out_specs=(VMEM,) * (keep + 1),
            scratch_shapes=[
                vmem((fixed, channels + EXTRA, side), BF16),
                vmem((blocks + 1, channels + EXTRA, side), F32),
            ],
            compiler_params=params(),
        )(tile_dst, tile_src, index, others, total, hop, arrived)

    own = pl.pallas_call(
        lambda *refs: sketch_kernel(reps, chunks, *refs),
        out_shape=(out((channels, width)),) * reps,
        in_specs=[SMEM, HBM, HBM],
        out_specs=(VMEM,) * reps,
        scratch_shapes=[
            vmem((reps, channels, width), BF16),
            vmem(features.shape, BF16),
            vmem(sketch_matrix.shape, BF16),
            dma((chunks + 1,)),
        ],
        compiler_params=params(),
        name="sketch",
    )(me, in_hbm(features), in_hbm(sketch_matrix))
    arrived = [own[0]]
    for step in range(1, reps):
        arrived.append(lax.ppermute(own[step], "rep", pairs(step, reps)))
    hop0, send = pl.pallas_call(
        lambda *refs: pick_kernel(reps, group, *refs),
        out_shape=(out(hop_shape), out(halo_shape)),
        in_specs=[SMEM, HBM] + [VMEM] * reps,
        out_specs=(VMEM, VMEM),
        scratch_shapes=[vmem(halo_index.shape, jnp.int32), dma],
        compiler_params=params(),
        name="pick",
    )(me, in_hbm(halo_index), *arrived)
    slot = nodes // peers
    whole_lanes = slot % 128 == 0 and (halo // peers) % 128 == 0
    if whole_lanes and peers > 1 and peers & (peers - 1) == 0:
        half = peers // 2
        rank = lax.axis_index("dom").astype(jnp.int32).reshape(1, 1)
        halo0 = exchange(send, peers)
        early0, total, others = early(hop0, 1)
        others = others[0]
        hop1, send = late(1, halo_index, others, total, hop0, halo0)
        halo1 = exchange(send, peers)
        early1, total, _ = early(hop1, 0)
        (send,) = late(0, send_order, others, total, hop1, halo1)
        last = exchange(send, peers)
        moved = pl.pallas_call(
            relay_kernel,
            out_shape=(out((4 * channels, slot)),) * half,
            in_specs=[VMEM] * 4,
            out_specs=(VMEM,) * half,
            compiler_params=params(),
            cost_estimate=cost(0, 16 * channels * nodes),
            name="relay",
        )(*early0, *early1)
        moved = [moved[0]] + [
            lax.ppermute(moved[step], "dom", pairs(step, peers)) for step in range(1, half)
        ]
        return pl.pallas_call(
            lambda *refs: place_steps_kernel(peers, side, *refs),
            out_shape=out((3, channels, nodes)),
            in_specs=[SMEM, VMEM] + [VMEM] * (half + 1),
            out_specs=HBM,
            scratch_shapes=[vmem((3, channels, nodes), BF16), dma((blocks,))],
            compiler_params=params(),
            name="place",
        )(rank, arrival_place, *moved, last)
    halo0 = exchange(send, peers)

    def work(index):
        return [
            smem(tile_dst.shape, jnp.int32),
            smem(tile_src.shape, jnp.int32),
            vmem(index.shape, jnp.int32),
            vmem(tiles.shape, BF16),
            vmem((fixed, channels + EXTRA, side), BF16),
            vmem((blocks + 1, channels + EXTRA, side), F32),
            dma((3 + slots // 4,)),
        ]

    hop1, send = pl.pallas_call(
        lambda *refs: combine_pick_kernel(group, *refs),
        out_shape=(out(hop_shape), out(halo_shape)),
        in_specs=[HBM] * 4 + [VMEM] * 2,
        out_specs=(VMEM, VMEM),
        scratch_shapes=work(halo_index),
        compiler_params=params(),
        name="combine_pick",
    )(in_hbm(tile_dst), in_hbm(tile_src), in_hbm(halo_index), in_hbm(tiles), hop0, halo0)
    halo1 = exchange(send, peers)
    send = pl.pallas_call(
        lambda *refs: combine_last_kernel(group, *refs),
        out_shape=out(last_shape),
        in_specs=[HBM] * 4 + [VMEM] * 3,
        out_specs=VMEM,
        scratch_shapes=work(send_order),
        compiler_params=params(),
        name="combine_last",
    )(in_hbm(tile_dst), in_hbm(tile_src), in_hbm(send_order), in_hbm(tiles), hop1, halo1, hop0)
    last = exchange(send, peers)
    return pl.pallas_call(
        lambda *refs: place_kernel(side, *refs),
        out_shape=out((3, channels, nodes)),
        in_specs=[VMEM, VMEM],
        out_specs=VMEM,
        compiler_params=params(),
        name="place",
    )(arrival_place, last)


def solution(mesh):
    in_specs = (
        P(("dom", "rep"), None),
        P(),
        P("dom", None, None, None),
        P("dom", None),
        P("dom", None),
        P("dom", None),
        P("dom", None),
        P("dom", None),
    )
    out_specs = P(None, "rep", "dom")

    return jax.shard_map(
        on_device, mesh=mesh, in_specs=in_specs, out_specs=out_specs, check_vma=False
    )
```

```python
import jax
import jax.numpy as jnp
from jax import lax
from jax.experimental import pallas as pl
from jax.experimental.pallas import tpu as pltpu
from jax.sharding import PartitionSpec as P


BF16 = jnp.bfloat16
F32 = jnp.float32
EXTRA = 16
NN = (((1,), (0,)), ((), ()))
NT = (((1,), (1,)), ((), ()))
VMEM = pl.BlockSpec(memory_space=pltpu.VMEM)
HBM = pl.BlockSpec(memory_space=pltpu.HBM)
ANY = pl.BlockSpec(memory_space=pl.ANY)


def params():
    return pltpu.CompilerParams(vmem_limit_bytes=40 * 1024 * 1024)


def cost(flops, size):
    return pl.CostEstimate(flops=flops, bytes_accessed=size, transcendentals=0)


def in_hbm(array):
    return pltpu.with_memory_space_constraint(array, pltpu.HBM)


def dot(left, right, dims=NN):
    return lax.dot_general(left, right, dims, preferred_element_type=F32)


def split(index, side, blocks):
    block = jnp.zeros_like(index)
    for edge in range(1, blocks):
        block += (index >= edge * side).astype(jnp.int32)
    return block, index - block * side


def one_hot(index, rows):
    row = lax.broadcasted_iota(jnp.int32, (rows, index.shape[1]), 0)
    return jnp.where(row == index, 1.0, 0.0).astype(BF16)


def pick(stack, blocks, index, side, group):
    rows = stack.shape[0] // blocks
    parts = []
    for start in range(0, index.shape[1], group):
        block, inner = split(index[:, start : start + group], side, blocks)
        every = dot(stack, one_hot(inner, side))
        chosen = every[:rows]
        for other in range(1, blocks):
            chosen = jnp.where(block == other, every[other * rows : (other + 1) * rows], chosen)
        parts.append(chosen.astype(BF16))
    return parts


def store_slots(buffer, parts, group):
    if len(buffer.shape) == 2:
        for place, part in enumerate(parts):
            buffer[:, place * group : (place + 1) * group] = part
        return
    slot = buffer.shape[2]
    for place, part in enumerate(parts):
        for start in range(0, group, slot):
            buffer[(place * group + start) // slot] = part[:, start : start + slot]


def send_shape(channels, peers, slot):
    if slot % 128:
        return (channels, peers * slot)
    return (peers, channels, slot)


def exchange(send, peers):
    if send.ndim == 2:
        send = send.reshape(send.shape[0], peers, -1).transpose(1, 0, 2)
    arrived = lax.all_to_all(send, "dom", 0, 0, tiled=True)
    if arrived.shape[2] % 128 == 0:
        return arrived
    return arrived.transpose(1, 0, 2).reshape(arrived.shape[1], -1)


def load_wide(ref):
    if len(ref.shape) == 2:
        return ref[...]
    return jnp.concatenate([ref[peer] for peer in range(ref.shape[0])], axis=1)


def partner(me, step, count):
    if count & (count - 1) == 0:
        return me ^ step
    return lax.rem(me + step, count)


def source(me, step, count):
    if count & (count - 1) == 0:
        return me ^ step
    return lax.rem(me + count - step, count)


def pairs(step, count):
    if count & (count - 1) == 0:
        return [(rank, rank ^ step) for rank in range(count)]
    return [(rank, (rank + step) % count) for rank in range(count)]


def sketch_kernel(count, chunks, features_in, sketch_in, index_in, *rest):
    outs, (index_out, full, features, sketch, sems) = rest[:count], rest[count:]
    channels, width = outs[0].shape
    step = width // chunks
    copies = [pltpu.make_async_copy(sketch_in, sketch, sems.at[chunks])]
    for chunk in range(chunks):
        rows = pl.ds(chunk * step, step)
        copies.append(
            pltpu.make_async_copy(features_in.at[rows, :], features.at[rows, :], sems.at[chunk])
        )
    copies.append(pltpu.make_async_copy(index_in, index_out, sems.at[chunks + 1]))
    for copy in copies:
        copy.start()
    copies[0].wait()
    for chunk in range(chunks):
        copies[chunk + 1].wait()
        rows = slice(chunk * step, (chunk + 1) * step)
        product = dot(features[rows, :], sketch[...]).T.astype(BF16)
        for part in range(count):
            full[part, :, rows] = product[part * channels : (part + 1) * channels]
    me = lax.axis_index("rep")
    for part in range(count):
        outs[part][...] = full[partner(me, part, count)]
    copies[-1].wait()


def pick_kernel(count, group, index, *rest):
    arrived, (hop, send) = rest[:count], rest[count:]
    blocks, _, side = hop.shape
    per = blocks // count
    me = lax.axis_index("rep")
    for step in range(count):
        first = source(me, step, count) * per
        for part in range(per):
            hop[first + part] = arrived[step][:, part * side : (part + 1) * side]
    stack = jnp.concatenate([hop[block] for block in range(blocks)], 0)
    store_slots(send, pick(stack, blocks, index[...], side, group), group)


def combine(dst_in, src_in, index_in, tiles_in, hop, arrived_ref, scratch, store):
    dst, src, index, tiles, columns, sums, sems = scratch
    blocks, channels, side = hop.shape
    slots = tiles.shape[0]
    fixed = columns.shape[0]
    small = [
        pltpu.make_async_copy(dst_in, dst, sems.at[0]),
        pltpu.make_async_copy(src_in, src, sems.at[1]),
        pltpu.make_async_copy(index_in, index, sems.at[2]),
    ]
    chunk = 4
    large = []
    for start in range(0, slots, chunk):
        rows = pl.ds(start, chunk)
        large.append(
            pltpu.make_async_copy(tiles_in.at[rows], tiles.at[rows], sems.at[3 + start // chunk])
        )
    for copy in large + small:
        copy.start()
    columns[:, channels:, :] = jnp.ones((fixed, EXTRA, side), BF16)
    for block in range(blocks):
        columns[block, :channels, :] = hop[block]
    arrived = load_wide(arrived_ref)
    for block in range(blocks, fixed):
        start = (block - blocks) * side
        columns[block, :channels, :] = arrived[:, start : start + side]
    for slot in range(slots):
        if slot % chunk == 0:
            large[slot // chunk].wait()
        if slot < blocks:
            sums[slot] = dot(columns[slot], tiles[slot], NT)
            continue
        if slot == blocks:
            for copy in small:
                copy.wait()
        target = dst[0, slot]
        target = jnp.where(target < 0, blocks, target)
        start = slot if slot < fixed else src[0, slot]
        sums[target] = sums[target] + dot(columns[start], tiles[slot], NT)
    results = []
    for block in range(blocks):
        total = sums[block]
        result = (total[:channels] / total[channels : channels + 1]).astype(BF16)
        store(block, result)
        results.append(result)
    return results


def combine_pick_kernel(
    group, dst_in, src_in, index_in, tiles_in, hop, arrived_ref, result, send, *scratch
):
    def store(block, value):
        result[block] = value

    results = combine(dst_in, src_in, index_in, tiles_in, hop, arrived_ref, scratch, store)
    blocks, _, side = hop.shape
    index = scratch[2]
    stack = jnp.concatenate(results, 0)
    store_slots(send, pick(stack, blocks, index[...], side, group), group)


def early_kernel(staged, index_in, tiles_in, hop, near, far, total, *rest):
    full, index, tiles, sems = rest[-4:]
    blocks, _, side = hop.shape
    copies = [
        pltpu.make_async_copy(index_in, index, sems.at[0]),
        pltpu.make_async_copy(tiles_in.at[pl.ds(0, blocks)], tiles, sems.at[1]),
    ]
    if staged:
        others = tiles_in.shape[0] - blocks
        copies.append(
            pltpu.make_async_copy(tiles_in.at[pl.ds(blocks, others)], rest[0], sems.at[2])
        )
    for copy in copies:
        copy.start()
    peers, _, slot = full.shape
    stack = jnp.concatenate([hop[block] for block in range(blocks)], 0)
    copies[0].wait()
    for peer, part in enumerate(pick(stack, blocks, index[...], side, slot)):
        full[peer] = part
    me = lax.axis_index("dom")
    half = peers // 2
    for step in range(half):
        near[step] = full[me ^ step]
        far[step] = full[me ^ half ^ step]
    ones = jnp.ones((EXTRA, side), BF16)
    copies[1].wait()
    for block in range(blocks):
        columns = jnp.concatenate([hop[block], ones], 0)
        total[block] = dot(columns, tiles[block], NT)
    if staged:
        copies[2].wait()


def finish(dst_in, src_in, tiles, total, hop, arrived, columns, sums, products, dst, src, sems):
    blocks, channels, side = hop.shape
    fixed = columns.shape[0]
    copies = [
        pltpu.make_async_copy(dst_in, dst, sems.at[0]),
        pltpu.make_async_copy(src_in, src, sems.at[1]),
    ]
    for copy in copies:
        copy.start()
    columns[:, channels:, :] = jnp.ones((fixed, EXTRA, side), BF16)
    for block in range(blocks):
        columns[block, :channels, :] = hop[block]
        sums[block] = total[block]
    wide = load_wide(arrived)
    for block in range(blocks, fixed):
        start = (block - blocks) * side
        columns[block, :channels, :] = wide[:, start : start + side]
    for other in range(fixed - blocks):
        products[other] = dot(columns[blocks + other], tiles[other], NT)
    for copy in copies:
        copy.wait()
    for other in range(tiles.shape[0]):
        slot = blocks + other
        target = dst[0, slot]
        target = jnp.where(target < 0, blocks, target)
        if slot < fixed:
            product = products[other]
        else:
            product = dot(columns[src[0, slot]], tiles[other], NT)
        sums[target] = sums[target] + product
    results = []
    for block in range(blocks):
        whole = sums[block]
        results.append((whole[:channels] / whole[channels : channels + 1]).astype(BF16))
    return results


def finish_kernel(
    group, keep, dst, src, index, tiles, total, hop, arrived, *rest
):
    send, scratch = rest[keep], rest[keep + 1 :]
    results = finish(dst, src, tiles, total, hop, arrived, *scratch)
    blocks, _, side = hop.shape
    if keep:
        for block, result in enumerate(results):
            rest[0][block] = result
    stack = jnp.concatenate(results, 0)
    store_slots(send, pick(stack, blocks, index[...], side, group), group)


def relay_kernel(*refs):
    half = refs[0].shape[0]
    ins, outs = refs[: len(refs) - half], refs[len(refs) - half :]
    channels = ins[0].shape[1]
    for step in range(half):
        for place, blocks in enumerate(ins):
            outs[step][place * channels : (place + 1) * channels] = blocks[step]


def combine_last_kernel(
    group, dst_in, src_in, index_in, tiles_in, hop, arrived_ref, hop0, send, *scratch
):
    results = combine(
        dst_in, src_in, index_in, tiles_in, hop, arrived_ref, scratch, lambda *_: None
    )
    blocks, _, side = hop.shape
    index = scratch[2]
    stack = []
    for block in range(blocks):
        stack += [hop0[block], hop[block], results[block]]
    stack = jnp.concatenate(stack, 0)
    store_slots(send, pick(stack, blocks, index[...], side, group), group)


def place_steps_kernel(peers, side, index_ref, *rest):
    half = peers // 2
    moved, last, (out_ref, out, sems) = rest[:half], rest[half], rest[half + 1 :]
    hops, channels, nodes = out.shape
    blocks = nodes // side
    slot = nodes // peers
    me = lax.axis_index("dom")
    parts, indexes = [], []
    for step in range(peers):
        origin = me ^ step
        start = pl.multiple_of(origin * slot, slot)
        indexes.append(index_ref[:, pl.ds(start, slot)])
        first = (step // half) * channels
        from_step = moved[step % half]
        parts.append(
            jnp.concatenate(
                [
                    from_step[first + 2 * channels * hop : first + (2 * hop + 1) * channels]
                    for hop in range(hops - 1)
                ]
                + [last[origin]],
                0,
            )
        )
    block, inner = split(jnp.concatenate(indexes, 1), side, blocks)
    table = jnp.concatenate(
        [one_hot(inner[:, start : start + side], side).T for start in range(0, nodes, side)], 0
    )
    stacked = jnp.concatenate(parts, 1)
    copies = []
    for other in range(blocks):
        mask = jnp.where(block == other, 1.0, 0.0).astype(BF16)
        placed = dot(stacked * mask, table).astype(BF16)
        columns = slice(other * side, (other + 1) * side)
        for hop in range(hops):
            out[hop, :, columns] = placed[hop * channels : (hop + 1) * channels]
        columns = pl.ds(other * side, side)
        copies.append(
            pltpu.make_async_copy(
                out.at[:, :, columns], out_ref.at[:, :, columns], sems.at[other]
            )
        )
        copies[-1].start()
    for copy in copies:
        copy.wait()


def place_kernel(side, index_ref, arrived_ref, out_ref):
    hops, channels, nodes = out_ref.shape
    blocks = nodes // side
    stacked = load_wide(arrived_ref)
    block, inner = split(index_ref[...], side, blocks)
    table = one_hot(inner, side)
    for other in range(blocks):
        mask = jnp.where(block == other, 1.0, 0.0).astype(BF16)
        placed = dot(stacked * mask, table, NT).astype(BF16)
        for hop in range(hops):
            out_ref[hop, :, other * side : (other + 1) * side] = placed[
                hop * channels : (hop + 1) * channels
            ]


def on_device(
    features, sketch_matrix, tiles, tile_dst, tile_src, halo_index, send_order, arrival_place
):
    reps = lax.axis_size("rep")
    peers = lax.axis_size("dom")
    width = features.shape[0]
    nodes = width * reps
    channels = sketch_matrix.shape[1] // reps
    halo = halo_index.shape[1]
    tiles = tiles[0]
    slots, side, _ = tiles.shape
    blocks = nodes // side
    fixed = (nodes + halo) // side
    vmem, smem, dma = pltpu.VMEM, pltpu.SMEM, pltpu.SemaphoreType.DMA
    hop_shape = (blocks, channels, side)
    halo_shape = send_shape(channels, peers, halo // peers)
    last_shape = send_shape(3 * channels, peers, nodes // peers)
    group = 256
    chunks = 4

    def out(shape):
        return jax.ShapeDtypeStruct(shape, BF16)

    def early(hop, staged):
        shape = (peers // 2, channels, slot)
        others = (slots - blocks, side, side)
        near, far, total, *rest = pl.pallas_call(
            lambda *refs: early_kernel(staged, *refs),
            out_shape=(
                out(shape),
                out(shape),
                jax.ShapeDtypeStruct((blocks, channels + EXTRA, side), F32),
            )
            + (out(others),) * staged,
            in_specs=[HBM, HBM, VMEM],
            out_specs=(VMEM,) * (3 + staged),
            scratch_shapes=[
                vmem((peers, channels, slot), BF16),
                vmem(send_order.shape, jnp.int32),
                vmem((blocks, side, side), BF16),
                dma((3,)),
            ],
            compiler_params=params(),
            cost_estimate=cost(2 * channels * nodes * nodes, 8 * channels * nodes),
            name="early",
        )(in_hbm(send_order), in_hbm(tiles), hop)
        sent = lax.ppermute(far, "dom", pairs(peers // 2, peers))
        return (near, sent), total, rest

    def late(keep, index, others, total, hop, arrived):
        shape = (peers, channels, index.shape[1] // peers)
        return pl.pallas_call(
            lambda *refs: finish_kernel(group, keep, *refs),
            out_shape=(out(hop_shape),) * keep + (out(shape),),
            in_specs=[ANY] * 2 + [VMEM] * 5,
            out_specs=(VMEM,) * (keep + 1),
            scratch_shapes=[
                vmem((fixed, channels + EXTRA, side), BF16),
                vmem((blocks + 1, channels + EXTRA, side), F32),
                vmem((fixed - blocks, channels + EXTRA, side), F32),
                smem(tile_dst.shape, jnp.int32),
                smem(tile_src.shape, jnp.int32),
                dma((2,)),
            ],
            compiler_params=params(),
        )(tile_dst, tile_src, index, others, total, hop, arrived)

    *own, halo_rows = pl.pallas_call(
        lambda *refs: sketch_kernel(reps, chunks, *refs),
        out_shape=(out((channels, width)),) * reps
        + (jax.ShapeDtypeStruct(halo_index.shape, jnp.int32),),
        in_specs=[HBM] * 3,
        out_specs=(VMEM,) * (reps + 1),
        scratch_shapes=[
            vmem((reps, channels, width), BF16),
            vmem(features.shape, BF16),
            vmem(sketch_matrix.shape, BF16),
            dma((chunks + 2,)),
        ],
        compiler_params=params(),
        name="sketch",
    )(in_hbm(features), in_hbm(sketch_matrix), in_hbm(halo_index))
    arrived = [own[0]]
    for step in range(1, reps):
        arrived.append(lax.ppermute(own[step], "rep", pairs(step, reps)))
    hop0, send = pl.pallas_call(
        lambda *refs: pick_kernel(reps, group, *refs),
        out_shape=(out(hop_shape), out(halo_shape)),
        in_specs=[VMEM] * (reps + 1),
        out_specs=(VMEM, VMEM),
        compiler_params=params(),
        name="pick",
    )(halo_rows, *arrived)
    slot = nodes // peers
    whole_lanes = slot % 128 == 0 and (halo // peers) % 128 == 0
    if whole_lanes and peers > 1 and peers & (peers - 1) == 0:
        half = peers // 2
        halo0 = exchange(send, peers)
        early0, total, others = early(hop0, 1)
        others = others[0]
        hop1, send = late(1, halo_rows, others, total, hop0, halo0)
        halo1 = exchange(send, peers)
        early1, total, _ = early(hop1, 0)
        (send,) = late(0, send_order, others, total, hop1, halo1)
        last = exchange(send, peers)
        moved = pl.pallas_call(
            relay_kernel,
            out_shape=(out((4 * channels, slot)),) * half,
            in_specs=[VMEM] * 4,
            out_specs=(VMEM,) * half,
            compiler_params=params(),
            cost_estimate=cost(0, 16 * channels * nodes),
            name="relay",
        )(*early0, *early1)
        moved = [moved[0]] + [
            lax.ppermute(moved[step], "dom", pairs(step, peers)) for step in range(1, half)
        ]
        return pl.pallas_call(
            lambda *refs: place_steps_kernel(peers, side, *refs),
            out_shape=out((3, channels, nodes)),
            in_specs=[VMEM] * (half + 2),
            out_specs=HBM,
            scratch_shapes=[vmem((3, channels, nodes), BF16), dma((blocks,))],
            compiler_params=params(),
            name="place",
        )(arrival_place, *moved, last)
    halo0 = exchange(send, peers)

    def work(index):
        return [
            smem(tile_dst.shape, jnp.int32),
            smem(tile_src.shape, jnp.int32),
            vmem(index.shape, jnp.int32),
            vmem(tiles.shape, BF16),
            vmem((fixed, channels + EXTRA, side), BF16),
            vmem((blocks + 1, channels + EXTRA, side), F32),
            dma((3 + slots // 4,)),
        ]

    hop1, send = pl.pallas_call(
        lambda *refs: combine_pick_kernel(group, *refs),
        out_shape=(out(hop_shape), out(halo_shape)),
        in_specs=[HBM] * 4 + [VMEM] * 2,
        out_specs=(VMEM, VMEM),
        scratch_shapes=work(halo_index),
        compiler_params=params(),
        name="combine_pick",
    )(in_hbm(tile_dst), in_hbm(tile_src), in_hbm(halo_index), in_hbm(tiles), hop0, halo0)
    halo1 = exchange(send, peers)
    send = pl.pallas_call(
        lambda *refs: combine_last_kernel(group, *refs),
        out_shape=out(last_shape),
        in_specs=[HBM] * 4 + [VMEM] * 3,
        out_specs=VMEM,
        scratch_shapes=work(send_order),
        compiler_params=params(),
        name="combine_last",
    )(in_hbm(tile_dst), in_hbm(tile_src), in_hbm(send_order), in_hbm(tiles), hop1, halo1, hop0)
    last = exchange(send, peers)
    return pl.pallas_call(
        lambda *refs: place_kernel(side, *refs),
        out_shape=out((3, channels, nodes)),
        in_specs=[VMEM, VMEM],
        out_specs=VMEM,
        compiler_params=params(),
        name="place",
    )(arrival_place, last)


def solution(mesh):
    in_specs = (
        P(("dom", "rep"), None),
        P(),
        P("dom", None, None, None),
        P("dom", None),
        P("dom", None),
        P("dom", None),
        P("dom", None),
        P("dom", None),
    )
    out_specs = P(None, "rep", "dom")

    return jax.shard_map(
        on_device, mesh=mesh, in_specs=in_specs, out_specs=out_specs, check_vma=False
    )
```

```python
import jax
import jax.numpy as jnp
from jax import lax
from jax.experimental import pallas as pl
from jax.experimental.pallas import tpu as pltpu
from jax.sharding import PartitionSpec as P


BF16 = jnp.bfloat16
F32 = jnp.float32
EXTRA = 16
NN = (((1,), (0,)), ((), ()))
NT = (((1,), (1,)), ((), ()))
VMEM = pl.BlockSpec(memory_space=pltpu.VMEM)
HBM = pl.BlockSpec(memory_space=pltpu.HBM)


def params():
    return pltpu.CompilerParams(vmem_limit_bytes=40 * 1024 * 1024)


def cost(flops, size):
    return pl.CostEstimate(flops=flops, bytes_accessed=size, transcendentals=0)


def in_hbm(array):
    return pltpu.with_memory_space_constraint(array, pltpu.HBM)


def dot(left, right, dims=NN):
    return lax.dot_general(left, right, dims, preferred_element_type=F32)


def split(index, side, blocks):
    block = jnp.zeros_like(index)
    for edge in range(1, blocks):
        block += (index >= edge * side).astype(jnp.int32)
    return block, index - block * side


def one_hot(index, rows):
    row = lax.broadcasted_iota(jnp.int32, (rows, index.shape[1]), 0)
    return jnp.where(row == index, 1.0, 0.0).astype(BF16)


def pick(stack, blocks, index, side, group):
    rows = stack.shape[0] // blocks
    parts = []
    for start in range(0, index.shape[1], group):
        block, inner = split(index[:, start : start + group], side, blocks)
        every = dot(stack, one_hot(inner, side))
        chosen = every[:rows]
        for other in range(1, blocks):
            chosen = jnp.where(block == other, every[other * rows : (other + 1) * rows], chosen)
        parts.append(chosen.astype(BF16))
    return parts


def store_slots(buffer, parts, group):
    if len(buffer.shape) == 2:
        for place, part in enumerate(parts):
            buffer[:, place * group : (place + 1) * group] = part
        return
    slot = buffer.shape[2]
    for place, part in enumerate(parts):
        for start in range(0, group, slot):
            buffer[(place * group + start) // slot] = part[:, start : start + slot]


def send_shape(channels, peers, slot):
    if slot % 128:
        return (channels, peers * slot)
    return (peers, channels, slot)


def exchange(send, peers):
    if send.ndim == 2:
        send = send.reshape(send.shape[0], peers, -1).transpose(1, 0, 2)
    arrived = lax.all_to_all(send, "dom", 0, 0, tiled=True)
    if arrived.shape[2] % 128 == 0:
        return arrived
    return arrived.transpose(1, 0, 2).reshape(arrived.shape[1], -1)


def load_wide(ref):
    if len(ref.shape) == 2:
        return ref[...]
    return jnp.concatenate([ref[peer] for peer in range(ref.shape[0])], axis=1)


def partner(me, step, count):
    if count & (count - 1) == 0:
        return me ^ step
    return lax.rem(me + step, count)


def source(me, step, count):
    if count & (count - 1) == 0:
        return me ^ step
    return lax.rem(me + count - step, count)


def pairs(step, count):
    if count & (count - 1) == 0:
        return [(rank, rank ^ step) for rank in range(count)]
    return [(rank, (rank + step) % count) for rank in range(count)]


def sketch_kernel(count, chunks, features_in, sketch_in, index_in, *rest):
    outs, (index_out, full, features, sketch, sems) = rest[:count], rest[count:]
    channels, width = outs[0].shape
    step = width // chunks
    copies = [pltpu.make_async_copy(sketch_in, sketch, sems.at[chunks])]
    for chunk in range(chunks):
        rows = pl.ds(chunk * step, step)
        copies.append(
            pltpu.make_async_copy(features_in.at[rows, :], features.at[rows, :], sems.at[chunk])
        )
    copies.append(pltpu.make_async_copy(index_in, index_out, sems.at[chunks + 1]))
    for copy in copies:
        copy.start()
    copies[0].wait()
    for chunk in range(chunks):
        copies[chunk + 1].wait()
        rows = slice(chunk * step, (chunk + 1) * step)
        product = dot(features[rows, :], sketch[...]).T.astype(BF16)
        for part in range(count):
            full[part, :, rows] = product[part * channels : (part + 1) * channels]
    me = lax.axis_index("rep")
    for part in range(count):
        outs[part][...] = full[partner(me, part, count)]
    copies[-1].wait()


def pick_kernel(count, group, index, *rest):
    arrived, (hop, send) = rest[:count], rest[count:]
    blocks, _, side = hop.shape
    per = blocks // count
    me = lax.axis_index("rep")
    for step in range(count):
        first = source(me, step, count) * per
        for part in range(per):
            hop[first + part] = arrived[step][:, part * side : (part + 1) * side]
    stack = jnp.concatenate([hop[block] for block in range(blocks)], 0)
    store_slots(send, pick(stack, blocks, index[...], side, group), group)


def combine(dst_in, src_in, index_in, tiles_in, hop, arrived_ref, scratch, store):
    dst, src, index, tiles, columns, sums, sems = scratch
    blocks, channels, side = hop.shape
    slots = tiles.shape[0]
    fixed = columns.shape[0]
    small = [
        pltpu.make_async_copy(dst_in, dst, sems.at[0]),
        pltpu.make_async_copy(src_in, src, sems.at[1]),
        pltpu.make_async_copy(index_in, index, sems.at[2]),
    ]
    chunk = 4
    large = []
    for start in range(0, slots, chunk):
        rows = pl.ds(start, chunk)
        large.append(
            pltpu.make_async_copy(tiles_in.at[rows], tiles.at[rows], sems.at[3 + start // chunk])
        )
    for copy in large + small:
        copy.start()
    columns[:, channels:, :] = jnp.ones((fixed, EXTRA, side), BF16)
    for block in range(blocks):
        columns[block, :channels, :] = hop[block]
    arrived = load_wide(arrived_ref)
    for block in range(blocks, fixed):
        start = (block - blocks) * side
        columns[block, :channels, :] = arrived[:, start : start + side]
    for slot in range(slots):
        if slot % chunk == 0:
            large[slot // chunk].wait()
        if slot < blocks:
            sums[slot] = dot(columns[slot], tiles[slot], NT)
            continue
        if slot == blocks:
            for copy in small:
                copy.wait()
        target = dst[0, slot]
        target = jnp.where(target < 0, blocks, target)
        start = slot if slot < fixed else src[0, slot]
        sums[target] = sums[target] + dot(columns[start], tiles[slot], NT)
    results = []
    for block in range(blocks):
        total = sums[block]
        result = (total[:channels] / total[channels : channels + 1]).astype(BF16)
        store(block, result)
        results.append(result)
    return results


def combine_pick_kernel(
    group, dst_in, src_in, index_in, tiles_in, hop, arrived_ref, result, send, *scratch
):
    def store(block, value):
        result[block] = value

    results = combine(dst_in, src_in, index_in, tiles_in, hop, arrived_ref, scratch, store)
    blocks, _, side = hop.shape
    index = scratch[2]
    stack = jnp.concatenate(results, 0)
    store_slots(send, pick(stack, blocks, index[...], side, group), group)


def early_kernel(staged, index_in, tiles_in, hop, near, far, total, *rest):
    full, index, tiles, sems = rest[-4:]
    blocks, _, side = hop.shape
    copies = [
        pltpu.make_async_copy(index_in, index, sems.at[0]),
        pltpu.make_async_copy(tiles_in.at[pl.ds(0, blocks)], tiles, sems.at[1]),
    ]
    if staged:
        others = tiles_in.shape[0] - blocks
        copies.append(
            pltpu.make_async_copy(tiles_in.at[pl.ds(blocks, others)], rest[0], sems.at[2])
        )
    for copy in copies:
        copy.start()
    peers, _, slot = full.shape
    stack = jnp.concatenate([hop[block] for block in range(blocks)], 0)
    copies[0].wait()
    for peer, part in enumerate(pick(stack, blocks, index[...], side, slot)):
        full[peer] = part
    me = lax.axis_index("dom")
    half = peers // 2
    for step in range(half):
        near[step] = full[me ^ step]
        far[step] = full[me ^ half ^ step]
    ones = jnp.ones((EXTRA, side), BF16)
    copies[1].wait()
    for block in range(blocks):
        columns = jnp.concatenate([hop[block], ones], 0)
        total[block] = dot(columns, tiles[block], NT)
    if staged:
        copies[2].wait()


def finish(dst, src, tiles, total, hop, arrived, columns, sums):
    blocks, channels, side = hop.shape
    fixed = columns.shape[0]
    slots = blocks + tiles.shape[0]
    lane = lax.broadcasted_iota(jnp.int32, dst.shape, 1)
    targets, starts = {}, {slot: slot for slot in range(fixed)}
    for slot in range(blocks, slots):
        target = jnp.sum(jnp.where(lane == slot, dst[...], 0))
        targets[slot] = jnp.where(target < 0, blocks, target)
    for slot in range(fixed, slots):
        starts[slot] = jnp.sum(jnp.where(lane == slot, src[...], 0))
    columns[:, channels:, :] = jnp.ones((fixed, EXTRA, side), BF16)
    for block in range(blocks):
        columns[block, :channels, :] = hop[block]
        sums[block] = total[block]
    wide = load_wide(arrived)
    for block in range(blocks, fixed):
        start = (block - blocks) * side
        columns[block, :channels, :] = wide[:, start : start + side]
    products = [
        dot(columns[starts[slot]], tiles[slot - blocks], NT) for slot in range(blocks, fixed)
    ]
    for slot in range(blocks, slots):
        target = targets[slot]
        if slot < fixed:
            product = products[slot - blocks]
        else:
            product = dot(columns[starts[slot]], tiles[slot - blocks], NT)
        sums[target] = sums[target] + product
    results = []
    for block in range(blocks):
        whole = sums[block]
        results.append((whole[:channels] / whole[channels : channels + 1]).astype(BF16))
    return results


def finish_kernel(
    group, keep, dst, src, index, tiles, total, hop, arrived, *rest
):
    send, scratch = rest[keep], rest[keep + 1 :]
    results = finish(dst, src, tiles, total, hop, arrived, *scratch)
    blocks, _, side = hop.shape
    if keep:
        for block, result in enumerate(results):
            rest[0][block] = result
    stack = jnp.concatenate(results, 0)
    store_slots(send, pick(stack, blocks, index[...], side, group), group)


def relay_kernel(*refs):
    half = refs[0].shape[0]
    ins, outs = refs[: len(refs) - half], refs[len(refs) - half :]
    channels = ins[0].shape[1]
    for step in range(half):
        for place, blocks in enumerate(ins):
            outs[step][place * channels : (place + 1) * channels] = blocks[step]


def combine_last_kernel(
    group, dst_in, src_in, index_in, tiles_in, hop, arrived_ref, hop0, send, *scratch
):
    results = combine(
        dst_in, src_in, index_in, tiles_in, hop, arrived_ref, scratch, lambda *_: None
    )
    blocks, _, side = hop.shape
    index = scratch[2]
    stack = []
    for block in range(blocks):
        stack += [hop0[block], hop[block], results[block]]
    stack = jnp.concatenate(stack, 0)
    store_slots(send, pick(stack, blocks, index[...], side, group), group)


def place_steps_kernel(peers, side, index_ref, *rest):
    half = peers // 2
    moved, last, (out_ref, out, sems) = rest[:half], rest[half], rest[half + 1 :]
    hops, channels, nodes = out.shape
    blocks = nodes // side
    slot = nodes // peers
    me = lax.axis_index("dom")
    parts, indexes = [], []
    for step in range(peers):
        origin = me ^ step
        start = pl.multiple_of(origin * slot, slot)
        indexes.append(index_ref[:, pl.ds(start, slot)])
        first = (step // half) * channels
        from_step = moved[step % half]
        parts.append(
            jnp.concatenate(
                [
                    from_step[first + 2 * channels * hop : first + (2 * hop + 1) * channels]
                    for hop in range(hops - 1)
                ]
                + [last[origin]],
                0,
            )
        )
    block, inner = split(jnp.concatenate(indexes, 1), side, blocks)
    table = jnp.concatenate(
        [one_hot(inner[:, start : start + side], side).T for start in range(0, nodes, side)], 0
    )
    stacked = jnp.concatenate(parts, 1)
    copies = []
    for other in range(blocks):
        mask = jnp.where(block == other, 1.0, 0.0).astype(BF16)
        placed = dot(stacked * mask, table).astype(BF16)
        columns = slice(other * side, (other + 1) * side)
        for hop in range(hops):
            out[hop, :, columns] = placed[hop * channels : (hop + 1) * channels]
        columns = pl.ds(other * side, side)
        copies.append(
            pltpu.make_async_copy(
                out.at[:, :, columns], out_ref.at[:, :, columns], sems.at[other]
            )
        )
        copies[-1].start()
    for copy in copies:
        copy.wait()


def place_kernel(side, index_ref, arrived_ref, out_ref):
    hops, channels, nodes = out_ref.shape
    blocks = nodes // side
    stacked = load_wide(arrived_ref)
    block, inner = split(index_ref[...], side, blocks)
    table = one_hot(inner, side)
    for other in range(blocks):
        mask = jnp.where(block == other, 1.0, 0.0).astype(BF16)
        placed = dot(stacked * mask, table, NT).astype(BF16)
        for hop in range(hops):
            out_ref[hop, :, other * side : (other + 1) * side] = placed[
                hop * channels : (hop + 1) * channels
            ]


def on_device(
    features, sketch_matrix, tiles, tile_dst, tile_src, halo_index, send_order, arrival_place
):
    reps = lax.axis_size("rep")
    peers = lax.axis_size("dom")
    width = features.shape[0]
    nodes = width * reps
    channels = sketch_matrix.shape[1] // reps
    halo = halo_index.shape[1]
    tiles = tiles[0]
    slots, side, _ = tiles.shape
    blocks = nodes // side
    fixed = (nodes + halo) // side
    vmem, smem, dma = pltpu.VMEM, pltpu.SMEM, pltpu.SemaphoreType.DMA
    hop_shape = (blocks, channels, side)
    halo_shape = send_shape(channels, peers, halo // peers)
    last_shape = send_shape(3 * channels, peers, nodes // peers)
    group = 256
    chunks = 1

    def out(shape):
        return jax.ShapeDtypeStruct(shape, BF16)

    def early(hop, staged):
        shape = (peers // 2, channels, slot)
        others = (slots - blocks, side, side)
        near, far, total, *rest = pl.pallas_call(
            lambda *refs: early_kernel(staged, *refs),
            out_shape=(
                out(shape),
                out(shape),
                jax.ShapeDtypeStruct((blocks, channels + EXTRA, side), F32),
            )
            + (out(others),) * staged,
            in_specs=[HBM, HBM, VMEM],
            out_specs=(VMEM,) * (3 + staged),
            scratch_shapes=[
                vmem((peers, channels, slot), BF16),
                vmem(send_order.shape, jnp.int32),
                vmem((blocks, side, side), BF16),
                dma((3,)),
            ],
            compiler_params=params(),
            cost_estimate=cost(2 * channels * nodes * nodes, 8 * channels * nodes),
            name="early",
        )(in_hbm(send_order), in_hbm(tiles), hop)
        sent = lax.ppermute(far, "dom", pairs(peers // 2, peers))
        return (near, sent), total, rest

    def late(keep, index, others, total, hop, arrived):
        shape = (peers, channels, index.shape[1] // peers)
        return pl.pallas_call(
            lambda *refs: finish_kernel(group, keep, *refs),
            out_shape=(out(hop_shape),) * keep + (out(shape),),
            in_specs=[VMEM] * 7,
            out_specs=(VMEM,) * (keep + 1),
            scratch_shapes=[
                vmem((fixed, channels + EXTRA, side), BF16),
                vmem((blocks + 1, channels + EXTRA, side), F32),
            ],
            compiler_params=params(),
        )(tile_dst, tile_src, index, others, total, hop, arrived)

    *own, halo_rows = pl.pallas_call(
        lambda *refs: sketch_kernel(reps, chunks, *refs),
        out_shape=(out((channels, width)),) * reps
        + (jax.ShapeDtypeStruct(halo_index.shape, jnp.int32),),
        in_specs=[HBM] * 3,
        out_specs=(VMEM,) * (reps + 1),
        scratch_shapes=[
            vmem((reps, channels, width), BF16),
            vmem(features.shape, BF16),
            vmem(sketch_matrix.shape, BF16),
            dma((chunks + 2,)),
        ],
        compiler_params=params(),
        name="sketch",
    )(in_hbm(features), in_hbm(sketch_matrix), in_hbm(halo_index))
    arrived = [own[0]]
    for step in range(1, reps):
        arrived.append(lax.ppermute(own[step], "rep", pairs(step, reps)))
    hop0, send = pl.pallas_call(
        lambda *refs: pick_kernel(reps, group, *refs),
        out_shape=(out(hop_shape), out(halo_shape)),
        in_specs=[VMEM] * (reps + 1),
        out_specs=(VMEM, VMEM),
        compiler_params=params(),
        name="pick",
    )(halo_rows, *arrived)
    slot = nodes // peers
    whole_lanes = slot % 128 == 0 and (halo // peers) % 128 == 0
    if whole_lanes and peers > 1 and peers & (peers - 1) == 0:
        half = peers // 2
        halo0 = exchange(send, peers)
        early0, total, others = early(hop0, 1)
        others = others[0]
        hop1, send = late(1, halo_rows, others, total, hop0, halo0)
        halo1 = exchange(send, peers)
        early1, total, _ = early(hop1, 0)
        (send,) = late(0, send_order, others, total, hop1, halo1)
        last = exchange(send, peers)
        moved = pl.pallas_call(
            relay_kernel,
            out_shape=(out((4 * channels, slot)),) * half,
            in_specs=[VMEM] * 4,
            out_specs=(VMEM,) * half,
            compiler_params=params(),
            cost_estimate=cost(0, 16 * channels * nodes),
            name="relay",
        )(*early0, *early1)
        moved = [moved[0]] + [
            lax.ppermute(moved[step], "dom", pairs(step, peers)) for step in range(1, half)
        ]
        return pl.pallas_call(
            lambda *refs: place_steps_kernel(peers, side, *refs),
            out_shape=out((3, channels, nodes)),
            in_specs=[VMEM] * (half + 2),
            out_specs=HBM,
            scratch_shapes=[vmem((3, channels, nodes), BF16), dma((blocks,))],
            compiler_params=params(),
            name="place",
        )(arrival_place, *moved, last)
    halo0 = exchange(send, peers)

    def work(index):
        return [
            smem(tile_dst.shape, jnp.int32),
            smem(tile_src.shape, jnp.int32),
            vmem(index.shape, jnp.int32),
            vmem(tiles.shape, BF16),
            vmem((fixed, channels + EXTRA, side), BF16),
            vmem((blocks + 1, channels + EXTRA, side), F32),
            dma((3 + slots // 4,)),
        ]

    hop1, send = pl.pallas_call(
        lambda *refs: combine_pick_kernel(group, *refs),
        out_shape=(out(hop_shape), out(halo_shape)),
        in_specs=[HBM] * 4 + [VMEM] * 2,
        out_specs=(VMEM, VMEM),
        scratch_shapes=work(halo_index),
        compiler_params=params(),
        name="combine_pick",
    )(in_hbm(tile_dst), in_hbm(tile_src), in_hbm(halo_index), in_hbm(tiles), hop0, halo0)
    halo1 = exchange(send, peers)
    send = pl.pallas_call(
        lambda *refs: combine_last_kernel(group, *refs),
        out_shape=out(last_shape),
        in_specs=[HBM] * 4 + [VMEM] * 3,
        out_specs=VMEM,
        scratch_shapes=work(send_order),
        compiler_params=params(),
        name="combine_last",
    )(in_hbm(tile_dst), in_hbm(tile_src), in_hbm(send_order), in_hbm(tiles), hop1, halo1, hop0)
    last = exchange(send, peers)
    return pl.pallas_call(
        lambda *refs: place_kernel(side, *refs),
        out_shape=out((3, channels, nodes)),
        in_specs=[VMEM, VMEM],
        out_specs=VMEM,
        compiler_params=params(),
        name="place",
    )(arrival_place, last)


def solution(mesh):
    in_specs = (
        P(("dom", "rep"), None),
        P(),
        P("dom", None, None, None),
        P("dom", None),
        P("dom", None),
        P("dom", None),
        P("dom", None),
        P("dom", None),
    )
    out_specs = P(None, "rep", "dom")

    return jax.shard_map(
        on_device, mesh=mesh, in_specs=in_specs, out_specs=out_specs, check_vma=False
    )
```

```python
import jax
import jax.numpy as jnp
from jax import lax
from jax.experimental import pallas as pl
from jax.experimental.pallas import tpu as pltpu
from jax.sharding import PartitionSpec as P


BF16 = jnp.bfloat16
F32 = jnp.float32
EXTRA = 16
NN = (((1,), (0,)), ((), ()))
NT = (((1,), (1,)), ((), ()))
VMEM = pl.BlockSpec(memory_space=pltpu.VMEM)
HBM = pl.BlockSpec(memory_space=pltpu.HBM)


def params():
    return pltpu.CompilerParams(vmem_limit_bytes=40 * 1024 * 1024)


def cost(flops, size):
    return pl.CostEstimate(flops=flops, bytes_accessed=size, transcendentals=0)


def in_hbm(array):
    return pltpu.with_memory_space_constraint(array, pltpu.HBM)


def dot(left, right, dims=NN):
    return lax.dot_general(left, right, dims, preferred_element_type=F32)


def split(index, side, blocks):
    block = jnp.zeros_like(index)
    for edge in range(1, blocks):
        block += (index >= edge * side).astype(jnp.int32)
    return block, index - block * side


def one_hot(index, rows):
    row = lax.broadcasted_iota(jnp.int32, (rows, index.shape[1]), 0)
    return jnp.where(row == index, 1.0, 0.0).astype(BF16)


def pick(stack, blocks, index, side, group):
    rows = stack.shape[0] // blocks
    parts = []
    for start in range(0, index.shape[1], group):
        block, inner = split(index[:, start : start + group], side, blocks)
        every = dot(stack, one_hot(inner, side))
        chosen = every[:rows]
        for other in range(1, blocks):
            chosen = jnp.where(block == other, every[other * rows : (other + 1) * rows], chosen)
        parts.append(chosen.astype(BF16))
    return parts


def store_slots(buffer, parts, group):
    if len(buffer.shape) == 2:
        for place, part in enumerate(parts):
            buffer[:, place * group : (place + 1) * group] = part
        return
    slot = buffer.shape[2]
    for place, part in enumerate(parts):
        for start in range(0, group, slot):
            buffer[(place * group + start) // slot] = part[:, start : start + slot]


def send_shape(channels, peers, slot):
    if slot % 128:
        return (channels, peers * slot)
    return (peers, channels, slot)


def exchange(send, peers):
    if send.ndim == 2:
        send = send.reshape(send.shape[0], peers, -1).transpose(1, 0, 2)
    arrived = lax.all_to_all(send, "dom", 0, 0, tiled=True)
    if arrived.shape[2] % 128 == 0:
        return arrived
    return arrived.transpose(1, 0, 2).reshape(arrived.shape[1], -1)


def load_wide(ref):
    if len(ref.shape) == 2:
        return ref[...]
    return jnp.concatenate([ref[peer] for peer in range(ref.shape[0])], axis=1)


def partner(me, step, count):
    if count & (count - 1) == 0:
        return me ^ step
    return lax.rem(me + step, count)


def source(me, step, count):
    if count & (count - 1) == 0:
        return me ^ step
    return lax.rem(me + count - step, count)


def pairs(step, count):
    if count & (count - 1) == 0:
        return [(rank, rank ^ step) for rank in range(count)]
    return [(rank, (rank + step) % count) for rank in range(count)]


def sketch_kernel(count, chunks, features_in, sketch_in, index_in, *rest):
    outs, (index_out, full, features, sketch, sems) = rest[:count], rest[count:]
    channels, width = outs[0].shape
    step = width // chunks
    copies = [pltpu.make_async_copy(sketch_in, sketch, sems.at[chunks])]
    for chunk in range(chunks):
        rows = pl.ds(chunk * step, step)
        copies.append(
            pltpu.make_async_copy(features_in.at[rows, :], features.at[rows, :], sems.at[chunk])
        )
    copies.append(pltpu.make_async_copy(index_in, index_out, sems.at[chunks + 1]))
    for copy in copies:
        copy.start()
    copies[0].wait()
    for chunk in range(chunks):
        copies[chunk + 1].wait()
        rows = slice(chunk * step, (chunk + 1) * step)
        product = dot(features[rows, :], sketch[...]).T.astype(BF16)
        for part in range(count):
            full[part, :, rows] = product[part * channels : (part + 1) * channels]
    me = lax.axis_index("rep")
    for part in range(count):
        outs[part][...] = full[partner(me, part, count)]
    copies[-1].wait()


def pick_kernel(count, group, index, *rest):
    arrived, (hop, send) = rest[:count], rest[count:]
    blocks, _, side = hop.shape
    per = blocks // count
    me = lax.axis_index("rep")
    for step in range(count):
        first = source(me, step, count) * per
        for part in range(per):
            hop[first + part] = arrived[step][:, part * side : (part + 1) * side]
    stack = jnp.concatenate([hop[block] for block in range(blocks)], 0)
    store_slots(send, pick(stack, blocks, index[...], side, group), group)


def combine(dst_in, src_in, index_in, tiles_in, hop, arrived_ref, scratch, store):
    dst, src, index, tiles, columns, sums, sems = scratch
    blocks, channels, side = hop.shape
    slots = tiles.shape[0]
    fixed = columns.shape[0]
    small = [
        pltpu.make_async_copy(dst_in, dst, sems.at[0]),
        pltpu.make_async_copy(src_in, src, sems.at[1]),
        pltpu.make_async_copy(index_in, index, sems.at[2]),
    ]
    chunk = 4
    large = []
    for start in range(0, slots, chunk):
        rows = pl.ds(start, chunk)
        large.append(
            pltpu.make_async_copy(tiles_in.at[rows], tiles.at[rows], sems.at[3 + start // chunk])
        )
    for copy in large + small:
        copy.start()
    columns[:, channels:, :] = jnp.ones((fixed, EXTRA, side), BF16)
    for block in range(blocks):
        columns[block, :channels, :] = hop[block]
    arrived = load_wide(arrived_ref)
    for block in range(blocks, fixed):
        start = (block - blocks) * side
        columns[block, :channels, :] = arrived[:, start : start + side]
    for slot in range(slots):
        if slot % chunk == 0:
            large[slot // chunk].wait()
        if slot < blocks:
            sums[slot] = dot(columns[slot], tiles[slot], NT)
            continue
        if slot == blocks:
            for copy in small:
                copy.wait()
        target = dst[0, slot]
        target = jnp.where(target < 0, blocks, target)
        start = slot if slot < fixed else src[0, slot]
        sums[target] = sums[target] + dot(columns[start], tiles[slot], NT)
    results = []
    for block in range(blocks):
        total = sums[block]
        result = (total[:channels] / total[channels : channels + 1]).astype(BF16)
        store(block, result)
        results.append(result)
    return results


def combine_pick_kernel(
    group, dst_in, src_in, index_in, tiles_in, hop, arrived_ref, result, send, *scratch
):
    def store(block, value):
        result[block] = value

    results = combine(dst_in, src_in, index_in, tiles_in, hop, arrived_ref, scratch, store)
    blocks, _, side = hop.shape
    index = scratch[2]
    stack = jnp.concatenate(results, 0)
    store_slots(send, pick(stack, blocks, index[...], side, group), group)


def early_kernel(staged, index_in, tiles_in, hop, near, far, total, *rest):
    full, index, tiles, sems = rest[-4:]
    blocks, _, side = hop.shape
    copies = [
        pltpu.make_async_copy(index_in, index, sems.at[0]),
        pltpu.make_async_copy(tiles_in.at[pl.ds(0, blocks)], tiles, sems.at[1]),
    ]
    if staged:
        others = tiles_in.shape[0] - blocks
        copies.append(
            pltpu.make_async_copy(tiles_in.at[pl.ds(blocks, others)], rest[0], sems.at[2])
        )
    for copy in copies:
        copy.start()
    peers, _, slot = full.shape
    stack = jnp.concatenate([hop[block] for block in range(blocks)], 0)
    copies[0].wait()
    for peer, part in enumerate(pick(stack, blocks, index[...], side, slot)):
        full[peer] = part
    me = lax.axis_index("dom")
    half = peers // 2
    for step in range(half):
        near[step] = full[me ^ step]
        far[step] = full[me ^ half ^ step]
    ones = jnp.ones((EXTRA, side), BF16)
    copies[1].wait()
    for block in range(blocks):
        columns = jnp.concatenate([hop[block], ones], 0)
        total[block] = dot(columns, tiles[block], NT)
    if staged:
        copies[2].wait()


def finish(dst, src, tiles, total, hop, arrived, columns, sums):
    blocks, channels, side = hop.shape
    fixed = columns.shape[0]
    slots = blocks + tiles.shape[0]
    lane = lax.broadcasted_iota(jnp.int32, dst.shape, 1)
    targets, starts = {}, {slot: slot for slot in range(fixed)}
    for slot in range(blocks, slots):
        target = jnp.sum(jnp.where(lane == slot, dst[...], 0))
        targets[slot] = jnp.where(target < 0, blocks, target)
    for slot in range(fixed, slots):
        starts[slot] = jnp.sum(jnp.where(lane == slot, src[...], 0))
    columns[:, channels:, :] = jnp.ones((fixed, EXTRA, side), BF16)
    for block in range(blocks):
        columns[block, :channels, :] = hop[block]
        sums[block] = total[block]
    wide = load_wide(arrived)
    for block in range(blocks, fixed):
        start = (block - blocks) * side
        columns[block, :channels, :] = wide[:, start : start + side]
    products = [
        dot(columns[starts[slot]], tiles[slot - blocks], NT) for slot in range(blocks, fixed)
    ]
    for slot in range(blocks, slots):
        target = targets[slot]
        if slot < fixed:
            product = products[slot - blocks]
        else:
            product = dot(columns[starts[slot]], tiles[slot - blocks], NT)
        sums[target] = sums[target] + product
    results = []
    for block in range(blocks):
        whole = sums[block]
        results.append((whole[:channels] / whole[channels : channels + 1]).astype(BF16))
    return results


def finish_kernel(
    group, keep, dst, src, index, tiles, total, hop, arrived, *rest
):
    send, scratch = rest[keep], rest[keep + 1 :]
    results = finish(dst, src, tiles, total, hop, arrived, *scratch)
    blocks, _, side = hop.shape
    if keep:
        for block, result in enumerate(results):
            rest[0][block] = result
    stack = jnp.concatenate(results, 0)
    store_slots(send, pick(stack, blocks, index[...], side, group), group)


def relay_kernel(near, sent, *outs):
    channels = near.shape[1]
    for step, out in enumerate(outs):
        out[:channels] = near[step]
        out[channels:] = sent[step]


def combine_last_kernel(
    group, dst_in, src_in, index_in, tiles_in, hop, arrived_ref, hop0, send, *scratch
):
    results = combine(
        dst_in, src_in, index_in, tiles_in, hop, arrived_ref, scratch, lambda *_: None
    )
    blocks, _, side = hop.shape
    index = scratch[2]
    stack = []
    for block in range(blocks):
        stack += [hop0[block], hop[block], results[block]]
    stack = jnp.concatenate(stack, 0)
    store_slots(send, pick(stack, blocks, index[...], side, group), group)


def place_steps_kernel(peers, side, index_ref, *rest):
    half = peers // 2
    moved, last, (out_ref, out, sems) = rest[:-4], rest[-4], rest[-3:]
    hops, channels, nodes = out.shape
    blocks = nodes // side
    slot = nodes // peers
    me = lax.axis_index("dom")
    parts, indexes = [], []
    for step in range(peers):
        origin = me ^ step
        start = pl.multiple_of(origin * slot, slot)
        indexes.append(index_ref[:, pl.ds(start, slot)])
        first = (step // half) * channels
        arrived = [
            moved[hop * half + step % half][first : first + channels] for hop in range(hops - 1)
        ]
        parts.append(jnp.concatenate(arrived + [last[origin]], 0))
    block, inner = split(jnp.concatenate(indexes, 1), side, blocks)
    table = jnp.concatenate(
        [one_hot(inner[:, start : start + side], side).T for start in range(0, nodes, side)], 0
    )
    stacked = jnp.concatenate(parts, 1)
    copies = []
    for other in range(blocks):
        mask = jnp.where(block == other, 1.0, 0.0).astype(BF16)
        placed = dot(stacked * mask, table).astype(BF16)
        columns = slice(other * side, (other + 1) * side)
        for hop in range(hops):
            out[hop, :, columns] = placed[hop * channels : (hop + 1) * channels]
        columns = pl.ds(other * side, side)
        copies.append(
            pltpu.make_async_copy(
                out.at[:, :, columns], out_ref.at[:, :, columns], sems.at[other]
            )
        )
        copies[-1].start()
    for copy in copies:
        copy.wait()


def place_kernel(side, index_ref, arrived_ref, out_ref):
    hops, channels, nodes = out_ref.shape
    blocks = nodes // side
    stacked = load_wide(arrived_ref)
    block, inner = split(index_ref[...], side, blocks)
    table = one_hot(inner, side)
    for other in range(blocks):
        mask = jnp.where(block == other, 1.0, 0.0).astype(BF16)
        placed = dot(stacked * mask, table, NT).astype(BF16)
        for hop in range(hops):
            out_ref[hop, :, other * side : (other + 1) * side] = placed[
                hop * channels : (hop + 1) * channels
            ]


def on_device(
    features, sketch_matrix, tiles, tile_dst, tile_src, halo_index, send_order, arrival_place
):
    reps = lax.axis_size("rep")
    peers = lax.axis_size("dom")
    width = features.shape[0]
    nodes = width * reps
    channels = sketch_matrix.shape[1] // reps
    halo = halo_index.shape[1]
    tiles = tiles[0]
    slots, side, _ = tiles.shape
    blocks = nodes // side
    fixed = (nodes + halo) // side
    vmem, smem, dma = pltpu.VMEM, pltpu.SMEM, pltpu.SemaphoreType.DMA
    hop_shape = (blocks, channels, side)
    halo_shape = send_shape(channels, peers, halo // peers)
    last_shape = send_shape(3 * channels, peers, nodes // peers)
    group = 256
    chunks = 1

    def out(shape):
        return jax.ShapeDtypeStruct(shape, BF16)

    def early(hop, staged):
        shape = (peers // 2, channels, slot)
        others = (slots - blocks, side, side)
        near, far, total, *rest = pl.pallas_call(
            lambda *refs: early_kernel(staged, *refs),
            out_shape=(
                out(shape),
                out(shape),
                jax.ShapeDtypeStruct((blocks, channels + EXTRA, side), F32),
            )
            + (out(others),) * staged,
            in_specs=[HBM, HBM, VMEM],
            out_specs=(VMEM,) * (3 + staged),
            scratch_shapes=[
                vmem((peers, channels, slot), BF16),
                vmem(send_order.shape, jnp.int32),
                vmem((blocks, side, side), BF16),
                dma((3,)),
            ],
            compiler_params=params(),
            cost_estimate=cost(2 * channels * nodes * nodes, 8 * channels * nodes),
            name="early",
        )(in_hbm(send_order), in_hbm(tiles), hop)
        sent = lax.ppermute(far, "dom", pairs(peers // 2, peers))
        return (near, sent), total, rest

    def relay(blocks_of):
        steps = peers // 2
        moved = pl.pallas_call(
            relay_kernel,
            out_shape=(out((2 * channels, slot)),) * steps,
            in_specs=[VMEM] * 2,
            out_specs=(VMEM,) * steps,
            compiler_params=params(),
            cost_estimate=cost(0, 8 * channels * nodes),
            name="relay",
        )(*blocks_of)
        return [moved[0]] + [
            lax.ppermute(moved[step], "dom", pairs(step, peers)) for step in range(1, steps)
        ]

    def late(keep, index, others, total, hop, arrived):
        shape = (peers, channels, index.shape[1] // peers)
        return pl.pallas_call(
            lambda *refs: finish_kernel(group, keep, *refs),
            out_shape=(out(hop_shape),) * keep + (out(shape),),
            in_specs=[VMEM] * 7,
            out_specs=(VMEM,) * (keep + 1),
            scratch_shapes=[
                vmem((fixed, channels + EXTRA, side), BF16),
                vmem((blocks + 1, channels + EXTRA, side), F32),
            ],
            compiler_params=params(),
        )(tile_dst, tile_src, index, others, total, hop, arrived)

    *own, halo_rows = pl.pallas_call(
        lambda *refs: sketch_kernel(reps, chunks, *refs),
        out_shape=(out((channels, width)),) * reps
        + (jax.ShapeDtypeStruct(halo_index.shape, jnp.int32),),
        in_specs=[HBM] * 3,
        out_specs=(VMEM,) * (reps + 1),
        scratch_shapes=[
            vmem((reps, channels, width), BF16),
            vmem(features.shape, BF16),
            vmem(sketch_matrix.shape, BF16),
            dma((chunks + 2,)),
        ],
        compiler_params=params(),
        name="sketch",
    )(in_hbm(features), in_hbm(sketch_matrix), in_hbm(halo_index))
    arrived = [own[0]]
    for step in range(1, reps):
        arrived.append(lax.ppermute(own[step], "rep", pairs(step, reps)))
    hop0, send = pl.pallas_call(
        lambda *refs: pick_kernel(reps, group, *refs),
        out_shape=(out(hop_shape), out(halo_shape)),
        in_specs=[VMEM] * (reps + 1),
        out_specs=(VMEM, VMEM),
        compiler_params=params(),
        name="pick",
    )(halo_rows, *arrived)
    slot = nodes // peers
    whole_lanes = slot % 128 == 0 and (halo // peers) % 128 == 0
    if whole_lanes and peers > 1 and peers & (peers - 1) == 0:
        half = peers // 2
        halo0 = exchange(send, peers)
        early0, total, others = early(hop0, 1)
        others = others[0]
        hop1, send = late(1, halo_rows, others, total, hop0, halo0)
        halo1 = exchange(send, peers)
        early1, total, _ = early(hop1, 0)
        (send,) = late(0, send_order, others, total, hop1, halo1)
        last = exchange(send, peers)
        return pl.pallas_call(
            lambda *refs: place_steps_kernel(peers, side, *refs),
            out_shape=out((3, channels, nodes)),
            in_specs=[VMEM] * (2 * half + 2),
            out_specs=HBM,
            scratch_shapes=[vmem((3, channels, nodes), BF16), dma((blocks,))],
            compiler_params=params(),
            name="place",
        )(arrival_place, *relay(early0), *relay(early1), last)
    halo0 = exchange(send, peers)

    def work(index):
        return [
            smem(tile_dst.shape, jnp.int32),
            smem(tile_src.shape, jnp.int32),
            vmem(index.shape, jnp.int32),
            vmem(tiles.shape, BF16),
            vmem((fixed, channels + EXTRA, side), BF16),
            vmem((blocks + 1, channels + EXTRA, side), F32),
            dma((3 + slots // 4,)),
        ]

    hop1, send = pl.pallas_call(
        lambda *refs: combine_pick_kernel(group, *refs),
        out_shape=(out(hop_shape), out(halo_shape)),
        in_specs=[HBM] * 4 + [VMEM] * 2,
        out_specs=(VMEM, VMEM),
        scratch_shapes=work(halo_index),
        compiler_params=params(),
        name="combine_pick",
    )(in_hbm(tile_dst), in_hbm(tile_src), in_hbm(halo_index), in_hbm(tiles), hop0, halo0)
    halo1 = exchange(send, peers)
    send = pl.pallas_call(
        lambda *refs: combine_last_kernel(group, *refs),
        out_shape=out(last_shape),
        in_specs=[HBM] * 4 + [VMEM] * 3,
        out_specs=VMEM,
        scratch_shapes=work(send_order),
        compiler_params=params(),
        name="combine_last",
    )(in_hbm(tile_dst), in_hbm(tile_src), in_hbm(send_order), in_hbm(tiles), hop1, halo1, hop0)
    last = exchange(send, peers)
    return pl.pallas_call(
        lambda *refs: place_kernel(side, *refs),
        out_shape=out((3, channels, nodes)),
        in_specs=[VMEM, VMEM],
        out_specs=VMEM,
        compiler_params=params(),
        name="place",
    )(arrival_place, last)


def solution(mesh):
    in_specs = (
        P(("dom", "rep"), None),
        P(),
        P("dom", None, None, None),
        P("dom", None),
        P("dom", None),
        P("dom", None),
        P("dom", None),
        P("dom", None),
    )
    out_specs = P(None, "rep", "dom")

    return jax.shard_map(
        on_device, mesh=mesh, in_specs=in_specs, out_specs=out_specs, check_vma=False
    )
```

```python
import jax
import jax.numpy as jnp
from jax import lax
from jax.experimental import pallas as pl
from jax.experimental.pallas import tpu as pltpu
from jax.sharding import PartitionSpec as P


BF16 = jnp.bfloat16
F32 = jnp.float32
EXTRA = 16
NN = (((1,), (0,)), ((), ()))
NT = (((1,), (1,)), ((), ()))
VMEM = pl.BlockSpec(memory_space=pltpu.VMEM)
HBM = pl.BlockSpec(memory_space=pltpu.HBM)


def params():
    return pltpu.CompilerParams(vmem_limit_bytes=40 * 1024 * 1024)


def cost(flops, size):
    return pl.CostEstimate(flops=flops, bytes_accessed=size, transcendentals=0)


def in_hbm(array):
    return pltpu.with_memory_space_constraint(array, pltpu.HBM)


def dot(left, right, dims=NN):
    return lax.dot_general(left, right, dims, preferred_element_type=F32)


def split(index, side, blocks):
    block = jnp.zeros_like(index)
    for edge in range(1, blocks):
        block += (index >= edge * side).astype(jnp.int32)
    return block, index - block * side


def one_hot(index, rows):
    row = lax.broadcasted_iota(jnp.int32, (rows, index.shape[1]), 0)
    return jnp.where(row == index, 1.0, 0.0).astype(BF16)


def pick(stack, blocks, index, side, group):
    rows = stack.shape[0] // blocks
    parts = []
    for start in range(0, index.shape[1], group):
        block, inner = split(index[:, start : start + group], side, blocks)
        every = dot(stack, one_hot(inner, side))
        chosen = every[:rows]
        for other in range(1, blocks):
            chosen = jnp.where(block == other, every[other * rows : (other + 1) * rows], chosen)
        parts.append(chosen.astype(BF16))
    return parts


def store_slots(buffer, parts, group):
    if len(buffer.shape) == 2:
        for place, part in enumerate(parts):
            buffer[:, place * group : (place + 1) * group] = part
        return
    slot = buffer.shape[2]
    for place, part in enumerate(parts):
        for start in range(0, group, slot):
            buffer[(place * group + start) // slot] = part[:, start : start + slot]


def send_shape(channels, peers, slot):
    if slot % 128:
        return (channels, peers * slot)
    return (peers, channels, slot)


def exchange(send, peers):
    if send.ndim == 2:
        send = send.reshape(send.shape[0], peers, -1).transpose(1, 0, 2)
    arrived = lax.all_to_all(send, "dom", 0, 0, tiled=True)
    if arrived.shape[2] % 128 == 0:
        return arrived
    return arrived.transpose(1, 0, 2).reshape(arrived.shape[1], -1)


def load_wide(ref):
    if len(ref.shape) == 2:
        return ref[...]
    return jnp.concatenate([ref[peer] for peer in range(ref.shape[0])], axis=1)


def partner(me, step, count):
    if count & (count - 1) == 0:
        return me ^ step
    return lax.rem(me + step, count)


def source(me, step, count):
    if count & (count - 1) == 0:
        return me ^ step
    return lax.rem(me + count - step, count)


def pairs(step, count):
    if count & (count - 1) == 0:
        return [(rank, rank ^ step) for rank in range(count)]
    return [(rank, (rank + step) % count) for rank in range(count)]


def sketch_kernel(count, chunks, features_in, sketch_in, index_in, *rest):
    outs, (index_out, full, features, sketch, sems) = rest[:count], rest[count:]
    channels, width = outs[0].shape
    step = width // chunks
    copies = [pltpu.make_async_copy(sketch_in, sketch, sems.at[chunks])]
    for chunk in range(chunks):
        rows = pl.ds(chunk * step, step)
        copies.append(
            pltpu.make_async_copy(features_in.at[rows, :], features.at[rows, :], sems.at[chunk])
        )
    copies.append(pltpu.make_async_copy(index_in, index_out, sems.at[chunks + 1]))
    for copy in copies:
        copy.start()
    copies[0].wait()
    for chunk in range(chunks):
        copies[chunk + 1].wait()
        rows = slice(chunk * step, (chunk + 1) * step)
        product = dot(features[rows, :], sketch[...]).T.astype(BF16)
        for part in range(count):
            full[part, :, rows] = product[part * channels : (part + 1) * channels]
    me = lax.axis_index("rep")
    for part in range(count):
        outs[part][...] = full[partner(me, part, count)]
    copies[-1].wait()


def pick_kernel(count, group, index, *rest):
    arrived, (hop, send) = rest[:count], rest[count:]
    blocks, _, side = hop.shape
    per = blocks // count
    me = lax.axis_index("rep")
    for step in range(count):
        first = source(me, step, count) * per
        for part in range(per):
            hop[first + part] = arrived[step][:, part * side : (part + 1) * side]
    stack = jnp.concatenate([hop[block] for block in range(blocks)], 0)
    store_slots(send, pick(stack, blocks, index[...], side, group), group)


def combine(dst_in, src_in, index_in, tiles_in, hop, arrived_ref, scratch, store):
    dst, src, index, tiles, columns, sums, sems = scratch
    blocks, channels, side = hop.shape
    slots = tiles.shape[0]
    fixed = columns.shape[0]
    small = [
        pltpu.make_async_copy(dst_in, dst, sems.at[0]),
        pltpu.make_async_copy(src_in, src, sems.at[1]),
        pltpu.make_async_copy(index_in, index, sems.at[2]),
    ]
    chunk = 4
    large = []
    for start in range(0, slots, chunk):
        rows = pl.ds(start, chunk)
        large.append(
            pltpu.make_async_copy(tiles_in.at[rows], tiles.at[rows], sems.at[3 + start // chunk])
        )
    for copy in large + small:
        copy.start()
    columns[:, channels:, :] = jnp.ones((fixed, EXTRA, side), BF16)
    for block in range(blocks):
        columns[block, :channels, :] = hop[block]
    arrived = load_wide(arrived_ref)
    for block in range(blocks, fixed):
        start = (block - blocks) * side
        columns[block, :channels, :] = arrived[:, start : start + side]
    for slot in range(slots):
        if slot % chunk == 0:
            large[slot // chunk].wait()
        if slot < blocks:
            sums[slot] = dot(columns[slot], tiles[slot], NT)
            continue
        if slot == blocks:
            for copy in small:
                copy.wait()
        target = dst[0, slot]
        target = jnp.where(target < 0, blocks, target)
        start = slot if slot < fixed else src[0, slot]
        sums[target] = sums[target] + dot(columns[start], tiles[slot], NT)
    results = []
    for block in range(blocks):
        total = sums[block]
        result = (total[:channels] / total[channels : channels + 1]).astype(BF16)
        store(block, result)
        results.append(result)
    return results


def combine_pick_kernel(
    group, dst_in, src_in, index_in, tiles_in, hop, arrived_ref, result, send, *scratch
):
    def store(block, value):
        result[block] = value

    results = combine(dst_in, src_in, index_in, tiles_in, hop, arrived_ref, scratch, store)
    blocks, _, side = hop.shape
    index = scratch[2]
    stack = jnp.concatenate(results, 0)
    store_slots(send, pick(stack, blocks, index[...], side, group), group)


def early_kernel(staged, index_in, tiles_in, hop, near, far, total, *rest):
    full, index, tiles, sems = rest[-4:]
    blocks, _, side = hop.shape
    copies = [
        pltpu.make_async_copy(index_in, index, sems.at[0]),
        pltpu.make_async_copy(tiles_in.at[pl.ds(0, blocks)], tiles, sems.at[1]),
    ]
    if staged:
        others = tiles_in.shape[0] - blocks
        copies.append(
            pltpu.make_async_copy(tiles_in.at[pl.ds(blocks, others)], rest[0], sems.at[2])
        )
    for copy in copies:
        copy.start()
    peers, _, slot = full.shape
    stack = jnp.concatenate([hop[block] for block in range(blocks)], 0)
    copies[0].wait()
    for peer, part in enumerate(pick(stack, blocks, index[...], side, slot)):
        full[peer] = part
    me = lax.axis_index("dom")
    half = peers // 2
    for step in range(half):
        near[step] = full[me ^ step]
        far[step] = full[me ^ half ^ step]
    ones = jnp.ones((EXTRA, side), BF16)
    copies[1].wait()
    for block in range(blocks):
        columns = jnp.concatenate([hop[block], ones], 0)
        total[block] = dot(columns, tiles[block], NT)
    if staged:
        copies[2].wait()


def finish(dst, src, tiles, total, hop, arrived, columns, sums):
    blocks, channels, side = hop.shape
    fixed = columns.shape[0]
    slots = blocks + tiles.shape[0]
    lane = lax.broadcasted_iota(jnp.int32, dst.shape, 1)
    targets, starts = {}, {slot: slot for slot in range(fixed)}
    for slot in range(blocks, slots):
        target = jnp.sum(jnp.where(lane == slot, dst[...], 0))
        targets[slot] = jnp.where(target < 0, blocks, target)
    for slot in range(fixed, slots):
        starts[slot] = jnp.sum(jnp.where(lane == slot, src[...], 0))
    columns[:, channels:, :] = jnp.ones((fixed, EXTRA, side), BF16)
    for block in range(blocks):
        columns[block, :channels, :] = hop[block]
        sums[block] = total[block]
    wide = load_wide(arrived)
    for block in range(blocks, fixed):
        start = (block - blocks) * side
        columns[block, :channels, :] = wide[:, start : start + side]
    products = [
        dot(columns[starts[slot]], tiles[slot - blocks], NT) for slot in range(blocks, fixed)
    ]
    for slot in range(blocks, slots):
        target = targets[slot]
        if slot < fixed:
            product = products[slot - blocks]
        else:
            product = dot(columns[starts[slot]], tiles[slot - blocks], NT)
        sums[target] = sums[target] + product
    results = []
    for block in range(blocks):
        whole = sums[block]
        results.append((whole[:channels] / whole[channels : channels + 1]).astype(BF16))
    return results


def finish_kernel(
    group, keep, dst, src, index, tiles, total, hop, arrived, *rest
):
    send, scratch = rest[keep], rest[keep + 1 :]
    results = finish(dst, src, tiles, total, hop, arrived, *scratch)
    blocks, _, side = hop.shape
    if keep:
        for block, result in enumerate(results):
            rest[0][block] = result
    stack = jnp.concatenate(results, 0)
    store_slots(send, pick(stack, blocks, index[...], side, group), group)


def relay_kernel(near, sent, *outs):
    channels = near.shape[1]
    for step, out in enumerate(outs):
        out[:channels] = near[step]
        out[channels:] = sent[step]


def combine_last_kernel(
    group, dst_in, src_in, index_in, tiles_in, hop, arrived_ref, hop0, send, *scratch
):
    results = combine(
        dst_in, src_in, index_in, tiles_in, hop, arrived_ref, scratch, lambda *_: None
    )
    blocks, _, side = hop.shape
    index = scratch[2]
    stack = []
    for block in range(blocks):
        stack += [hop0[block], hop[block], results[block]]
    stack = jnp.concatenate(stack, 0)
    store_slots(send, pick(stack, blocks, index[...], side, group), group)


def scatter(parts, table, block, out, out_ref, first, sems):
    hops, channels, nodes = out.shape
    side = table.shape[1]
    stacked = jnp.concatenate(parts, 1)
    rows = stacked.shape[0]
    group = max(128 // rows, 1)
    copies = []
    for start in range(0, nodes // side, group):
        masks = [
            jnp.where(block == other, 1.0, 0.0).astype(BF16)
            for other in range(start, start + group)
        ]
        placed = dot(jnp.concatenate([stacked * mask for mask in masks], 0), table).astype(BF16)
        for other in range(group):
            columns = slice((start + other) * side, (start + other + 1) * side)
            for hop in range(hops):
                row = other * rows + hop * channels
                out[hop, :, columns] = placed[row : row + channels]
        columns = pl.ds(start * side, group * side)
        copies.append(
            pltpu.make_async_copy(
                out.at[:, :, columns],
                out_ref.at[pl.ds(first, hops), :, columns],
                sems.at[start],
            )
        )
        copies[-1].start()
    for copy in copies:
        copy.wait()


def place_first_kernel(peers, index_ref, *rest):
    moved, (out_ref, table_ref, block_ref, out, sems) = rest[:-5], rest[-5:]
    _, channels, nodes = out.shape
    side = table_ref.shape[1]
    blocks = nodes // side
    half = peers // 2
    slot = nodes // peers
    me = lax.axis_index("dom")
    parts, indexes = [], []
    for step in range(peers):
        start = pl.multiple_of((me ^ step) * slot, slot)
        indexes.append(index_ref[:, pl.ds(start, slot)])
        first = (step // half) * channels
        parts.append(moved[step % half][first : first + channels])
    block, inner = split(jnp.concatenate(indexes, 1), side, blocks)
    block_ref[...] = block
    table = jnp.concatenate(
        [one_hot(inner[:, start : start + side], side).T for start in range(0, nodes, side)], 0
    )
    table_ref[...] = table
    scatter(parts, table, block, out, out_ref, 0, sems)


def place_rest_kernel(peers, _, table_ref, block_ref, *rest):
    moved, last, (out_ref, out, sems) = rest[:-4], rest[-4], rest[-3:]
    channels = out.shape[1]
    half = peers // 2
    me = lax.axis_index("dom")
    parts = []
    for step in range(peers):
        first = (step // half) * channels
        arrived = moved[step % half][first : first + channels]
        parts.append(jnp.concatenate([arrived, last[me ^ step]], 0))
    scatter(parts, table_ref[...], block_ref[...], out, out_ref, 1, sems)


def place_kernel(side, index_ref, arrived_ref, out_ref):
    hops, channels, nodes = out_ref.shape
    blocks = nodes // side
    stacked = load_wide(arrived_ref)
    block, inner = split(index_ref[...], side, blocks)
    table = one_hot(inner, side)
    for other in range(blocks):
        mask = jnp.where(block == other, 1.0, 0.0).astype(BF16)
        placed = dot(stacked * mask, table, NT).astype(BF16)
        for hop in range(hops):
            out_ref[hop, :, other * side : (other + 1) * side] = placed[
                hop * channels : (hop + 1) * channels
            ]


def on_device(
    features, sketch_matrix, tiles, tile_dst, tile_src, halo_index, send_order, arrival_place
):
    reps = lax.axis_size("rep")
    peers = lax.axis_size("dom")
    width = features.shape[0]
    nodes = width * reps
    channels = sketch_matrix.shape[1] // reps
    halo = halo_index.shape[1]
    tiles = tiles[0]
    slots, side, _ = tiles.shape
    blocks = nodes // side
    fixed = (nodes + halo) // side
    vmem, smem, dma = pltpu.VMEM, pltpu.SMEM, pltpu.SemaphoreType.DMA
    hop_shape = (blocks, channels, side)
    halo_shape = send_shape(channels, peers, halo // peers)
    last_shape = send_shape(3 * channels, peers, nodes // peers)
    group = 256
    chunks = 1

    def out(shape):
        return jax.ShapeDtypeStruct(shape, BF16)

    def early(hop, staged):
        shape = (peers // 2, channels, slot)
        others = (slots - blocks, side, side)
        near, far, total, *rest = pl.pallas_call(
            lambda *refs: early_kernel(staged, *refs),
            out_shape=(
                out(shape),
                out(shape),
                jax.ShapeDtypeStruct((blocks, channels + EXTRA, side), F32),
            )
            + (out(others),) * staged,
            in_specs=[HBM, HBM, VMEM],
            out_specs=(VMEM,) * (3 + staged),
            scratch_shapes=[
                vmem((peers, channels, slot), BF16),
                vmem(send_order.shape, jnp.int32),
                vmem((blocks, side, side), BF16),
                dma((3,)),
            ],
            compiler_params=params(),
            cost_estimate=cost(2 * channels * nodes * nodes, 8 * channels * nodes),
            name="early",
        )(in_hbm(send_order), in_hbm(tiles), hop)
        sent = lax.ppermute(far, "dom", pairs(peers // 2, peers))
        return (near, sent), total, rest

    def relay(blocks_of):
        steps = peers // 2
        moved = pl.pallas_call(
            relay_kernel,
            out_shape=(out((2 * channels, slot)),) * steps,
            in_specs=[VMEM] * 2,
            out_specs=(VMEM,) * steps,
            compiler_params=params(),
            cost_estimate=cost(0, 8 * channels * nodes),
            name="relay",
        )(*blocks_of)
        return [moved[0]] + [
            lax.ppermute(moved[step], "dom", pairs(step, peers)) for step in range(1, steps)
        ]

    def late(keep, index, others, total, hop, arrived):
        shape = (peers, channels, index.shape[1] // peers)
        return pl.pallas_call(
            lambda *refs: finish_kernel(group, keep, *refs),
            out_shape=(out(hop_shape),) * keep + (out(shape),),
            in_specs=[VMEM] * 7,
            out_specs=(VMEM,) * (keep + 1),
            scratch_shapes=[
                vmem((fixed, channels + EXTRA, side), BF16),
                vmem((blocks + 1, channels + EXTRA, side), F32),
            ],
            compiler_params=params(),
        )(tile_dst, tile_src, index, others, total, hop, arrived)

    *own, halo_rows = pl.pallas_call(
        lambda *refs: sketch_kernel(reps, chunks, *refs),
        out_shape=(out((channels, width)),) * reps
        + (jax.ShapeDtypeStruct(halo_index.shape, jnp.int32),),
        in_specs=[HBM] * 3,
        out_specs=(VMEM,) * (reps + 1),
        scratch_shapes=[
            vmem((reps, channels, width), BF16),
            vmem(features.shape, BF16),
            vmem(sketch_matrix.shape, BF16),
            dma((chunks + 2,)),
        ],
        compiler_params=params(),
        name="sketch",
    )(in_hbm(features), in_hbm(sketch_matrix), in_hbm(halo_index))
    arrived = [own[0]]
    for step in range(1, reps):
        arrived.append(lax.ppermute(own[step], "rep", pairs(step, reps)))
    hop0, send = pl.pallas_call(
        lambda *refs: pick_kernel(reps, group, *refs),
        out_shape=(out(hop_shape), out(halo_shape)),
        in_specs=[VMEM] * (reps + 1),
        out_specs=(VMEM, VMEM),
        compiler_params=params(),
        name="pick",
    )(halo_rows, *arrived)
    slot = nodes // peers
    whole_lanes = slot % 128 == 0 and (halo // peers) % 128 == 0
    if whole_lanes and peers > 1 and peers & (peers - 1) == 0:
        half = peers // 2
        halo0 = exchange(send, peers)
        early0, total, others = early(hop0, 1)
        others = others[0]
        hop1, send = late(1, halo_rows, others, total, hop0, halo0)
        halo1 = exchange(send, peers)
        early1, total, _ = early(hop1, 0)
        (send,) = late(0, send_order, others, total, hop1, halo1)
        last = exchange(send, peers)
        moved0, moved1 = relay(early0), relay(early1)
        whole = out((3, channels, nodes))
        placed, table, block = pl.pallas_call(
            lambda *refs: place_first_kernel(peers, *refs),
            out_shape=(
                whole,
                out((nodes, side)),
                jax.ShapeDtypeStruct((1, nodes), jnp.int32),
            ),
            in_specs=[VMEM] * (half + 1),
            out_specs=(HBM, VMEM, VMEM),
            scratch_shapes=[vmem((1, channels, nodes), BF16), dma((blocks,))],
            compiler_params=params(),
            cost_estimate=cost(2 * channels * nodes * nodes, 4 * channels * nodes),
            name="place0",
        )(arrival_place, *moved0)
        return pl.pallas_call(
            lambda *refs: place_rest_kernel(peers, *refs),
            out_shape=whole,
            in_specs=[HBM] + [VMEM] * (half + 3),
            out_specs=HBM,
            scratch_shapes=[vmem((2, channels, nodes), BF16), dma((blocks,))],
            input_output_aliases={0: 0},
            compiler_params=params(),
            name="place",
        )(placed, table, block, *moved1, last)
    halo0 = exchange(send, peers)

    def work(index):
        return [
            smem(tile_dst.shape, jnp.int32),
            smem(tile_src.shape, jnp.int32),
            vmem(index.shape, jnp.int32),
            vmem(tiles.shape, BF16),
            vmem((fixed, channels + EXTRA, side), BF16),
            vmem((blocks + 1, channels + EXTRA, side), F32),
            dma((3 + slots // 4,)),
        ]

    hop1, send = pl.pallas_call(
        lambda *refs: combine_pick_kernel(group, *refs),
        out_shape=(out(hop_shape), out(halo_shape)),
        in_specs=[HBM] * 4 + [VMEM] * 2,
        out_specs=(VMEM, VMEM),
        scratch_shapes=work(halo_index),
        compiler_params=params(),
        name="combine_pick",
    )(in_hbm(tile_dst), in_hbm(tile_src), in_hbm(halo_index), in_hbm(tiles), hop0, halo0)
    halo1 = exchange(send, peers)
    send = pl.pallas_call(
        lambda *refs: combine_last_kernel(group, *refs),
        out_shape=out(last_shape),
        in_specs=[HBM] * 4 + [VMEM] * 3,
        out_specs=VMEM,
        scratch_shapes=work(send_order),
        compiler_params=params(),
        name="combine_last",
    )(in_hbm(tile_dst), in_hbm(tile_src), in_hbm(send_order), in_hbm(tiles), hop1, halo1, hop0)
    last = exchange(send, peers)
    return pl.pallas_call(
        lambda *refs: place_kernel(side, *refs),
        out_shape=out((3, channels, nodes)),
        in_specs=[VMEM, VMEM],
        out_specs=VMEM,
        compiler_params=params(),
        name="place",
    )(arrival_place, last)


def solution(mesh):
    in_specs = (
        P(("dom", "rep"), None),
        P(),
        P("dom", None, None, None),
        P("dom", None),
        P("dom", None),
        P("dom", None),
        P("dom", None),
        P("dom", None),
    )
    out_specs = P(None, "rep", "dom")

    return jax.shard_map(
        on_device, mesh=mesh, in_specs=in_specs, out_specs=out_specs, check_vma=False
    )
```

```python
import jax
import jax.numpy as jnp
from jax import lax
from jax.experimental import pallas as pl
from jax.experimental.pallas import tpu as pltpu
from jax.sharding import PartitionSpec as P


BF16 = jnp.bfloat16
F32 = jnp.float32
EXTRA = 16
KEPT = 8
NN = (((1,), (0,)), ((), ()))
NT = (((1,), (1,)), ((), ()))
VMEM = pl.BlockSpec(memory_space=pltpu.VMEM)
HBM = pl.BlockSpec(memory_space=pltpu.HBM)


def params():
    return pltpu.CompilerParams(vmem_limit_bytes=40 * 1024 * 1024)


def cost(flops, size):
    return pl.CostEstimate(flops=flops, bytes_accessed=size, transcendentals=0)


def in_hbm(array):
    return pltpu.with_memory_space_constraint(array, pltpu.HBM)


def dot(left, right, dims=NN):
    return lax.dot_general(left, right, dims, preferred_element_type=F32)


def split(index, side, blocks):
    block = jnp.zeros_like(index)
    for edge in range(1, blocks):
        block += (index >= edge * side).astype(jnp.int32)
    return block, index - block * side


def one_hot(index, rows):
    row = lax.broadcasted_iota(jnp.int32, (rows, index.shape[1]), 0)
    return jnp.where(row == index, 1.0, 0.0).astype(BF16)


def pick(stack, blocks, index, side, group):
    rows = stack.shape[0] // blocks
    parts = []
    for start in range(0, index.shape[1], group):
        block, inner = split(index[:, start : start + group], side, blocks)
        every = dot(stack, one_hot(inner, side))
        chosen = every[:rows]
        for other in range(1, blocks):
            chosen = jnp.where(block == other, every[other * rows : (other + 1) * rows], chosen)
        parts.append(chosen.astype(BF16))
    return parts


def store_slots(buffer, parts, group):
    if len(buffer.shape) == 2:
        for place, part in enumerate(parts):
            buffer[:, place * group : (place + 1) * group] = part
        return
    slot = buffer.shape[2]
    for place, part in enumerate(parts):
        for start in range(0, group, slot):
            buffer[(place * group + start) // slot] = part[:, start : start + slot]


def send_shape(channels, peers, slot):
    if slot % 128:
        return (channels, peers * slot)
    return (peers, channels, slot)


def exchange(send, peers):
    if send.ndim == 2:
        send = send.reshape(send.shape[0], peers, -1).transpose(1, 0, 2)
    arrived = lax.all_to_all(send, "dom", 0, 0, tiled=True)
    if arrived.shape[2] % 128 == 0:
        return arrived
    return arrived.transpose(1, 0, 2).reshape(arrived.shape[1], -1)


def load_wide(ref):
    if len(ref.shape) == 2:
        return ref[...]
    return jnp.concatenate([ref[peer] for peer in range(ref.shape[0])], axis=1)


def partner(me, step, count):
    if count & (count - 1) == 0:
        return me ^ step
    return lax.rem(me + step, count)


def source(me, step, count):
    if count & (count - 1) == 0:
        return me ^ step
    return lax.rem(me + count - step, count)


def pairs(step, count):
    if count & (count - 1) == 0:
        return [(rank, rank ^ step) for rank in range(count)]
    return [(rank, (rank + step) % count) for rank in range(count)]


def sketch_kernel(count, chunks, features_in, sketch_in, index_in, *rest):
    outs, (index_out, full, features, sketch, sems) = rest[:count], rest[count:]
    channels, width = outs[0].shape
    step = width // chunks
    copies = [pltpu.make_async_copy(sketch_in, sketch, sems.at[chunks])]
    for chunk in range(chunks):
        rows = pl.ds(chunk * step, step)
        copies.append(
            pltpu.make_async_copy(features_in.at[rows, :], features.at[rows, :], sems.at[chunk])
        )
    copies.append(pltpu.make_async_copy(index_in, index_out, sems.at[chunks + 1]))
    for copy in copies:
        copy.start()
    copies[0].wait()
    for chunk in range(chunks):
        copies[chunk + 1].wait()
        rows = slice(chunk * step, (chunk + 1) * step)
        product = dot(features[rows, :], sketch[...]).T.astype(BF16)
        for part in range(count):
            full[part, :, rows] = product[part * channels : (part + 1) * channels]
    me = lax.axis_index("rep")
    for part in range(count):
        outs[part][...] = full[partner(me, part, count)]
    copies[-1].wait()


def pick_kernel(count, group, index, *rest):
    arrived, (hop, send) = rest[:count], rest[count:]
    blocks, _, side = hop.shape
    per = blocks // count
    me = lax.axis_index("rep")
    for step in range(count):
        first = source(me, step, count) * per
        for part in range(per):
            hop[first + part] = arrived[step][:, part * side : (part + 1) * side]
    stack = jnp.concatenate([hop[block] for block in range(blocks)], 0)
    store_slots(send, pick(stack, blocks, index[...], side, group), group)


def combine(dst_in, src_in, index_in, tiles_in, hop, arrived_ref, scratch, store):
    dst, src, index, tiles, columns, sums, sems = scratch
    blocks, channels, side = hop.shape
    slots = tiles.shape[0]
    fixed = columns.shape[0]
    small = [
        pltpu.make_async_copy(dst_in, dst, sems.at[0]),
        pltpu.make_async_copy(src_in, src, sems.at[1]),
        pltpu.make_async_copy(index_in, index, sems.at[2]),
    ]
    chunk = 4
    large = []
    for start in range(0, slots, chunk):
        rows = pl.ds(start, chunk)
        large.append(
            pltpu.make_async_copy(tiles_in.at[rows], tiles.at[rows], sems.at[3 + start // chunk])
        )
    for copy in large + small:
        copy.start()
    columns[:, channels:, :] = jnp.ones((fixed, EXTRA, side), BF16)
    for block in range(blocks):
        columns[block, :channels, :] = hop[block]
    arrived = load_wide(arrived_ref)
    for block in range(blocks, fixed):
        start = (block - blocks) * side
        columns[block, :channels, :] = arrived[:, start : start + side]
    for slot in range(slots):
        if slot % chunk == 0:
            large[slot // chunk].wait()
        if slot < blocks:
            sums[slot] = dot(columns[slot], tiles[slot], NT)
            continue
        if slot == blocks:
            for copy in small:
                copy.wait()
        target = dst[0, slot]
        target = jnp.where(target < 0, blocks, target)
        start = slot if slot < fixed else src[0, slot]
        sums[target] = sums[target] + dot(columns[start], tiles[slot], NT)
    results = []
    for block in range(blocks):
        total = sums[block]
        result = (total[:channels] / total[channels : channels + 1]).astype(BF16)
        store(block, result)
        results.append(result)
    return results


def combine_pick_kernel(
    group, dst_in, src_in, index_in, tiles_in, hop, arrived_ref, result, send, *scratch
):
    def store(block, value):
        result[block] = value

    results = combine(dst_in, src_in, index_in, tiles_in, hop, arrived_ref, scratch, store)
    blocks, _, side = hop.shape
    index = scratch[2]
    stack = jnp.concatenate(results, 0)
    store_slots(send, pick(stack, blocks, index[...], side, group), group)


def early_kernel(staged, index_in, tiles_in, hop, near, far, total, *rest):
    full, index, tiles, sems = rest[-4:]
    blocks, channels, side = hop.shape
    copies = [
        pltpu.make_async_copy(index_in, index, sems.at[0]),
        pltpu.make_async_copy(tiles_in.at[pl.ds(0, blocks)], tiles, sems.at[1]),
    ]
    if staged:
        others = tiles_in.shape[0] - blocks
        copies.append(
            pltpu.make_async_copy(tiles_in.at[pl.ds(blocks, others)], rest[0], sems.at[2])
        )
    for copy in copies:
        copy.start()
    peers, _, slot = full.shape
    stack = jnp.concatenate([hop[block] for block in range(blocks)], 0)
    copies[0].wait()
    for peer, part in enumerate(pick(stack, blocks, index[...], side, slot)):
        full[peer] = part
    me = lax.axis_index("dom")
    half = peers // 2
    for step in range(half):
        near[step] = full[me ^ step]
        far[step] = full[me ^ half ^ step]
    ones = jnp.ones((EXTRA, side), BF16)
    copies[1].wait()
    for block in range(blocks):
        columns = jnp.concatenate([hop[block], ones], 0)
        total[block] = dot(columns, tiles[block], NT)[: channels + KEPT]
    if staged:
        copies[2].wait()


def finish(dst, src, tiles, total, hop, arrived, columns, sums):
    blocks, channels, side = hop.shape
    fixed = columns.shape[0]
    slots = blocks + tiles.shape[0]
    lane = lax.broadcasted_iota(jnp.int32, dst.shape, 1)
    targets, starts = {}, {slot: slot for slot in range(fixed)}
    for slot in range(blocks, slots):
        target = jnp.sum(jnp.where(lane == slot, dst[...], 0))
        targets[slot] = jnp.where(target < 0, blocks, target)
    for slot in range(fixed, slots):
        starts[slot] = jnp.sum(jnp.where(lane == slot, src[...], 0))
    columns[:, channels:, :] = jnp.ones((fixed, EXTRA, side), BF16)
    for block in range(blocks):
        columns[block, :channels, :] = hop[block]
        sums[block] = total[block]
    wide = load_wide(arrived)
    for block in range(blocks, fixed):
        start = (block - blocks) * side
        columns[block, :channels, :] = wide[:, start : start + side]
    products = [
        dot(columns[starts[slot]], tiles[slot - blocks], NT) for slot in range(blocks, fixed)
    ]
    for slot in range(blocks, slots):
        target = targets[slot]
        if slot < fixed:
            product = products[slot - blocks]
        else:
            product = dot(columns[starts[slot]], tiles[slot - blocks], NT)
        sums[target] = sums[target] + product[: channels + KEPT]
    results = []
    for block in range(blocks):
        whole = sums[block]
        results.append((whole[:channels] / whole[channels : channels + 1]).astype(BF16))
    return results


def finish_kernel(
    group, keep, dst, src, index, tiles, total, hop, arrived, *rest
):
    send, scratch = rest[keep], rest[keep + 1 :]
    results = finish(dst, src, tiles, total, hop, arrived, *scratch)
    blocks, _, side = hop.shape
    if keep:
        for block, result in enumerate(results):
            rest[0][block] = result
    stack = jnp.concatenate(results, 0)
    store_slots(send, pick(stack, blocks, index[...], side, group), group)


def relay_kernel(near, sent, *outs):
    channels = near.shape[1]
    for step, out in enumerate(outs):
        out[:channels] = near[step]
        out[channels:] = sent[step]


def combine_last_kernel(
    group, dst_in, src_in, index_in, tiles_in, hop, arrived_ref, hop0, send, *scratch
):
    results = combine(
        dst_in, src_in, index_in, tiles_in, hop, arrived_ref, scratch, lambda *_: None
    )
    blocks, _, side = hop.shape
    index = scratch[2]
    stack = []
    for block in range(blocks):
        stack += [hop0[block], hop[block], results[block]]
    stack = jnp.concatenate(stack, 0)
    store_slots(send, pick(stack, blocks, index[...], side, group), group)


def scatter(parts, table, block, out, out_ref, first, sems):
    hops, channels, nodes = out.shape
    side = table.shape[1]
    stacked = jnp.concatenate(parts, 1)
    rows = stacked.shape[0]
    group = max(128 // rows, 1)
    copies = []
    for start in range(0, nodes // side, group):
        masks = [
            jnp.where(block == other, 1.0, 0.0).astype(BF16)
            for other in range(start, start + group)
        ]
        placed = dot(jnp.concatenate([stacked * mask for mask in masks], 0), table).astype(BF16)
        for other in range(group):
            columns = slice((start + other) * side, (start + other + 1) * side)
            for hop in range(hops):
                row = other * rows + hop * channels
                out[hop, :, columns] = placed[row : row + channels]
        columns = pl.ds(start * side, group * side)
        copies.append(
            pltpu.make_async_copy(
                out.at[:, :, columns],
                out_ref.at[pl.ds(first, hops), :, columns],
                sems.at[start],
            )
        )
        copies[-1].start()
    for copy in copies:
        copy.wait()


def place_first_kernel(peers, index_ref, *rest):
    moved, (out_ref, table_ref, block_ref, out, sems) = rest[:-5], rest[-5:]
    _, channels, nodes = out.shape
    side = table_ref.shape[1]
    blocks = nodes // side
    half = peers // 2
    slot = nodes // peers
    me = lax.axis_index("dom")
    parts, indexes = [], []
    for step in range(peers):
        start = pl.multiple_of((me ^ step) * slot, slot)
        indexes.append(index_ref[:, pl.ds(start, slot)])
        first = (step // half) * channels
        parts.append(moved[step % half][first : first + channels])
    block, inner = split(jnp.concatenate(indexes, 1), side, blocks)
    block_ref[...] = block
    table = jnp.concatenate(
        [one_hot(inner[:, start : start + side], side).T for start in range(0, nodes, side)], 0
    )
    table_ref[...] = table
    scatter(parts, table, block, out, out_ref, 0, sems)


def place_rest_kernel(peers, _, table_ref, block_ref, *rest):
    moved, last, (out_ref, out, sems) = rest[:-4], rest[-4], rest[-3:]
    channels = out.shape[1]
    half = peers // 2
    me = lax.axis_index("dom")
    parts = []
    for step in range(peers):
        first = (step // half) * channels
        arrived = moved[step % half][first : first + channels]
        parts.append(jnp.concatenate([arrived, last[me ^ step]], 0))
    scatter(parts, table_ref[...], block_ref[...], out, out_ref, 1, sems)


def place_kernel(side, index_ref, arrived_ref, out_ref):
    hops, channels, nodes = out_ref.shape
    blocks = nodes // side
    stacked = load_wide(arrived_ref)
    block, inner = split(index_ref[...], side, blocks)
    table = one_hot(inner, side)
    for other in range(blocks):
        mask = jnp.where(block == other, 1.0, 0.0).astype(BF16)
        placed = dot(stacked * mask, table, NT).astype(BF16)
        for hop in range(hops):
            out_ref[hop, :, other * side : (other + 1) * side] = placed[
                hop * channels : (hop + 1) * channels
            ]


def on_device(
    features, sketch_matrix, tiles, tile_dst, tile_src, halo_index, send_order, arrival_place
):
    reps = lax.axis_size("rep")
    peers = lax.axis_size("dom")
    width = features.shape[0]
    nodes = width * reps
    channels = sketch_matrix.shape[1] // reps
    halo = halo_index.shape[1]
    tiles = tiles[0]
    slots, side, _ = tiles.shape
    blocks = nodes // side
    fixed = (nodes + halo) // side
    vmem, smem, dma = pltpu.VMEM, pltpu.SMEM, pltpu.SemaphoreType.DMA
    hop_shape = (blocks, channels, side)
    halo_shape = send_shape(channels, peers, halo // peers)
    last_shape = send_shape(3 * channels, peers, nodes // peers)
    group = 256
    chunks = 1

    def out(shape):
        return jax.ShapeDtypeStruct(shape, BF16)

    def early(hop, staged):
        shape = (peers // 2, channels, slot)
        others = (slots - blocks, side, side)
        near, far, total, *rest = pl.pallas_call(
            lambda *refs: early_kernel(staged, *refs),
            out_shape=(
                out(shape),
                out(shape),
                jax.ShapeDtypeStruct((blocks, channels + KEPT, side), F32),
            )
            + (out(others),) * staged,
            in_specs=[HBM, HBM, VMEM],
            out_specs=(VMEM,) * (3 + staged),
            scratch_shapes=[
                vmem((peers, channels, slot), BF16),
                vmem(send_order.shape, jnp.int32),
                vmem((blocks, side, side), BF16),
                dma((3,)),
            ],
            compiler_params=params(),
            cost_estimate=cost(2 * channels * nodes * nodes, 8 * channels * nodes),
            name="early",
        )(in_hbm(send_order), in_hbm(tiles), hop)
        sent = lax.ppermute(far, "dom", pairs(peers // 2, peers))
        return (near, sent), total, rest

    def relay(blocks_of):
        steps = peers // 2
        moved = pl.pallas_call(
            relay_kernel,
            out_shape=(out((2 * channels, slot)),) * steps,
            in_specs=[VMEM] * 2,
            out_specs=(VMEM,) * steps,
            compiler_params=params(),
            cost_estimate=cost(0, 8 * channels * nodes),
            name="relay",
        )(*blocks_of)
        sent = [moved[0]]
        for step in range(1, steps):
            sent.append(lax.ppermute(moved[step], "dom", pairs(step, peers)))
        return sent

    def late(keep, index, others, total, hop, arrived):
        shape = (peers, channels, index.shape[1] // peers)
        return pl.pallas_call(
            lambda *refs: finish_kernel(group, keep, *refs),
            out_shape=(out(hop_shape),) * keep + (out(shape),),
            in_specs=[VMEM] * 7,
            out_specs=(VMEM,) * (keep + 1),
            scratch_shapes=[
                vmem((fixed, channels + EXTRA, side), BF16),
                vmem((blocks + 1, channels + KEPT, side), F32),
            ],
            compiler_params=params(),
        )(tile_dst, tile_src, index, others, total, hop, arrived)

    *own, halo_rows = pl.pallas_call(
        lambda *refs: sketch_kernel(reps, chunks, *refs),
        out_shape=(out((channels, width)),) * reps
        + (jax.ShapeDtypeStruct(halo_index.shape, jnp.int32),),
        in_specs=[HBM] * 3,
        out_specs=(VMEM,) * (reps + 1),
        scratch_shapes=[
            vmem((reps, channels, width), BF16),
            vmem(features.shape, BF16),
            vmem(sketch_matrix.shape, BF16),
            dma((chunks + 2,)),
        ],
        compiler_params=params(),
        name="sketch",
    )(in_hbm(features), in_hbm(sketch_matrix), in_hbm(halo_index))
    arrived = [own[0]]
    for step in range(1, reps):
        arrived.append(lax.ppermute(own[step], "rep", pairs(step, reps)))
    hop0, send = pl.pallas_call(
        lambda *refs: pick_kernel(reps, group, *refs),
        out_shape=(out(hop_shape), out(halo_shape)),
        in_specs=[VMEM] * (reps + 1),
        out_specs=(VMEM, VMEM),
        compiler_params=params(),
        name="pick",
    )(halo_rows, *arrived)
    slot = nodes // peers
    whole_lanes = slot % 128 == 0 and (halo // peers) % 128 == 0
    if whole_lanes and peers > 1 and peers & (peers - 1) == 0:
        half = peers // 2
        halo0 = exchange(send, peers)
        early0, total, others = early(hop0, 1)
        others = others[0]
        hop1, send = late(1, halo_rows, others, total, hop0, halo0)
        halo1 = exchange(send, peers)
        early1, total, _ = early(hop1, 0)
        (send,) = late(0, send_order, others, total, hop1, halo1)
        last = exchange(send, peers)
        moved0, moved1 = relay(early0), relay(early1)
        whole = out((3, channels, nodes))
        placed, table, block = pl.pallas_call(
            lambda *refs: place_first_kernel(peers, *refs),
            out_shape=(
                whole,
                out((nodes, side)),
                jax.ShapeDtypeStruct((1, nodes), jnp.int32),
            ),
            in_specs=[VMEM] * (half + 1),
            out_specs=(HBM, VMEM, VMEM),
            scratch_shapes=[vmem((1, channels, nodes), BF16), dma((blocks,))],
            compiler_params=params(),
            cost_estimate=cost(2 * channels * nodes * nodes, 4 * channels * nodes),
            name="place0",
        )(arrival_place, *moved0)
        return pl.pallas_call(
            lambda *refs: place_rest_kernel(peers, *refs),
            out_shape=whole,
            in_specs=[HBM] + [VMEM] * (half + 3),
            out_specs=HBM,
            scratch_shapes=[vmem((2, channels, nodes), BF16), dma((blocks,))],
            input_output_aliases={0: 0},
            compiler_params=params(),
            name="place",
        )(placed, table, block, *moved1, last)
    halo0 = exchange(send, peers)

    def work(index):
        return [
            smem(tile_dst.shape, jnp.int32),
            smem(tile_src.shape, jnp.int32),
            vmem(index.shape, jnp.int32),
            vmem(tiles.shape, BF16),
            vmem((fixed, channels + EXTRA, side), BF16),
            vmem((blocks + 1, channels + EXTRA, side), F32),
            dma((3 + slots // 4,)),
        ]

    hop1, send = pl.pallas_call(
        lambda *refs: combine_pick_kernel(group, *refs),
        out_shape=(out(hop_shape), out(halo_shape)),
        in_specs=[HBM] * 4 + [VMEM] * 2,
        out_specs=(VMEM, VMEM),
        scratch_shapes=work(halo_index),
        compiler_params=params(),
        name="combine_pick",
    )(in_hbm(tile_dst), in_hbm(tile_src), in_hbm(halo_index), in_hbm(tiles), hop0, halo0)
    halo1 = exchange(send, peers)
    send = pl.pallas_call(
        lambda *refs: combine_last_kernel(group, *refs),
        out_shape=out(last_shape),
        in_specs=[HBM] * 4 + [VMEM] * 3,
        out_specs=VMEM,
        scratch_shapes=work(send_order),
        compiler_params=params(),
        name="combine_last",
    )(in_hbm(tile_dst), in_hbm(tile_src), in_hbm(send_order), in_hbm(tiles), hop1, halo1, hop0)
    last = exchange(send, peers)
    return pl.pallas_call(
        lambda *refs: place_kernel(side, *refs),
        out_shape=out((3, channels, nodes)),
        in_specs=[VMEM, VMEM],
        out_specs=VMEM,
        compiler_params=params(),
        name="place",
    )(arrival_place, last)


def solution(mesh):
    in_specs = (
        P(("dom", "rep"), None),
        P(),
        P("dom", None, None, None),
        P("dom", None),
        P("dom", None),
        P("dom", None),
        P("dom", None),
        P("dom", None),
    )
    out_specs = P(None, "rep", "dom")

    return jax.shard_map(
        on_device, mesh=mesh, in_specs=in_specs, out_specs=out_specs, check_vma=False
    )
```

```python
import jax
import jax.numpy as jnp
from jax import lax
from jax.experimental import pallas as pl
from jax.experimental.pallas import tpu as pltpu
from jax.sharding import PartitionSpec as P


BF16 = jnp.bfloat16
F32 = jnp.float32
EXTRA = 16
KEPT = 8
NN = (((1,), (0,)), ((), ()))
NT = (((1,), (1,)), ((), ()))
VMEM = pl.BlockSpec(memory_space=pltpu.VMEM)
HBM = pl.BlockSpec(memory_space=pltpu.HBM)


def params():
    return pltpu.CompilerParams(vmem_limit_bytes=40 * 1024 * 1024)


def cost(flops, size):
    return pl.CostEstimate(flops=flops, bytes_accessed=size, transcendentals=0)


def in_hbm(array):
    return pltpu.with_memory_space_constraint(array, pltpu.HBM)


def dot(left, right, dims=NN):
    return lax.dot_general(left, right, dims, preferred_element_type=F32)


def split(index, side, blocks):
    block = jnp.zeros_like(index)
    for edge in range(1, blocks):
        block += (index >= edge * side).astype(jnp.int32)
    return block, index - block * side


def one_hot(index, rows):
    row = lax.broadcasted_iota(jnp.int32, (rows, index.shape[1]), 0)
    return jnp.where(row == index, 1.0, 0.0).astype(BF16)


def pick(stack, blocks, index, side, group):
    rows = stack.shape[0] // blocks
    parts = []
    for start in range(0, index.shape[1], group):
        block, inner = split(index[:, start : start + group], side, blocks)
        every = dot(stack, one_hot(inner, side))
        chosen = every[:rows]
        for other in range(1, blocks):
            chosen = jnp.where(block == other, every[other * rows : (other + 1) * rows], chosen)
        parts.append(chosen.astype(BF16))
    return parts


def store_slots(buffer, parts, group, turn=0):
    if len(buffer.shape) == 2:
        for place, part in enumerate(parts):
            buffer[:, place * group : (place + 1) * group] = part
        return
    slot = buffer.shape[2]
    for place, part in enumerate(parts):
        for start in range(0, group, slot):
            peer = (place * group + start) // slot
            buffer[peer ^ turn] = part[:, start : start + slot]


def send_shape(channels, peers, slot):
    if slot % 128:
        return (channels, peers * slot)
    return (peers, channels, slot)


def exchange(send, peers, turn=0):
    if send.ndim == 2:
        send = send.reshape(send.shape[0], peers, -1).transpose(1, 0, 2)
    ranks = [[rank ^ turn for rank in range(peers)]] if turn else None
    arrived = lax.all_to_all(send, "dom", 0, 0, tiled=True, axis_index_groups=ranks)
    if arrived.shape[2] % 128 == 0:
        return arrived
    return arrived.transpose(1, 0, 2).reshape(arrived.shape[1], -1)


def load_wide(ref, turn=0):
    if len(ref.shape) == 2:
        return ref[...]
    return jnp.concatenate([ref[peer ^ turn] for peer in range(ref.shape[0])], axis=1)


def partner(me, step, count):
    if count & (count - 1) == 0:
        return me ^ step
    return lax.rem(me + step, count)


def source(me, step, count):
    if count & (count - 1) == 0:
        return me ^ step
    return lax.rem(me + count - step, count)


def pairs(step, count):
    if count & (count - 1) == 0:
        return [(rank, rank ^ step) for rank in range(count)]
    return [(rank, (rank + step) % count) for rank in range(count)]


def sketch_kernel(count, chunks, features_in, sketch_in, index_in, *rest):
    outs, (index_out, full, features, sketch, sems) = rest[:count], rest[count:]
    channels, width = outs[0].shape
    step = width // chunks
    copies = [pltpu.make_async_copy(sketch_in, sketch, sems.at[chunks])]
    for chunk in range(chunks):
        rows = pl.ds(chunk * step, step)
        copies.append(
            pltpu.make_async_copy(features_in.at[rows, :], features.at[rows, :], sems.at[chunk])
        )
    copies.append(pltpu.make_async_copy(index_in, index_out, sems.at[chunks + 1]))
    for copy in copies:
        copy.start()
    copies[0].wait()
    for chunk in range(chunks):
        copies[chunk + 1].wait()
        rows = slice(chunk * step, (chunk + 1) * step)
        product = dot(features[rows, :], sketch[...]).T.astype(BF16)
        for part in range(count):
            full[part, :, rows] = product[part * channels : (part + 1) * channels]
    me = lax.axis_index("rep")
    for part in range(count):
        outs[part][...] = full[partner(me, part, count)]
    copies[-1].wait()


def pick_kernel(count, group, turn, index, *rest):
    arrived, (hop, send) = rest[:count], rest[count:]
    blocks, _, side = hop.shape
    per = blocks // count
    me = lax.axis_index("rep")
    for step in range(count):
        first = source(me, step, count) * per
        for part in range(per):
            hop[first + part] = arrived[step][:, part * side : (part + 1) * side]
    stack = jnp.concatenate([hop[block] for block in range(blocks)], 0)
    store_slots(send, pick(stack, blocks, index[...], side, group), group, turn)


def combine(dst_in, src_in, index_in, tiles_in, hop, arrived_ref, scratch, store):
    dst, src, index, tiles, columns, sums, sems = scratch
    blocks, channels, side = hop.shape
    slots = tiles.shape[0]
    fixed = columns.shape[0]
    small = [
        pltpu.make_async_copy(dst_in, dst, sems.at[0]),
        pltpu.make_async_copy(src_in, src, sems.at[1]),
        pltpu.make_async_copy(index_in, index, sems.at[2]),
    ]
    chunk = 4
    large = []
    for start in range(0, slots, chunk):
        rows = pl.ds(start, chunk)
        large.append(
            pltpu.make_async_copy(tiles_in.at[rows], tiles.at[rows], sems.at[3 + start // chunk])
        )
    for copy in large + small:
        copy.start()
    columns[:, channels:, :] = jnp.ones((fixed, EXTRA, side), BF16)
    for block in range(blocks):
        columns[block, :channels, :] = hop[block]
    arrived = load_wide(arrived_ref)
    for block in range(blocks, fixed):
        start = (block - blocks) * side
        columns[block, :channels, :] = arrived[:, start : start + side]
    for slot in range(slots):
        if slot % chunk == 0:
            large[slot // chunk].wait()
        if slot < blocks:
            sums[slot] = dot(columns[slot], tiles[slot], NT)
            continue
        if slot == blocks:
            for copy in small:
                copy.wait()
        target = dst[0, slot]
        target = jnp.where(target < 0, blocks, target)
        start = slot if slot < fixed else src[0, slot]
        sums[target] = sums[target] + dot(columns[start], tiles[slot], NT)
    results = []
    for block in range(blocks):
        total = sums[block]
        result = (total[:channels] / total[channels : channels + 1]).astype(BF16)
        store(block, result)
        results.append(result)
    return results


def combine_pick_kernel(
    group, dst_in, src_in, index_in, tiles_in, hop, arrived_ref, result, send, *scratch
):
    def store(block, value):
        result[block] = value

    results = combine(dst_in, src_in, index_in, tiles_in, hop, arrived_ref, scratch, store)
    blocks, _, side = hop.shape
    index = scratch[2]
    stack = jnp.concatenate(results, 0)
    store_slots(send, pick(stack, blocks, index[...], side, group), group)


def early_kernel(staged, index_in, tiles_in, hop, near, far, total, *rest):
    full, index, tiles, sems = rest[-4:]
    blocks, channels, side = hop.shape
    copies = [
        pltpu.make_async_copy(index_in, index, sems.at[0]),
        pltpu.make_async_copy(tiles_in.at[pl.ds(0, blocks)], tiles, sems.at[1]),
    ]
    if staged:
        others = tiles_in.shape[0] - blocks
        copies.append(
            pltpu.make_async_copy(tiles_in.at[pl.ds(blocks, others)], rest[0], sems.at[2])
        )
    for copy in copies:
        copy.start()
    peers, _, slot = full.shape
    stack = jnp.concatenate([hop[block] for block in range(blocks)], 0)
    copies[0].wait()
    for peer, part in enumerate(pick(stack, blocks, index[...], side, slot)):
        full[peer] = part
    me = lax.axis_index("dom")
    half = peers // 2
    for step in range(half):
        near[step] = full[me ^ step]
        far[step] = full[me ^ half ^ step]
    ones = jnp.ones((EXTRA, side), BF16)
    copies[1].wait()
    for block in range(blocks):
        columns = jnp.concatenate([hop[block], ones], 0)
        total[block] = dot(columns, tiles[block], NT)[: channels + KEPT]
    if staged:
        copies[2].wait()


def finish(turn, dst, src, tiles, total, hop, arrived, columns, sums):
    blocks, channels, side = hop.shape
    fixed = columns.shape[0]
    slots = blocks + tiles.shape[0]
    lane = lax.broadcasted_iota(jnp.int32, dst.shape, 1)
    targets, starts = {}, {slot: slot for slot in range(fixed)}
    for slot in range(blocks, slots):
        target = jnp.sum(jnp.where(lane == slot, dst[...], 0))
        targets[slot] = jnp.where(target < 0, blocks, target)
    for slot in range(fixed, slots):
        starts[slot] = jnp.sum(jnp.where(lane == slot, src[...], 0))
    columns[:, channels:, :] = jnp.ones((fixed, EXTRA, side), BF16)
    for block in range(blocks):
        columns[block, :channels, :] = hop[block]
        sums[block] = total[block]
    wide = load_wide(arrived, turn)
    for block in range(blocks, fixed):
        start = (block - blocks) * side
        columns[block, :channels, :] = wide[:, start : start + side]
    products = [
        dot(columns[starts[slot]], tiles[slot - blocks], NT) for slot in range(blocks, fixed)
    ]
    for slot in range(blocks, slots):
        target = targets[slot]
        if slot < fixed:
            product = products[slot - blocks]
        else:
            product = dot(columns[starts[slot]], tiles[slot - blocks], NT)
        sums[target] = sums[target] + product[: channels + KEPT]
    results = []
    for block in range(blocks):
        whole = sums[block]
        results.append((whole[:channels] / whole[channels : channels + 1]).astype(BF16))
    return results


def finish_kernel(
    group, turn, keep, dst, src, index, tiles, total, hop, arrived, *rest
):
    send, scratch = rest[keep], rest[keep + 1 :]
    results = finish(turn, dst, src, tiles, total, hop, arrived, *scratch)
    blocks, _, side = hop.shape
    if keep:
        for block, result in enumerate(results):
            rest[0][block] = result
    stack = jnp.concatenate(results, 0)
    store_slots(send, pick(stack, blocks, index[...], side, group), group, turn)


def relay_kernel(near, sent, *outs):
    channels = near.shape[1]
    for step, out in enumerate(outs):
        out[:channels] = near[step]
        out[channels:] = sent[step]


def combine_last_kernel(
    group, dst_in, src_in, index_in, tiles_in, hop, arrived_ref, hop0, send, *scratch
):
    results = combine(
        dst_in, src_in, index_in, tiles_in, hop, arrived_ref, scratch, lambda *_: None
    )
    blocks, _, side = hop.shape
    index = scratch[2]
    stack = []
    for block in range(blocks):
        stack += [hop0[block], hop[block], results[block]]
    stack = jnp.concatenate(stack, 0)
    store_slots(send, pick(stack, blocks, index[...], side, group), group)


def scatter(parts, table, block, out, out_ref, first, sems):
    hops, channels, nodes = out.shape
    side = table.shape[1]
    stacked = jnp.concatenate(parts, 1)
    rows = stacked.shape[0]
    group = max(128 // rows, 1)
    copies = []
    for start in range(0, nodes // side, group):
        masks = [
            jnp.where(block == other, 1.0, 0.0).astype(BF16)
            for other in range(start, start + group)
        ]
        placed = dot(jnp.concatenate([stacked * mask for mask in masks], 0), table).astype(BF16)
        for other in range(group):
            columns = slice((start + other) * side, (start + other + 1) * side)
            for hop in range(hops):
                row = other * rows + hop * channels
                out[hop, :, columns] = placed[row : row + channels]
        columns = pl.ds(start * side, group * side)
        copies.append(
            pltpu.make_async_copy(
                out.at[:, :, columns],
                out_ref.at[pl.ds(first, hops), :, columns],
                sems.at[start],
            )
        )
        copies[-1].start()
    for copy in copies:
        copy.wait()


def place_first_kernel(peers, index_ref, *rest):
    moved, (out_ref, table_ref, block_ref, out, sems) = rest[:-5], rest[-5:]
    _, channels, nodes = out.shape
    side = table_ref.shape[1]
    blocks = nodes // side
    half = peers // 2
    slot = nodes // peers
    me = lax.axis_index("dom")
    parts, indexes = [], []
    for step in range(peers):
        start = pl.multiple_of((me ^ step) * slot, slot)
        indexes.append(index_ref[:, pl.ds(start, slot)])
        first = (step // half) * channels
        parts.append(moved[step % half][first : first + channels])
    block, inner = split(jnp.concatenate(indexes, 1), side, blocks)
    block_ref[...] = block
    table = jnp.concatenate(
        [one_hot(inner[:, start : start + side], side).T for start in range(0, nodes, side)], 0
    )
    table_ref[...] = table
    scatter(parts, table, block, out, out_ref, 0, sems)


def place_rest_kernel(peers, _, table_ref, block_ref, *rest):
    moved, last, (out_ref, out, sems) = rest[:-4], rest[-4], rest[-3:]
    channels = out.shape[1]
    half = peers // 2
    me = lax.axis_index("dom")
    parts = []
    for step in range(peers):
        first = (step // half) * channels
        arrived = moved[step % half][first : first + channels]
        parts.append(jnp.concatenate([arrived, last[me ^ step ^ half]], 0))
    scatter(parts, table_ref[...], block_ref[...], out, out_ref, 1, sems)


def place_kernel(side, index_ref, arrived_ref, out_ref):
    hops, channels, nodes = out_ref.shape
    blocks = nodes // side
    stacked = load_wide(arrived_ref)
    block, inner = split(index_ref[...], side, blocks)
    table = one_hot(inner, side)
    for other in range(blocks):
        mask = jnp.where(block == other, 1.0, 0.0).astype(BF16)
        placed = dot(stacked * mask, table, NT).astype(BF16)
        for hop in range(hops):
            out_ref[hop, :, other * side : (other + 1) * side] = placed[
                hop * channels : (hop + 1) * channels
            ]


def on_device(
    features, sketch_matrix, tiles, tile_dst, tile_src, halo_index, send_order, arrival_place
):
    reps = lax.axis_size("rep")
    peers = lax.axis_size("dom")
    width = features.shape[0]
    nodes = width * reps
    channels = sketch_matrix.shape[1] // reps
    halo = halo_index.shape[1]
    tiles = tiles[0]
    slots, side, _ = tiles.shape
    blocks = nodes // side
    fixed = (nodes + halo) // side
    vmem, smem, dma = pltpu.VMEM, pltpu.SMEM, pltpu.SemaphoreType.DMA
    hop_shape = (blocks, channels, side)
    halo_shape = send_shape(channels, peers, halo // peers)
    last_shape = send_shape(3 * channels, peers, nodes // peers)
    group = 256
    chunks = 1
    slot = nodes // peers
    half = peers // 2
    whole_lanes = slot % 128 == 0 and (halo // peers) % 128 == 0
    turn = half if whole_lanes and peers & (peers - 1) == 0 else 0

    def out(shape):
        return jax.ShapeDtypeStruct(shape, BF16)

    def early(hop, staged):
        shape = (peers // 2, channels, slot)
        others = (slots - blocks, side, side)
        near, far, total, *rest = pl.pallas_call(
            lambda *refs: early_kernel(staged, *refs),
            out_shape=(
                out(shape),
                out(shape),
                jax.ShapeDtypeStruct((blocks, channels + KEPT, side), F32),
            )
            + (out(others),) * staged,
            in_specs=[HBM, HBM, VMEM],
            out_specs=(VMEM,) * (3 + staged),
            scratch_shapes=[
                vmem((peers, channels, slot), BF16),
                vmem(send_order.shape, jnp.int32),
                vmem((blocks, side, side), BF16),
                dma((3,)),
            ],
            compiler_params=params(),
            cost_estimate=cost(2 * channels * nodes * nodes, 8 * channels * nodes),
            name="early",
        )(in_hbm(send_order), in_hbm(tiles), hop)
        sent = lax.ppermute(far, "dom", pairs(peers // 2, peers))
        return (near, sent), total, rest

    def relay(blocks_of):
        steps = peers // 2
        moved = pl.pallas_call(
            relay_kernel,
            out_shape=(out((2 * channels, slot)),) * steps,
            in_specs=[VMEM] * 2,
            out_specs=(VMEM,) * steps,
            compiler_params=params(),
            cost_estimate=cost(0, 8 * channels * nodes),
            name="relay",
        )(*blocks_of)
        sent = [moved[0]]
        for step in range(1, steps):
            sent.append(lax.ppermute(moved[step], "dom", pairs(step, peers)))
        return sent

    def late(keep, index, others, total, hop, arrived):
        shape = (peers, channels, index.shape[1] // peers)
        return pl.pallas_call(
            lambda *refs: finish_kernel(group, half, keep, *refs),
            out_shape=(out(hop_shape),) * keep + (out(shape),),
            in_specs=[VMEM] * 7,
            out_specs=(VMEM,) * (keep + 1),
            scratch_shapes=[
                vmem((fixed, channels + EXTRA, side), BF16),
                vmem((blocks + 1, channels + KEPT, side), F32),
            ],
            compiler_params=params(),
        )(tile_dst, tile_src, index, others, total, hop, arrived)

    *own, halo_rows = pl.pallas_call(
        lambda *refs: sketch_kernel(reps, chunks, *refs),
        out_shape=(out((channels, width)),) * reps
        + (jax.ShapeDtypeStruct(halo_index.shape, jnp.int32),),
        in_specs=[HBM] * 3,
        out_specs=(VMEM,) * (reps + 1),
        scratch_shapes=[
            vmem((reps, channels, width), BF16),
            vmem(features.shape, BF16),
            vmem(sketch_matrix.shape, BF16),
            dma((chunks + 2,)),
        ],
        compiler_params=params(),
        name="sketch",
    )(in_hbm(features), in_hbm(sketch_matrix), in_hbm(halo_index))
    arrived = [own[0]]
    for step in range(1, reps):
        arrived.append(lax.ppermute(own[step], "rep", pairs(step, reps)))
    hop0, send = pl.pallas_call(
        lambda *refs: pick_kernel(reps, group, turn, *refs),
        out_shape=(out(hop_shape), out(halo_shape)),
        in_specs=[VMEM] * (reps + 1),
        out_specs=(VMEM, VMEM),
        compiler_params=params(),
        name="pick",
    )(halo_rows, *arrived)
    if turn:
        halo0 = exchange(send, peers, turn)
        early0, total, others = early(hop0, 1)
        others = others[0]
        hop1, send = late(1, halo_rows, others, total, hop0, halo0)
        halo1 = exchange(send, peers, turn)
        early1, total, _ = early(hop1, 0)
        (send,) = late(0, send_order, others, total, hop1, halo1)
        last = exchange(send, peers, turn)
        moved0, moved1 = relay(early0), relay(early1)
        whole = out((3, channels, nodes))
        placed, table, block = pl.pallas_call(
            lambda *refs: place_first_kernel(peers, *refs),
            out_shape=(
                whole,
                out((nodes, side)),
                jax.ShapeDtypeStruct((1, nodes), jnp.int32),
            ),
            in_specs=[VMEM] * (half + 1),
            out_specs=(HBM, VMEM, VMEM),
            scratch_shapes=[vmem((1, channels, nodes), BF16), dma((blocks,))],
            compiler_params=params(),
            cost_estimate=cost(2 * channels * nodes * nodes, 4 * channels * nodes),
            name="place0",
        )(arrival_place, *moved0)
        return pl.pallas_call(
            lambda *refs: place_rest_kernel(peers, *refs),
            out_shape=whole,
            in_specs=[HBM] + [VMEM] * (half + 3),
            out_specs=HBM,
            scratch_shapes=[vmem((2, channels, nodes), BF16), dma((blocks,))],
            input_output_aliases={0: 0},
            compiler_params=params(),
            name="place",
        )(placed, table, block, *moved1, last)
    halo0 = exchange(send, peers)

    def work(index):
        return [
            smem(tile_dst.shape, jnp.int32),
            smem(tile_src.shape, jnp.int32),
            vmem(index.shape, jnp.int32),
            vmem(tiles.shape, BF16),
            vmem((fixed, channels + EXTRA, side), BF16),
            vmem((blocks + 1, channels + EXTRA, side), F32),
            dma((3 + slots // 4,)),
        ]

    hop1, send = pl.pallas_call(
        lambda *refs: combine_pick_kernel(group, *refs),
        out_shape=(out(hop_shape), out(halo_shape)),
        in_specs=[HBM] * 4 + [VMEM] * 2,
        out_specs=(VMEM, VMEM),
        scratch_shapes=work(halo_index),
        compiler_params=params(),
        name="combine_pick",
    )(in_hbm(tile_dst), in_hbm(tile_src), in_hbm(halo_index), in_hbm(tiles), hop0, halo0)
    halo1 = exchange(send, peers)
    send = pl.pallas_call(
        lambda *refs: combine_last_kernel(group, *refs),
        out_shape=out(last_shape),
        in_specs=[HBM] * 4 + [VMEM] * 3,
        out_specs=VMEM,
        scratch_shapes=work(send_order),
        compiler_params=params(),
        name="combine_last",
    )(in_hbm(tile_dst), in_hbm(tile_src), in_hbm(send_order), in_hbm(tiles), hop1, halo1, hop0)
    last = exchange(send, peers)
    return pl.pallas_call(
        lambda *refs: place_kernel(side, *refs),
        out_shape=out((3, channels, nodes)),
        in_specs=[VMEM, VMEM],
        out_specs=VMEM,
        compiler_params=params(),
        name="place",
    )(arrival_place, last)


def solution(mesh):
    in_specs = (
        P(("dom", "rep"), None),
        P(),
        P("dom", None, None, None),
        P("dom", None),
        P("dom", None),
        P("dom", None),
        P("dom", None),
        P("dom", None),
    )
    out_specs = P(None, "rep", "dom")

    return jax.shard_map(
        on_device, mesh=mesh, in_specs=in_specs, out_specs=out_specs, check_vma=False
    )
```

```python
import jax
import jax.numpy as jnp
from jax import lax
from jax.experimental import pallas as pl
from jax.experimental.pallas import tpu as pltpu
from jax.sharding import PartitionSpec as P


BF16 = jnp.bfloat16
F32 = jnp.float32
EXTRA = 16
KEPT = 8
NN = (((1,), (0,)), ((), ()))
NT = (((1,), (1,)), ((), ()))
VMEM = pl.BlockSpec(memory_space=pltpu.VMEM)
HBM = pl.BlockSpec(memory_space=pltpu.HBM)


def params():
    return pltpu.CompilerParams(vmem_limit_bytes=20 * 1024 * 1024)


def cost(flops, size):
    return pl.CostEstimate(flops=flops, bytes_accessed=size, transcendentals=0)


def in_hbm(array):
    return pltpu.with_memory_space_constraint(array, pltpu.HBM)


def dot(left, right, dims=NN):
    return lax.dot_general(left, right, dims, preferred_element_type=F32)


def split(index, side, blocks):
    block = jnp.zeros_like(index)
    for edge in range(1, blocks):
        block += (index >= edge * side).astype(jnp.int32)
    return block, index - block * side


def one_hot(index, rows):
    row = lax.broadcasted_iota(jnp.int32, (rows, index.shape[1]), 0)
    return jnp.where(row == index, 1.0, 0.0).astype(BF16)


def pick(stack, blocks, index, side, group):
    rows = stack.shape[0] // blocks
    parts = []
    for start in range(0, index.shape[1], group):
        block, inner = split(index[:, start : start + group], side, blocks)
        every = dot(stack, one_hot(inner, side))
        chosen = every[:rows]
        for other in range(1, blocks):
            chosen = jnp.where(block == other, every[other * rows : (other + 1) * rows], chosen)
        parts.append(chosen.astype(BF16))
    return parts


def store_slots(buffer, parts, group, turn=0):
    if len(buffer.shape) == 2:
        for place, part in enumerate(parts):
            buffer[:, place * group : (place + 1) * group] = part
        return
    slot = buffer.shape[2]
    for place, part in enumerate(parts):
        for start in range(0, group, slot):
            peer = (place * group + start) // slot
            buffer[peer ^ turn] = part[:, start : start + slot]


def send_shape(channels, peers, slot):
    if slot % 128:
        return (channels, peers * slot)
    return (peers, channels, slot)


def exchange(send, peers, turn=0):
    if send.ndim == 2:
        send = send.reshape(send.shape[0], peers, -1).transpose(1, 0, 2)
    ranks = [[rank ^ turn for rank in range(peers)]] if turn else None
    arrived = lax.all_to_all(send, "dom", 0, 0, tiled=True, axis_index_groups=ranks)
    if arrived.shape[2] % 128 == 0:
        return arrived
    return arrived.transpose(1, 0, 2).reshape(arrived.shape[1], -1)


def load_wide(ref, turn=0):
    if len(ref.shape) == 2:
        return ref[...]
    return jnp.concatenate([ref[peer ^ turn] for peer in range(ref.shape[0])], axis=1)


def partner(me, step, count):
    if count & (count - 1) == 0:
        return me ^ step
    return lax.rem(me + step, count)


def source(me, step, count):
    if count & (count - 1) == 0:
        return me ^ step
    return lax.rem(me + count - step, count)


def pairs(step, count):
    if count & (count - 1) == 0:
        return [(rank, rank ^ step) for rank in range(count)]
    return [(rank, (rank + step) % count) for rank in range(count)]


def sketch_kernel(count, chunks, features_in, sketch_in, halo_in, order_in, *rest):
    outs, (halo_out, order_out, full, features, sketch, sems) = rest[:count], rest[count:]
    channels, width = outs[0].shape
    step = width // chunks
    copies = [pltpu.make_async_copy(sketch_in, sketch, sems.at[chunks])]
    for chunk in range(chunks):
        rows = pl.ds(chunk * step, step)
        copies.append(
            pltpu.make_async_copy(features_in.at[rows, :], features.at[rows, :], sems.at[chunk])
        )
    copies.append(pltpu.make_async_copy(halo_in, halo_out, sems.at[chunks + 1]))
    copies.append(pltpu.make_async_copy(order_in, order_out, sems.at[chunks + 2]))
    for copy in copies:
        copy.start()
    copies[0].wait()
    for chunk in range(chunks):
        copies[chunk + 1].wait()
        rows = slice(chunk * step, (chunk + 1) * step)
        product = dot(features[rows, :], sketch[...]).T.astype(BF16)
        for part in range(count):
            full[part, :, rows] = product[part * channels : (part + 1) * channels]
    me = lax.axis_index("rep")
    for part in range(count):
        outs[part][...] = full[partner(me, part, count)]
    copies[-2].wait()
    copies[-1].wait()


def pick_kernel(count, group, turn, index, *rest):
    arrived, (hop, send) = rest[:count], rest[count:]
    blocks, _, side = hop.shape
    per = blocks // count
    me = lax.axis_index("rep")
    for step in range(count):
        first = source(me, step, count) * per
        for part in range(per):
            hop[first + part] = arrived[step][:, part * side : (part + 1) * side]
    stack = jnp.concatenate([hop[block] for block in range(blocks)], 0)
    store_slots(send, pick(stack, blocks, index[...], side, group), group, turn)


def combine(dst_in, src_in, index_in, tiles_in, hop, arrived_ref, scratch, store):
    dst, src, index, tiles, columns, sums, sems = scratch
    blocks, channels, side = hop.shape
    slots = tiles.shape[0]
    fixed = columns.shape[0]
    small = [
        pltpu.make_async_copy(dst_in, dst, sems.at[0]),
        pltpu.make_async_copy(src_in, src, sems.at[1]),
        pltpu.make_async_copy(index_in, index, sems.at[2]),
    ]
    chunk = 4
    large = []
    for start in range(0, slots, chunk):
        rows = pl.ds(start, chunk)
        large.append(
            pltpu.make_async_copy(tiles_in.at[rows], tiles.at[rows], sems.at[3 + start // chunk])
        )
    for copy in large + small:
        copy.start()
    columns[:, channels:, :] = jnp.ones((fixed, EXTRA, side), BF16)
    for block in range(blocks):
        columns[block, :channels, :] = hop[block]
    arrived = load_wide(arrived_ref)
    for block in range(blocks, fixed):
        start = (block - blocks) * side
        columns[block, :channels, :] = arrived[:, start : start + side]
    for slot in range(slots):
        if slot % chunk == 0:
            large[slot // chunk].wait()
        if slot < blocks:
            sums[slot] = dot(columns[slot], tiles[slot], NT)
            continue
        if slot == blocks:
            for copy in small:
                copy.wait()
        target = dst[0, slot]
        target = jnp.where(target < 0, blocks, target)
        start = slot if slot < fixed else src[0, slot]
        sums[target] = sums[target] + dot(columns[start], tiles[slot], NT)
    results = []
    for block in range(blocks):
        total = sums[block]
        result = (total[:channels] / total[channels : channels + 1]).astype(BF16)
        store(block, result)
        results.append(result)
    return results


def combine_pick_kernel(
    group, dst_in, src_in, index_in, tiles_in, hop, arrived_ref, result, send, *scratch
):
    def store(block, value):
        result[block] = value

    results = combine(dst_in, src_in, index_in, tiles_in, hop, arrived_ref, scratch, store)
    blocks, _, side = hop.shape
    index = scratch[2]
    stack = jnp.concatenate(results, 0)
    store_slots(send, pick(stack, blocks, index[...], side, group), group)


def early_kernel(staged, index, tiles_in, hop, near, far, total, *rest):
    full, tiles, sems = rest[-3:]
    blocks, channels, side = hop.shape
    copies = [pltpu.make_async_copy(tiles_in.at[pl.ds(0, blocks)], tiles, sems.at[0])]
    if staged:
        others = tiles_in.shape[0] - blocks
        copies.append(
            pltpu.make_async_copy(tiles_in.at[pl.ds(blocks, others)], rest[0], sems.at[1])
        )
    for copy in copies:
        copy.start()
    peers, _, slot = full.shape
    stack = jnp.concatenate([hop[block] for block in range(blocks)], 0)
    for peer, part in enumerate(pick(stack, blocks, index[...], side, slot)):
        full[peer] = part
    me = lax.axis_index("dom")
    half = peers // 2
    for step in range(half):
        near[step] = full[me ^ step]
        far[step] = full[me ^ half ^ step]
    ones = jnp.ones((EXTRA, side), BF16)
    copies[0].wait()
    for block in range(blocks):
        columns = jnp.concatenate([hop[block], ones], 0)
        total[block] = dot(columns, tiles[block], NT)[: channels + KEPT]
    if staged:
        copies[1].wait()


def finish(turn, dst, src, tiles, total, hop, arrived, columns, sums):
    blocks, channels, side = hop.shape
    fixed = columns.shape[0]
    slots = blocks + tiles.shape[0]
    lane = lax.broadcasted_iota(jnp.int32, dst.shape, 1)
    targets, starts = {}, {slot: slot for slot in range(fixed)}
    for slot in range(blocks, slots):
        target = jnp.sum(jnp.where(lane == slot, dst[...], 0))
        targets[slot] = jnp.where(target < 0, blocks, target)
    for slot in range(fixed, slots):
        starts[slot] = jnp.sum(jnp.where(lane == slot, src[...], 0))
    columns[:, channels:, :] = jnp.ones((fixed, EXTRA, side), BF16)
    for block in range(blocks):
        columns[block, :channels, :] = hop[block]
        sums[block] = total[block]
    wide = load_wide(arrived, turn)
    for block in range(blocks, fixed):
        start = (block - blocks) * side
        columns[block, :channels, :] = wide[:, start : start + side]
    products = [
        dot(columns[starts[slot]], tiles[slot - blocks], NT) for slot in range(blocks, fixed)
    ]
    for slot in range(blocks, slots):
        target = targets[slot]
        if slot < fixed:
            product = products[slot - blocks]
        else:
            product = dot(columns[starts[slot]], tiles[slot - blocks], NT)
        sums[target] = sums[target] + product[: channels + KEPT]
    results = []
    for block in range(blocks):
        whole = sums[block]
        results.append((whole[:channels] / whole[channels : channels + 1]).astype(BF16))
    return results


def finish_kernel(
    group, turn, keep, dst, src, index, tiles, total, hop, arrived, *rest
):
    send, scratch = rest[keep], rest[keep + 1 :]
    results = finish(turn, dst, src, tiles, total, hop, arrived, *scratch)
    blocks, _, side = hop.shape
    if keep:
        for block, result in enumerate(results):
            rest[0][block] = result
    stack = jnp.concatenate(results, 0)
    store_slots(send, pick(stack, blocks, index[...], side, group), group, turn)


def relay_kernel(near, sent, *outs):
    channels = near.shape[1]
    for step, out in enumerate(outs):
        out[:channels] = near[step]
        out[channels:] = sent[step]


def combine_last_kernel(
    group, dst_in, src_in, index_in, tiles_in, hop, arrived_ref, hop0, send, *scratch
):
    results = combine(
        dst_in, src_in, index_in, tiles_in, hop, arrived_ref, scratch, lambda *_: None
    )
    blocks, _, side = hop.shape
    index = scratch[2]
    stack = []
    for block in range(blocks):
        stack += [hop0[block], hop[block], results[block]]
    stack = jnp.concatenate(stack, 0)
    store_slots(send, pick(stack, blocks, index[...], side, group), group)


def scatter(parts, table, block, out, out_ref, first, sems):
    hops, channels, nodes = out.shape
    side = table.shape[1]
    stacked = jnp.concatenate(parts, 1)
    rows = stacked.shape[0]
    group = max(128 // rows, 1)
    copies = []
    for start in range(0, nodes // side, group):
        masks = [
            jnp.where(block == other, 1.0, 0.0).astype(BF16)
            for other in range(start, start + group)
        ]
        placed = dot(jnp.concatenate([stacked * mask for mask in masks], 0), table).astype(BF16)
        for other in range(group):
            columns = slice((start + other) * side, (start + other + 1) * side)
            for hop in range(hops):
                row = other * rows + hop * channels
                out[hop, :, columns] = placed[row : row + channels]
        columns = pl.ds(start * side, group * side)
        copies.append(
            pltpu.make_async_copy(
                out.at[:, :, columns],
                out_ref.at[pl.ds(first, hops), :, columns],
                sems.at[start],
            )
        )
        copies[-1].start()
    for copy in copies:
        copy.wait()


def place_first_kernel(peers, index_ref, *rest):
    moved, (out_ref, table_ref, block_ref, out, sems) = rest[:-5], rest[-5:]
    _, channels, nodes = out.shape
    side = table_ref.shape[1]
    blocks = nodes // side
    half = peers // 2
    slot = nodes // peers
    me = lax.axis_index("dom")
    parts, indexes = [], []
    for step in range(peers):
        start = pl.multiple_of((me ^ step) * slot, slot)
        indexes.append(index_ref[:, pl.ds(start, slot)])
        first = (step // half) * channels
        parts.append(moved[step % half][first : first + channels])
    block, inner = split(jnp.concatenate(indexes, 1), side, blocks)
    block_ref[...] = block
    table = jnp.concatenate(
        [one_hot(inner[:, start : start + side], side).T for start in range(0, nodes, side)], 0
    )
    table_ref[...] = table
    scatter(parts, table, block, out, out_ref, 0, sems)


def place_rest_kernel(peers, turn, _, table_ref, block_ref, *rest):
    moved, last, (out_ref, out, sems) = rest[:-4], rest[-4], rest[-3:]
    channels = out.shape[1]
    half = peers // 2
    me = lax.axis_index("dom")
    parts = []
    for step in range(peers):
        first = (step // half) * channels
        arrived = moved[step % half][first : first + channels]
        parts.append(jnp.concatenate([arrived, last[me ^ step ^ turn]], 0))
    scatter(parts, table_ref[...], block_ref[...], out, out_ref, 1, sems)


def place_kernel(side, index_ref, arrived_ref, out_ref):
    hops, channels, nodes = out_ref.shape
    blocks = nodes // side
    stacked = load_wide(arrived_ref)
    block, inner = split(index_ref[...], side, blocks)
    table = one_hot(inner, side)
    for other in range(blocks):
        mask = jnp.where(block == other, 1.0, 0.0).astype(BF16)
        placed = dot(stacked * mask, table, NT).astype(BF16)
        for hop in range(hops):
            out_ref[hop, :, other * side : (other + 1) * side] = placed[
                hop * channels : (hop + 1) * channels
            ]


def on_device(
    features, sketch_matrix, tiles, tile_dst, tile_src, halo_index, send_order, arrival_place
):
    reps = lax.axis_size("rep")
    peers = lax.axis_size("dom")
    width = features.shape[0]
    nodes = width * reps
    channels = sketch_matrix.shape[1] // reps
    halo = halo_index.shape[1]
    tiles = tiles[0]
    slots, side, _ = tiles.shape
    blocks = nodes // side
    fixed = (nodes + halo) // side
    vmem, smem, dma = pltpu.VMEM, pltpu.SMEM, pltpu.SemaphoreType.DMA
    hop_shape = (blocks, channels, side)
    halo_shape = send_shape(channels, peers, halo // peers)
    last_shape = send_shape(3 * channels, peers, nodes // peers)
    group = 512
    chunks = 1
    slot = nodes // peers
    half = peers // 2
    whole_lanes = slot % 128 == 0 and (halo // peers) % 128 == 0
    turn = half ^ 1 if whole_lanes and peers & (peers - 1) == 0 else 0

    def out(shape):
        return jax.ShapeDtypeStruct(shape, BF16)

    def early(hop, staged):
        shape = (peers // 2, channels, slot)
        others = (slots - blocks, side, side)
        near, far, total, *rest = pl.pallas_call(
            lambda *refs: early_kernel(staged, *refs),
            out_shape=(
                out(shape),
                out(shape),
                jax.ShapeDtypeStruct((blocks, channels + KEPT, side), F32),
            )
            + (out(others),) * staged,
            in_specs=[VMEM, HBM, VMEM],
            out_specs=(VMEM,) * (3 + staged),
            scratch_shapes=[
                vmem((peers, channels, slot), BF16),
                vmem((blocks, side, side), BF16),
                dma((2,)),
            ],
            compiler_params=params(),
            cost_estimate=cost(2 * channels * nodes * nodes, 8 * channels * nodes),
            name="early",
        )(order_rows, in_hbm(tiles), hop)
        sent = lax.ppermute(far, "dom", pairs(peers // 2, peers))
        return (near, sent), total, rest

    def relay(blocks_of):
        steps = peers // 2
        moved = pl.pallas_call(
            relay_kernel,
            out_shape=(out((2 * channels, slot)),) * steps,
            in_specs=[VMEM] * 2,
            out_specs=(VMEM,) * steps,
            compiler_params=params(),
            cost_estimate=cost(0, 8 * channels * nodes),
            name="relay",
        )(*blocks_of)
        sent = [moved[0]]
        for step in range(1, steps):
            sent.append(lax.ppermute(moved[step], "dom", pairs(step, peers)))
        return sent

    def late(keep, index, others, total, hop, arrived):
        shape = (peers, channels, index.shape[1] // peers)
        return pl.pallas_call(
            lambda *refs: finish_kernel(group, turn, keep, *refs),
            out_shape=(out(hop_shape),) * keep + (out(shape),),
            in_specs=[VMEM] * 7,
            out_specs=(VMEM,) * (keep + 1),
            scratch_shapes=[
                vmem((fixed, channels + EXTRA, side), BF16),
                vmem((blocks + 1, channels + KEPT, side), F32),
            ],
            compiler_params=params(),
        )(tile_dst, tile_src, index, others, total, hop, arrived)

    *own, halo_rows, order_rows = pl.pallas_call(
        lambda *refs: sketch_kernel(reps, chunks, *refs),
        out_shape=(out((channels, width)),) * reps
        + (
            jax.ShapeDtypeStruct(halo_index.shape, jnp.int32),
            jax.ShapeDtypeStruct(send_order.shape, jnp.int32),
        ),
        in_specs=[HBM] * 4,
        out_specs=(VMEM,) * (reps + 2),
        scratch_shapes=[
            vmem((reps, channels, width), BF16),
            vmem(features.shape, BF16),
            vmem(sketch_matrix.shape, BF16),
            dma((chunks + 3,)),
        ],
        compiler_params=params(),
        name="sketch",
    )(in_hbm(features), in_hbm(sketch_matrix), in_hbm(halo_index), in_hbm(send_order))
    arrived = [own[0]]
    for step in range(1, reps):
        arrived.append(lax.ppermute(own[step], "rep", pairs(step, reps)))
    hop0, send = pl.pallas_call(
        lambda *refs: pick_kernel(reps, group, turn, *refs),
        out_shape=(out(hop_shape), out(halo_shape)),
        in_specs=[VMEM] * (reps + 1),
        out_specs=(VMEM, VMEM),
        compiler_params=params(),
        name="pick",
    )(halo_rows, *arrived)
    if turn:
        halo0 = exchange(send, peers, turn)
        early0, total, others = early(hop0, 1)
        others = others[0]
        hop1, send = late(1, halo_rows, others, total, hop0, halo0)
        halo1 = exchange(send, peers, turn)
        early1, total, _ = early(hop1, 0)
        (send,) = late(0, order_rows, others, total, hop1, halo1)
        last = exchange(send, peers, turn)
        moved0, moved1 = relay(early0), relay(early1)
        whole = out((3, channels, nodes))
        placed, table, block = pl.pallas_call(
            lambda *refs: place_first_kernel(peers, *refs),
            out_shape=(
                whole,
                out((nodes, side)),
                jax.ShapeDtypeStruct((1, nodes), jnp.int32),
            ),
            in_specs=[VMEM] * (half + 1),
            out_specs=(HBM, VMEM, VMEM),
            scratch_shapes=[vmem((1, channels, nodes), BF16), dma((blocks,))],
            compiler_params=params(),
            cost_estimate=cost(2 * channels * nodes * nodes, 4 * channels * nodes),
            name="place0",
        )(arrival_place, *moved0)
        return pl.pallas_call(
            lambda *refs: place_rest_kernel(peers, turn, *refs),
            out_shape=whole,
            in_specs=[HBM] + [VMEM] * (half + 3),
            out_specs=HBM,
            scratch_shapes=[vmem((2, channels, nodes), BF16), dma((blocks,))],
            input_output_aliases={0: 0},
            compiler_params=params(),
            name="place",
        )(placed, table, block, *moved1, last)
    halo0 = exchange(send, peers)

    def work(index):
        return [
            smem(tile_dst.shape, jnp.int32),
            smem(tile_src.shape, jnp.int32),
            vmem(index.shape, jnp.int32),
            vmem(tiles.shape, BF16),
            vmem((fixed, channels + EXTRA, side), BF16),
            vmem((blocks + 1, channels + EXTRA, side), F32),
            dma((3 + slots // 4,)),
        ]

    hop1, send = pl.pallas_call(
        lambda *refs: combine_pick_kernel(group, *refs),
        out_shape=(out(hop_shape), out(halo_shape)),
        in_specs=[HBM] * 4 + [VMEM] * 2,
        out_specs=(VMEM, VMEM),
        scratch_shapes=work(halo_index),
        compiler_params=params(),
        name="combine_pick",
    )(in_hbm(tile_dst), in_hbm(tile_src), in_hbm(halo_index), in_hbm(tiles), hop0, halo0)
    halo1 = exchange(send, peers)
    send = pl.pallas_call(
        lambda *refs: combine_last_kernel(group, *refs),
        out_shape=out(last_shape),
        in_specs=[HBM] * 4 + [VMEM] * 3,
        out_specs=VMEM,
        scratch_shapes=work(send_order),
        compiler_params=params(),
        name="combine_last",
    )(in_hbm(tile_dst), in_hbm(tile_src), in_hbm(send_order), in_hbm(tiles), hop1, halo1, hop0)
    last = exchange(send, peers)
    return pl.pallas_call(
        lambda *refs: place_kernel(side, *refs),
        out_shape=out((3, channels, nodes)),
        in_specs=[VMEM, VMEM],
        out_specs=VMEM,
        compiler_params=params(),
        name="place",
    )(arrival_place, last)


def solution(mesh):
    in_specs = (
        P(("dom", "rep"), None),
        P(),
        P("dom", None, None, None),
        P("dom", None),
        P("dom", None),
        P("dom", None),
        P("dom", None),
        P("dom", None),
    )
    out_specs = P(None, "rep", "dom")

    return jax.shard_map(
        on_device, mesh=mesh, in_specs=in_specs, out_specs=out_specs, check_vma=False
    )
```
